512 devices in a mesh: outer: 32 (over z_hi, y, core), inner: 16 (over x, z_lo).
Axes of the slice: x: 4, y: 8, z: 8 (z_hi: 2, z_lo: 4; z = z_hi * 4 + z_lo), core: 2. Of those that a mesh axis runs over, the one named last changes fastest.
Arguments:
- projected: bfloat16 [262144, 384], P(('outer', 'inner')), may hold values from -6 to 6
- short_taps: float32 [3, 384], replicated, may hold values from -3.5 to 3.5
- skip_gain: float32 [128], replicated, may hold values from 0.5 to 1.5
- long_filter: bfloat16 [262144], P(('outer', 'inner')), may hold values from -0.01171875 to 0.01171875
Outputs:
- output: float32 [262144, 128], P(('outer', 'inner'))
The draws below stay inside these ranges and needn't reach their ends.
All inputs are finite; a program needn't handle non-finite values.
Results may differ from the reference program's by a relative error of at most 0.0045.
Values may be sent and summed in bfloat16 or wider, within the bound.
No kernel may reach another device: no remote copies, remote signals or barrier semaphores. Data moves between devices by JAX's collectives and lax.ppermute only.
A program may use at most 64 MiB of HBM per device.

```python
import jax
import jax.numpy as jnp
from jax import lax

CH = 128
TAPS = 3
LENGTH = 262144


def block_levels(stream_key, extent, split, low, high):
    def one(dim, shards_of):
        heights = jax.random.uniform(jax.random.fold_in(jax.random.fold_in(stream_key, 6), dim), (shards_of,), jnp.float32, low / len(split), high / len(split))
        return jnp.repeat(jnp.exp(heights), extent[dim] // shards_of).reshape((-1,) + (1,) * (len(extent) - dim - 1))

    factor_of = one(*split[0])
    for cut in split[1:]:
        factor_of = factor_of * one(*cut)
    return factor_of


def gaussian(rng, shape, spread, reach, cuts=(), kind=jnp.bfloat16):
    entries = spread * jax.random.normal(rng, shape, jnp.float32)
    if cuts:
        entries = entries * block_levels(rng, shape, cuts, -0.22, 0.18)
    return jnp.clip(entries, -reach, reach).astype(kind)


def setup_inputs(seed: int = 0) -> dict:
    streams_of = jax.random.split(jax.random.key(seed), 5)
    projected = gaussian(streams_of[0], (LENGTH, 3 * CH), 1.0, 6.0, ((0, 512),))
    short_taps = gaussian(streams_of[1], (TAPS, 3 * CH), TAPS ** -0.5, 3.5, (), jnp.float32)
    skip_gain = jnp.clip(jax.random.uniform(streams_of[2], (CH,), jnp.float32, 0.5, 1.5), 0.5, 1.5)
    long_filter = gaussian(streams_of[3], (LENGTH,), LENGTH ** -0.5, 0.01171875, ((0, 512),))
    return dict(projected=projected, short_taps=short_taps, skip_gain=skip_gain, long_filter=long_filter)


def reference(projected, short_taps, skip_gain, long_filter):
    response = jnp.fft.fft(long_filter.astype(jnp.float32), n=2 * LENGTH)

    def one_block(block_number):
        first_col = block_number * 16

        def causal(column_offset):
            columns = lax.dynamic_slice_in_dim(projected, first_col + column_offset, 16, 1).astype(jnp.float32)
            weights = lax.dynamic_slice_in_dim(short_taps, first_col + column_offset, 16, 1)
            running = weights[0] * columns
            for tap_number in range(1, TAPS):
                shifted = jnp.pad(columns, ((tap_number, 0), (0, 0)))[:LENGTH]
                running = running + weights[tap_number] * shifted
            return running

        queries = causal(0)
        key_stream = causal(CH)
        value_stream = causal(2 * CH)
        rounded = lax.optimization_barrier((key_stream * value_stream).astype(jnp.bfloat16))
        mixture = rounded.astype(jnp.float32)
        transformed = jnp.fft.fft(mixture, n=2 * LENGTH, axis=0)
        convolved = jnp.real(jnp.fft.ifft(transformed * response[:, None], axis=0))[:LENGTH]
        weights_skip = lax.dynamic_slice_in_dim(skip_gain, first_col, 16, 0)
        return queries * (convolved + weights_skip * mixture)

    pieces = lax.map(one_block, jnp.arange(CH // 16, dtype=jnp.int32))
    return jnp.transpose(pieces, (1, 0, 2)).reshape(LENGTH, CH)
```

```python
import numpy as np

import jax
import jax.numpy as jnp
from jax import lax
from jax.experimental import pallas as pl
from jax.experimental.pallas import tpu as pltpu
from jax.sharding import PartitionSpec as P

LANE = 128
highest = lax.Precision.HIGHEST


def unit(phase):
    turn = 2.0 * np.pi * np.asarray(phase, np.float64)
    return np.cos(turn), np.sin(turn)


def tables(outer, inner, seg):
    span = inner * seg
    high = seg // LANE
    lines = span // LANE
    theta = (np.arange(outer) + 0.25) / outer
    place = np.arange(outer)[None, None, :] + np.arange(inner)[:, None, None] / inner
    cos, sin = unit(theta[None, :, None] * place)
    gather = np.concatenate([cos, sin], axis=1)
    spread = np.concatenate([cos, sin], axis=1).transpose(0, 2, 1) / (outer * span)
    cos, sin = unit(theta[:, None] * np.arange(seg)[None, :] / span)
    edge = np.concatenate([cos, sin], axis=1)
    row = (np.arange(high)[:, None] + high * np.arange(inner)[None, :]).reshape(-1)
    cos, sin = unit(np.outer(np.arange(lines), row) % lines / lines)
    first = np.block([[cos, -sin], [sin, cos]])
    first_back = first.T
    cos, sin = unit(np.outer(np.arange(lines), np.arange(LANE)) / span)
    turn = np.concatenate([cos, sin], axis=1)
    cos, sin = unit(np.outer(np.arange(LANE), np.arange(LANE)) % LANE / LANE)
    second = np.block([[cos, sin], [-sin, cos]])
    second_back = second.T
    named = (gather, spread, edge, first, first_back, turn, second, second_back)
    return tuple(item.astype(np.float32) for item in named)


def dot(left, right):
    return jnp.dot(left, right, precision=highest, preferred_element_type=jnp.float32)


def short_filter(projected_ref, earlier_ref, taps_ref, ext_ref):
    seg = projected_ref.shape[0]
    ext_ref[0:8, :] = earlier_ref[...].astype(jnp.float32)
    ext_ref[8 : 8 + seg, :] = projected_ref[...].astype(jnp.float32)
    total = taps_ref[0:1, :] * ext_ref[8 : 8 + seg, :]
    for tap in range(1, taps_ref.shape[0]):
        total = total + taps_ref[tap : tap + 1, :] * ext_ref[8 - tap : 8 - tap + seg, :]
    return total


def mix_of(filtered):
    width = filtered.shape[1] // 3
    return (filtered[:, width : 2 * width] * filtered[:, 2 * width :]).astype(jnp.bfloat16)


def pack_kernel(projected_ref, earlier_ref, taps_ref, filter_ref, out_ref, ext_ref):
    outer = out_ref.shape[0]
    high = filter_ref.shape[0]
    groups = LANE // outer
    mixture = mix_of(short_filter(projected_ref, earlier_ref, taps_ref, ext_ref))
    mixture = mixture.astype(jnp.float32)
    for hi in range(high):
        flipped = mixture[hi * LANE : (hi + 1) * LANE, :].T.astype(jnp.bfloat16)
        for ch in range(groups):
            at = (hi * (groups + 1) + ch) * LANE
            out_ref[:, at : at + LANE] = flipped[ch * outer : (ch + 1) * outer, :]
        at = (hi * (groups + 1) + groups) * LANE
        taps = filter_ref[hi : hi + 1, :].astype(jnp.float32)
        out_ref[:, at : at + LANE] = jnp.broadcast_to(taps, (outer, LANE)).astype(jnp.bfloat16)


def gather_kernel(data_ref, gather_ref, edge_ref, out_ref):
    outer, width = data_ref.shape
    inner = out_ref.shape[0]
    seg = edge_ref.shape[1] // 2
    high = seg // LANE
    series = width // seg
    sums = dot(gather_ref[...], data_ref[...].astype(jnp.float32))
    half = out_ref.shape[1] // (outer // inner)
    for hi in range(high):
        cos = edge_ref[:, hi * LANE : (hi + 1) * LANE]
        sin = edge_ref[:, seg + hi * LANE : seg + (hi + 1) * LANE]
        for ch in range(series):
            at = (hi * series + ch) * LANE
            real = sums[:outer, at : at + LANE]
            imag = sums[outer:, at : at + LANE]
            turned = (real * cos - imag * sin, real * sin + imag * cos)
            for part in range(2):
                value = turned[part].astype(jnp.bfloat16)
                for kk in range(outer // inner):
                    to = kk * half + ((part * high + hi) * series + ch) * LANE
                    out_ref[:, to : to + LANE] = value[kk * inner : (kk + 1) * inner, :]


def wave_kernel(data_ref, first_ref, first_back_ref, turn_ref, second_ref, second_back_ref, out_ref, *, copies, high):
    inner = data_ref.shape[0]
    in_half = data_ref.shape[1] // copies
    out_half = out_ref.shape[1] // copies
    in_width = in_half // (2 * high)
    out_width = out_half // (2 * high)
    series = in_width // LANE
    lines = turn_ref.shape[0]
    cos = turn_ref[:, :LANE]
    sin = turn_ref[:, LANE:]
    for kk in range(copies):
        rows = [data_ref[:, kk * in_half + q * in_width : kk * in_half + (q + 1) * in_width] for q in range(2 * high)]
        block = jnp.concatenate(rows, axis=0).astype(jnp.float32)
        waves = dot(first_ref[...], block)
        stacked = []
        for ch in range(series):
            real = waves[:lines, ch * LANE : (ch + 1) * LANE]
            imag = waves[lines:, ch * LANE : (ch + 1) * LANE]
            stacked.append(jnp.concatenate([real * cos - imag * sin, real * sin + imag * cos], axis=1))
        freq = dot(jnp.concatenate(stacked, axis=0), second_ref[...])
        last = freq[(series - 1) * lines :, :]
        tap_real = last[:, :LANE]
        tap_imag = last[:, LANE:]
        products = []
        for ch in range(series - 1):
            real = freq[ch * lines : (ch + 1) * lines, :LANE]
            imag = freq[ch * lines : (ch + 1) * lines, LANE:]
            products.append(
                jnp.concatenate([real * tap_real - imag * tap_imag, real * tap_imag + imag * tap_real], axis=1)
            )
        back = dot(jnp.concatenate(products, axis=0), second_back_ref[...])
        columns = []
        for ch in range(series - 1):
            real = back[ch * lines : (ch + 1) * lines, :LANE]
            imag = back[ch * lines : (ch + 1) * lines, LANE:]
            columns.append(jnp.concatenate([real * cos + imag * sin, imag * cos - real * sin], axis=0))
        done = dot(first_back_ref[...], jnp.concatenate(columns, axis=1)).astype(jnp.bfloat16)
        for q in range(2 * high):
            at = kk * out_half + q * out_width
            out_ref[:, at : at + out_width] = done[q * inner : (q + 1) * inner, :]


def spread_kernel(data_ref, spread_ref, edge_ref, out_ref):
    inner = data_ref.shape[0]
    outer, width = out_ref.shape
    seg = edge_ref.shape[1] // 2
    high = seg // LANE
    line = width // high
    half = data_ref.shape[1] // (outer // inner)
    for hi in range(high):
        cos = edge_ref[:, hi * LANE : (hi + 1) * LANE]
        sin = edge_ref[:, seg + hi * LANE : seg + (hi + 1) * LANE]

        def piece(part):
            at = (part * high + hi) * line
            rows = [data_ref[:, kk * half + at : kk * half + at + line] for kk in range(outer // inner)]
            return jnp.concatenate(rows, axis=0).astype(jnp.float32)

        real, imag = piece(0), piece(1)
        turned = []
        for ch in range(line // LANE):
            re = real[:, ch * LANE : (ch + 1) * LANE]
            im = imag[:, ch * LANE : (ch + 1) * LANE]
            turned.append(jnp.concatenate([re * cos + im * sin, im * cos - re * sin], axis=0))
        value = dot(spread_ref[...], jnp.concatenate(turned, axis=1))
        out_ref[:, hi * line : (hi + 1) * line] = value.astype(jnp.bfloat16)


def gate_kernel(projected_ref, earlier_ref, taps_ref, gain_ref, data_ref, out_ref, ext_ref):
    outer, width = data_ref.shape
    channels = out_ref.shape[1]
    filtered = short_filter(projected_ref, earlier_ref, taps_ref, ext_ref)
    mixture = mix_of(filtered).astype(jnp.float32)
    queries = filtered[:, :channels]
    groups = channels // outer
    high = width // (groups * LANE)
    for hi in range(high):
        rows = [
            data_ref[:, (hi * groups + ch) * LANE : (hi * groups + ch + 1) * LANE].astype(jnp.float32)
            for ch in range(groups)
        ]
        convolved = jnp.concatenate(rows, axis=0).T
        span = slice(hi * LANE, (hi + 1) * LANE)
        out_ref[span, :] = queries[span, :] * (convolved + gain_ref[...] * mixture[span, :])


def exchange(value, axis, count):
    shaped = value.reshape(count, -1, LANE)
    moved = lax.all_to_all(shaped, axis, split_axis=0, concat_axis=0, tiled=True)
    return moved.reshape(value.shape)


def on_device(projected, short_taps, skip_gain, long_filter):
    seg, wide = projected.shape
    channels = skip_gain.shape[0]
    outer = lax.axis_size("outer")
    inner = lax.axis_size("inner")
    count = outer * inner
    groups = channels // outer
    high = seg // LANE
    copies = outer // inner
    gather, spread, edge, first, first_back, turn, second, second_back = tables(outer, inner, seg)
    column = lax.axis_index("inner")
    gather = lax.dynamic_index_in_dim(jnp.asarray(gather), column, 0, keepdims=False)
    spread = lax.dynamic_index_in_dim(jnp.asarray(spread), column, 0, keepdims=False)

    earlier = lax.ppermute(projected[seg - 8 :], ("outer", "inner"), [(s, s + 1) for s in range(count - 1)])
    ext = pltpu.VMEM((seg + 8, wide), jnp.float32)
    packed = pl.pallas_call(
        pack_kernel,
        out_shape=jax.ShapeDtypeStruct((outer, (groups + 1) * seg), jnp.bfloat16),
        scratch_shapes=[ext],
        name="pack",
    )(projected, earlier, short_taps, long_filter.reshape(high, LANE))
    arrived = exchange(packed, "outer", outer)
    summed = pl.pallas_call(
        gather_kernel,
        out_shape=jax.ShapeDtypeStruct((inner, copies * 2 * (groups + 1) * seg), jnp.bfloat16),
        name="gather",
    )(arrived, gather, edge)
    lined = exchange(summed, "inner", inner)
    waves = pl.pallas_call(
        lambda *refs: wave_kernel(*refs, copies=copies, high=high),
        out_shape=jax.ShapeDtypeStruct((inner, copies * 2 * groups * seg), jnp.bfloat16),
        name="wave",
    )(lined, first, first_back, turn, second, second_back)
    returned = exchange(waves, "inner", inner)
    settled = pl.pallas_call(
        spread_kernel,
        out_shape=jax.ShapeDtypeStruct((outer, groups * seg), jnp.bfloat16),
        name="spread",
    )(returned, spread, edge)
    home = exchange(settled, "outer", outer)
    return pl.pallas_call(
        gate_kernel,
        out_shape=jax.ShapeDtypeStruct((seg, channels), jnp.float32),
        scratch_shapes=[ext],
        name="gate",
    )(projected, earlier, short_taps, skip_gain.reshape(1, channels), home)


def solution(mesh):
    placed = (P(("outer", "inner"), None), P(), P(), P(("outer", "inner")))
    return jax.shard_map(
        on_device,
        mesh=mesh,
        in_specs=placed,
        out_specs=P(("outer", "inner"), None),
        check_vma=False,
    )
```

```python
import numpy as np

import jax
import jax.numpy as jnp
from jax import lax
from jax.experimental import pallas as pl
from jax.experimental.pallas import tpu as pltpu
from jax.sharding import Mesh, PartitionSpec as P

LANE = 128
FIRST = ("zh", "x", "zl")
SECOND = ("y", "core")
EVERY = ("zh", "y", "core", "x", "zl")
SPLIT = (2, 8, 2, 4, 4)
ZH = 2
INNER = 16
SPAN = 8192
LINES = 64
HIGH = 4
SERIES = ((0, 0), (0, 1), (0, 2), (1, 0), (1, 1))


def turn_of(phase):
    turn = 2.0 * np.pi * np.asarray(phase, np.float64)
    return np.cos(turn), np.sin(turn)


def halves(table):
    table = np.asarray(table, np.float32)
    upper = table.astype(jnp.bfloat16)
    lower = (table - upper.astype(np.float32)).astype(jnp.bfloat16)
    return np.stack([upper, lower])


def tables():
    line = np.arange(LINES)
    cos, sin = turn_of(np.outer(line + 0.25, line) / LINES)
    same = np.eye(ZH)

    def forward(part):
        small = part.reshape(INNER, HIGH, INNER, HIGH)
        return np.einsum("jkir,zw,cd->cjzkwidr", small, same, np.eye(2)).reshape(2, 128, 256)

    first = np.stack([forward(cos), forward(sin)], axis=1).reshape(512, 256)

    def backward(part):
        small = part.reshape(INNER, HIGH, INNER, HIGH) / SPAN
        return np.einsum("jkir,zw,cd->wicrdjzk", small, same, np.eye(2)).reshape(256, 2, 128)

    first_back = np.stack([backward(cos), backward(sin)], axis=2).reshape(256, 512)
    cos, sin = turn_of(np.outer(line + 0.25, np.arange(LANE)) / SPAN)
    rows = (np.arange(INNER)[:, None, None] * HIGH + np.zeros((1, ZH, 1), int) + np.arange(HIGH)).reshape(-1)
    twist = np.concatenate([cos[rows], sin[rows]], axis=1).astype(np.float32)
    cos, sin = turn_of(np.outer(np.arange(LANE), np.arange(LANE)) / LANE)
    second = np.block([[cos, sin], [-sin, cos]])
    return halves(first), halves(first_back), twist, halves(second), halves(second.T)


def mxu(left, right):
    return jnp.dot(left, right, preferred_element_type=jnp.float32)


def cut(value):
    upper = value.astype(jnp.bfloat16)
    return upper, (value - upper.astype(jnp.float32)).astype(jnp.bfloat16)


def short_filter(projected_ref, earlier_ref, taps_ref, ext_ref):
    seg = projected_ref.shape[0]
    ext_ref[0:8, :] = earlier_ref[...].astype(jnp.float32)
    ext_ref[8 : 8 + seg, :] = projected_ref[...].astype(jnp.float32)
    total = taps_ref[0:1, :] * ext_ref[8 : 8 + seg, :]
    for tap in range(1, taps_ref.shape[0]):
        total = total + taps_ref[tap : tap + 1, :] * ext_ref[8 - tap : 8 - tap + seg, :]
    return total


def mix_of(filtered):
    width = filtered.shape[1] // 3
    return (filtered[:, width : 2 * width] * filtered[:, 2 * width :]).astype(jnp.bfloat16)


def pack_kernel(projected_ref, earlier_ref, taps_ref, filter_ref, out_ref, ext_ref, rows_ref):
    mixture = mix_of(short_filter(projected_ref, earlier_ref, taps_ref, ext_ref)).astype(jnp.float32)
    for hi in range(HIGH):
        flipped = mixture[hi * LANE : (hi + 1) * LANE, :].T
        for ch in range(4):
            chh, at = SERIES[ch]
            rows_ref[at, pl.ds(chh * 4 + hi, 32, stride=8), :] = flipped[ch * 32 : (ch + 1) * 32, :]
        taps = jnp.broadcast_to(filter_ref[hi : hi + 1, :].astype(jnp.float32), (32, LANE))
        rows_ref[1, pl.ds(4 + hi, 32, stride=8), :] = taps
        rows_ref[2, pl.ds(4 + hi, 32, stride=8), :] = jnp.zeros((32, LANE), jnp.float32)
    for at in range(3):
        out_ref[:, :, at * LANE : (at + 1) * LANE] = rows_ref[at].reshape(32, 8, LANE).astype(jnp.bfloat16)


def ahead_kernel(data_ref, first_ref, twist_ref, second_ref, out_ref):
    data = data_ref[...].astype(jnp.float32).reshape(256, 3 * LANE).astype(jnp.bfloat16)
    waves = mxu(first_ref[0], data) + mxu(first_ref[1], data)
    cos = twist_ref[:, :LANE]
    sin = twist_ref[:, LANE:]
    for number, (chh, at) in enumerate(SERIES):
        real = waves[chh * 256 : chh * 256 + 128, at * LANE : (at + 1) * LANE]
        imag = waves[chh * 256 + 128 : chh * 256 + 256, at * LANE : (at + 1) * LANE]
        turned = jnp.concatenate([real * cos - imag * sin, real * sin + imag * cos], axis=1)
        upper, lower = cut(turned)
        freq = mxu(upper, second_ref[0]) + (mxu(lower, second_ref[0]) + mxu(upper, second_ref[1]))
        out_ref[:, :, number * 256 : (number + 1) * 256] = freq.reshape(16, 8, 256).astype(jnp.bfloat16)


def blocks_kernel(data_ref, out_ref, wave_ref, tap_ref):
    low = lax.broadcasted_iota(jnp.int32, (8, LANE), 0) < 4

    def value(yc, number, part):
        at = number * 256 + part * LANE
        return data_ref[yc, :, at : at + LANE].astype(jnp.float32)

    def swap(item):
        return pltpu.roll(item, 4, 0)

    previous = None
    blocks = [None] * 32
    for yc in range(16):
        real, imag = value(yc, 4, 0), value(yc, 4, 1)
        real_swap, imag_swap = swap(real), swap(imag)
        blocks[yc] = (jnp.where(low, real, real_swap), jnp.where(low, imag, imag_swap))
        blocks[16 + yc] = (jnp.where(low, real_swap, real), jnp.where(low, imag_swap, imag))
    for gap in range(32):
        real, imag = blocks[gap]
        if gap:
            real, imag = real + previous[1], imag - previous[0]
        tap_ref[0, gap] = real
        tap_ref[1, gap] = imag
        previous = blocks[gap]
    for pair in range(2):
        for yc in range(16):
            for part in range(2):
                even, odd = value(yc, 2 * pair, part), value(yc, 2 * pair + 1, part)
                wave_ref[part, yc] = jnp.where(low, even, swap(odd))
                wave_ref[part, 16 + yc] = jnp.where(low, swap(even), odd)
        sums = [None] * 32
        for start in range(0, 32, 4):
            total = [[None, None] for _ in range(4)]
            for source in range(start + 4):
                real, imag = wave_ref[0, source], wave_ref[1, source]
                for step in range(4):
                    gap = start + step - source
                    if gap < 0:
                        continue
                    tap_real, tap_imag = tap_ref[0, gap], tap_ref[1, gap]
                    new_real = real * tap_real - imag * tap_imag
                    new_imag = real * tap_imag + imag * tap_real
                    if total[step][0] is None:
                        total[step] = [new_real, new_imag]
                    else:
                        total[step] = [total[step][0] + new_real, total[step][1] + new_imag]
            for step in range(4):
                sums[start + step] = total[step]
                for part in range(2):
                    block = start + step
                    yc = block % 16
                    if block >= 16:
                        first = sums[yc][part]
                        second = total[step][part]
                        for member, joined in enumerate(
                            (jnp.where(low, first, swap(second)), jnp.where(low, swap(first), second))
                        ):
                            at = (2 * pair + member) * 256 + part * LANE
                            out_ref[yc, :, at : at + LANE] = joined.astype(jnp.bfloat16)


def behind_kernel(data_ref, second_ref, twist_ref, first_ref, out_ref):
    cos = twist_ref[:, :LANE]
    sin = twist_ref[:, LANE:]
    stacks = [[], []]
    for ch in range(4):
        block = data_ref[:, :, ch * 256 : (ch + 1) * 256].astype(jnp.float32).reshape(128, 256).astype(jnp.bfloat16)
        lines = mxu(block, second_ref[0]) + mxu(block, second_ref[1])
        real = lines[:, :LANE]
        imag = lines[:, LANE:]
        turned = jnp.concatenate([real * cos + imag * sin, imag * cos - real * sin], axis=0)
        stacks[ch // 2].append(turned)
    upper, lower = cut(jnp.concatenate([jnp.concatenate(side, axis=1) for side in stacks], axis=0))
    value = mxu(first_ref[0], upper) + (mxu(first_ref[0], lower) + mxu(first_ref[1], upper))
    out_ref[...] = value.reshape(32, 8, 2 * LANE).astype(jnp.bfloat16)


def gate_kernel(projected_ref, earlier_ref, taps_ref, gain_ref, data_ref, out_ref, ext_ref, rows_ref):
    filtered = short_filter(projected_ref, earlier_ref, taps_ref, ext_ref)
    mixture = mix_of(filtered).astype(jnp.float32)
    for at in range(2):
        rows_ref[at] = data_ref[:, :, at * LANE : (at + 1) * LANE].astype(jnp.float32).reshape(256, LANE)
    for hi in range(HIGH):
        rows = [rows_ref[ch % 2, pl.ds(ch // 2 * 4 + hi, 32, stride=8), :] for ch in range(4)]
        convolved = jnp.concatenate(rows, axis=0).T
        span = slice(hi * LANE, (hi + 1) * LANE)
        out_ref[span, :] = filtered[span, :LANE] * (convolved + gain_ref[...] * mixture[span, :])


def exchange(value, axis):
    return lax.all_to_all(value, axis, split_axis=0, concat_axis=0, tiled=True)


def on_device(projected, short_taps, skip_gain, long_filter):
    seg, wide = projected.shape
    channels = skip_gain.shape[0]
    count = lax.axis_size(EVERY)
    first, first_back, twist, second, second_back = tables()
    earlier = lax.ppermute(projected[seg - 8 :], EVERY, [(s, s + 1) for s in range(count - 1)])
    ext = pltpu.VMEM((seg + 8, wide), jnp.float32)
    packed = pl.pallas_call(
        pack_kernel,
        out_shape=jax.ShapeDtypeStruct((32, 8, 3 * LANE), jnp.bfloat16),
        scratch_shapes=[ext, pltpu.VMEM((3, 256, LANE), jnp.float32)],
        name="pack",
    )(projected, earlier, short_taps, long_filter.reshape(HIGH, LANE))
    arrived = exchange(packed, FIRST)
    ahead = pl.pallas_call(
        ahead_kernel,
        out_shape=jax.ShapeDtypeStruct((16, 8, 5 * 256), jnp.bfloat16),
        name="ahead",
    )(arrived, first, twist, second)
    lined = exchange(ahead, SECOND)
    blocks = pl.pallas_call(
        blocks_kernel,
        out_shape=jax.ShapeDtypeStruct((16, 8, 4 * 256), jnp.bfloat16),
        scratch_shapes=[pltpu.VMEM((2, 32, 8, LANE), jnp.float32), pltpu.VMEM((2, 32, 8, LANE), jnp.float32)],
        name="blocks",
    )(lined)
    returned = exchange(blocks, SECOND)
    behind = pl.pallas_call(
        behind_kernel,
        out_shape=jax.ShapeDtypeStruct((32, 8, 2 * LANE), jnp.bfloat16),
        name="behind",
    )(returned, second_back, twist, first_back)
    home = exchange(behind, FIRST)
    return pl.pallas_call(
        gate_kernel,
        out_shape=jax.ShapeDtypeStruct((seg, channels), jnp.float32),
        scratch_shapes=[ext, pltpu.VMEM((2, 256, LANE), jnp.float32)],
        name="gate",
    )(projected, earlier, short_taps, skip_gain.reshape(1, channels), home)


def solution(mesh):
    fine = Mesh(mesh.devices.reshape(SPLIT), EVERY)
    placed = (P(EVERY, None), P(), P(), P(EVERY))
    return jax.shard_map(on_device, mesh=fine, in_specs=placed, out_specs=P(EVERY, None), check_vma=False)
```

```python
import numpy as np

import jax
import jax.numpy as jnp
from jax import lax
from jax.experimental import pallas as pl
from jax.experimental.pallas import tpu as pltpu
from jax.sharding import Mesh, PartitionSpec as P

LANE = 128
FIRST = ("zh", "x", "zl")
SECOND = ("y", "core")
EVERY = ("zh", "y", "core", "x", "zl")
SPLIT = (2, 8, 2, 4, 4)
ZH = 2
INNER = 16
SPAN = 8192
LINES = 64
HIGH = 4
SERIES = ((0, 0), (0, 1), (0, 2), (1, 0), (1, 1))


def turn_of(phase):
    turn = 2.0 * np.pi * np.asarray(phase, np.float64)
    return np.cos(turn), np.sin(turn)


def halves(table):
    table = np.asarray(table, np.float32)
    upper = table.astype(jnp.bfloat16)
    lower = (table - upper.astype(np.float32)).astype(jnp.bfloat16)
    return np.stack([upper, lower])


def tables():
    line = np.arange(LINES)
    cos, sin = turn_of(np.outer(line + 0.25, line) / LINES)
    same = np.eye(ZH)

    def forward(part):
        small = part.reshape(INNER, HIGH, INNER, HIGH)
        return np.einsum("jkir,zw,cd->cjzkwidr", small, same, np.eye(2)).reshape(2, 128, 256)

    first = np.stack([forward(cos), forward(sin)], axis=1).reshape(512, 256)

    def backward(part):
        small = part.reshape(INNER, HIGH, INNER, HIGH) / SPAN
        return np.einsum("jkir,zw,cd->wicrdjzk", small, same, np.eye(2)).reshape(256, 2, 128)

    first_back = np.stack([backward(cos), backward(sin)], axis=2).reshape(256, 512)
    cos, sin = turn_of(np.outer(line + 0.25, np.arange(LANE)) / SPAN)
    rows = (np.arange(INNER)[:, None, None] * HIGH + np.zeros((1, ZH, 1), int) + np.arange(HIGH)).reshape(-1)
    twist = np.concatenate([cos[rows], sin[rows]], axis=1).astype(np.float32)
    cos, sin = turn_of(np.outer(np.arange(LANE), np.arange(LANE)) / LANE)
    second = np.block([[cos, sin], [-sin, cos]])
    ahead = halves(np.concatenate([first, second], axis=0))
    behind = halves(np.concatenate([first_back, second.T], axis=1))
    return ahead, behind, twist


def mxu(left, right):
    return jnp.dot(left, right, preferred_element_type=jnp.float32)


def cut(value):
    upper = value.astype(jnp.bfloat16)
    return upper, (value - upper.astype(jnp.float32)).astype(jnp.bfloat16)


def short_filter(ext_ref, taps, seg):
    total = taps[0:1, :] * ext_ref[8 : 8 + seg, :]
    for tap in range(1, taps.shape[0]):
        total = total + taps[tap : tap + 1, :] * ext_ref[8 - tap : 8 - tap + seg, :]
    return total


def mix_of(filtered):
    width = filtered.shape[1] // 3
    mixture = (filtered[:, width : 2 * width] * filtered[:, 2 * width :]).astype(jnp.bfloat16)
    return mixture.astype(jnp.float32)


def pack_kernel(
    projected_ref, taps_ref, gain_ref, filter_ref, rows_ref, queries_ref, direct_ref, head_ref, ext_ref
):
    seg = projected_ref.shape[0]
    ext_ref[0:8, :] = jnp.zeros((8, 3 * LANE), jnp.float32)
    ext_ref[8 : 8 + seg, :] = projected_ref[...].astype(jnp.float32)
    head_ref[0:8, :] = ext_ref[8:16, :]
    head_ref[8:11, :] = taps_ref[...]
    head_ref[16:17, 0:LANE] = gain_ref[...]
    filtered = short_filter(ext_ref, taps_ref[...], seg)
    mixture = mix_of(filtered)
    queries_ref[...] = filtered[:, :LANE]
    direct_ref[...] = gain_ref[...] * mixture
    for hi in range(HIGH):
        flipped = mixture[hi * LANE : (hi + 1) * LANE, :].T
        for ch in range(4):
            chh, at = SERIES[ch]
            rows_ref[at, pl.ds(chh * 4 + hi, 32, stride=8), :] = flipped[ch * 32 : (ch + 1) * 32, :]
        taps = jnp.broadcast_to(filter_ref[hi : hi + 1, :].astype(jnp.float32), (32, LANE))
        rows_ref[1, pl.ds(4 + hi, 32, stride=8), :] = taps
        rows_ref[2, pl.ds(4 + hi, 32, stride=8), :] = jnp.zeros((32, LANE), jnp.float32)


def mend_kernel(rows_ref, head_ref, earlier_ref, out_ref, fixed_ref, ext_ref, block_ref):
    ext_ref[0:8, :] = earlier_ref[...].astype(jnp.float32)
    ext_ref[8:16, :] = head_ref[0:8, :]
    filtered = short_filter(ext_ref, head_ref[8:11, :], 8)
    mixture = mix_of(filtered)
    fixed_ref[0:8, :] = filtered[:, :LANE]
    fixed_ref[8:16, :] = head_ref[16:17, 0:LANE] * mixture
    block_ref[...] = rows_ref[...]
    flipped = jnp.concatenate([mixture, jnp.zeros((LANE - 8, LANE), jnp.float32)], axis=0).T
    fresh = lax.broadcasted_iota(jnp.int32, (32, LANE), 1) < 8
    for ch in range(4):
        chh, at = SERIES[ch]
        where = pl.ds(chh * 4, 32, stride=8)
        block_ref[at, where, :] = jnp.where(fresh, flipped[ch * 32 : (ch + 1) * 32, :], block_ref[at, where, :])
    for at in range(3):
        out_ref[:, :, at * LANE : (at + 1) * LANE] = block_ref[at].reshape(32, 8, LANE).astype(jnp.bfloat16)


def ahead_kernel(data_ref, table_ref, twist_ref, out_ref):
    first_ref = table_ref.at[:, :512, :]
    second_ref = table_ref.at[:, 512:, :]
    data = data_ref[...].astype(jnp.float32).reshape(256, 3 * LANE).astype(jnp.bfloat16)
    waves = mxu(first_ref[0], data) + mxu(first_ref[1], data)
    cos = twist_ref[:, :LANE]
    sin = twist_ref[:, LANE:]
    for number, (chh, at) in enumerate(SERIES):
        real = waves[chh * 256 : chh * 256 + 128, at * LANE : (at + 1) * LANE]
        imag = waves[chh * 256 + 128 : chh * 256 + 256, at * LANE : (at + 1) * LANE]
        turned = jnp.concatenate([real * cos - imag * sin, real * sin + imag * cos], axis=1)
        upper, lower = cut(turned)
        freq = mxu(upper, second_ref[0]) + (mxu(lower, second_ref[0]) + mxu(upper, second_ref[1]))
        out_ref[:, :, number * 256 : (number + 1) * 256] = freq.reshape(16, 8, 256).astype(jnp.bfloat16)


def blocks_kernel(data_ref, out_ref, wave_ref, tap_ref):
    low = lax.broadcasted_iota(jnp.int32, (8, LANE), 0) < 4

    def value(yc, number, part):
        at = number * 256 + part * LANE
        return data_ref[yc, :, at : at + LANE].astype(jnp.float32)

    def swap(item):
        return pltpu.roll(item, 4, 0)

    previous = None
    blocks = [None] * 32
    for yc in range(16):
        real, imag = value(yc, 4, 0), value(yc, 4, 1)
        real_swap, imag_swap = swap(real), swap(imag)
        blocks[yc] = (jnp.where(low, real, real_swap), jnp.where(low, imag, imag_swap))
        blocks[16 + yc] = (jnp.where(low, real_swap, real), jnp.where(low, imag_swap, imag))
    for gap in range(32):
        real, imag = blocks[gap]
        if gap:
            real, imag = real + previous[1], imag - previous[0]
        tap_ref[0, gap] = real
        tap_ref[1, gap] = imag
        previous = blocks[gap]
    for pair in range(2):
        for yc in range(16):
            for part in range(2):
                even, odd = value(yc, 2 * pair, part), value(yc, 2 * pair + 1, part)
                wave_ref[part, yc] = jnp.where(low, even, swap(odd))
                wave_ref[part, 16 + yc] = jnp.where(low, swap(even), odd)
        sums = [None] * 32
        for start in range(0, 32, 4):
            total = [[None, None] for _ in range(4)]
            for source in range(start + 4):
                real, imag = wave_ref[0, source], wave_ref[1, source]
                for step in range(4):
                    gap = start + step - source
                    if gap < 0:
                        continue
                    tap_real, tap_imag = tap_ref[0, gap], tap_ref[1, gap]
                    new_real = real * tap_real - imag * tap_imag
                    new_imag = real * tap_imag + imag * tap_real
                    if total[step][0] is None:
                        total[step] = [new_real, new_imag]
                    else:
                        total[step] = [total[step][0] + new_real, total[step][1] + new_imag]
            for step in range(4):
                sums[start + step] = total[step]
                for part in range(2):
                    block = start + step
                    yc = block % 16
                    if block >= 16:
                        first = sums[yc][part]
                        second = total[step][part]
                        for member, joined in enumerate(
                            (jnp.where(low, first, swap(second)), jnp.where(low, swap(first), second))
                        ):
                            at = (2 * pair + member) * 256 + part * LANE
                            out_ref[yc, :, at : at + LANE] = joined.astype(jnp.bfloat16)


def behind_kernel(data_ref, table_ref, twist_ref, out_ref):
    first_ref = table_ref.at[:, :, :512]
    second_ref = table_ref.at[:, :, 512:]
    cos = twist_ref[:, :LANE]
    sin = twist_ref[:, LANE:]
    stacks = [[], []]
    for ch in range(4):
        block = data_ref[:, :, ch * 256 : (ch + 1) * 256].astype(jnp.float32).reshape(128, 256).astype(jnp.bfloat16)
        lines = mxu(block, second_ref[0]) + mxu(block, second_ref[1])
        real = lines[:, :LANE]
        imag = lines[:, LANE:]
        turned = jnp.concatenate([real * cos + imag * sin, imag * cos - real * sin], axis=0)
        stacks[ch // 2].append(turned)
    upper, lower = cut(jnp.concatenate([jnp.concatenate(side, axis=1) for side in stacks], axis=0))
    value = mxu(first_ref[0], upper) + (mxu(first_ref[0], lower) + mxu(first_ref[1], upper))
    out_ref[...] = value.reshape(32, 8, 2 * LANE).astype(jnp.bfloat16)


def gate_kernel(queries_ref, direct_ref, fixed_ref, data_ref, out_ref, rows_ref):
    for at in range(2):
        rows_ref[at] = data_ref[:, :, at * LANE : (at + 1) * LANE].astype(jnp.float32).reshape(256, LANE)
    for hi in range(HIGH):
        rows = [rows_ref[ch % 2, pl.ds(ch // 2 * 4 + hi, 32, stride=8), :] for ch in range(4)]
        convolved = jnp.concatenate(rows, axis=0).T
        span = slice(hi * LANE, (hi + 1) * LANE)
        out_ref[span, :] = queries_ref[span, :] * (convolved + direct_ref[span, :])
        if hi == 0:
            out_ref[0:8, :] = fixed_ref[0:8, :] * (convolved[0:8, :] + fixed_ref[8:16, :])


def exchange(value, axis):
    return lax.all_to_all(value, axis, split_axis=0, concat_axis=0, tiled=True)


def on_chip(kernel, outs, scratch, name, *args):
    near = pl.BlockSpec(memory_space=pltpu.VMEM)
    return pl.pallas_call(
        kernel,
        in_specs=[near] * len(args),
        out_specs=tuple(near for _ in outs) if len(outs) > 1 else near,
        out_shape=outs if len(outs) > 1 else outs[0],
        scratch_shapes=scratch,
        name=name,
    )(*[pltpu.with_memory_space_constraint(arg, pltpu.VMEM) for arg in args])


def on_device(projected, short_taps, skip_gain, long_filter):
    seg, wide = projected.shape
    channels = skip_gain.shape[0]
    count = lax.axis_size(EVERY)
    near = pl.BlockSpec(memory_space=pltpu.VMEM)
    ahead_table, behind_table, twist = tables()
    earlier = lax.ppermute(projected[seg - 8 :], EVERY, [(s, s + 1) for s in range(count - 1)])
    plane = pltpu.VMEM((seg, channels), jnp.float32)
    stack = pltpu.VMEM((3, 256, LANE), jnp.float32)
    rows, queries, direct, head = pl.pallas_call(
        pack_kernel,
        out_specs=(near, near, near, near),
        out_shape=(stack, plane, plane, pltpu.VMEM((24, wide), jnp.float32)),
        scratch_shapes=[pltpu.VMEM((seg + 8, wide), jnp.float32)],
        name="pack",
    )(projected, short_taps, skip_gain.reshape(1, channels), long_filter.reshape(HIGH, LANE))
    packed, fixed = on_chip(
        mend_kernel,
        (pltpu.VMEM((32, 8, 3 * LANE), jnp.bfloat16), pltpu.VMEM((16, channels), jnp.float32)),
        [pltpu.VMEM((16, wide), jnp.float32), stack],
        "mend",
        rows,
        head,
        earlier,
    )
    arrived = exchange(packed, FIRST)
    ahead = on_chip(
        ahead_kernel, (pltpu.VMEM((16, 8, 5 * 256), jnp.bfloat16),), [], "ahead", arrived, ahead_table, twist
    )
    lined = exchange(ahead, SECOND)
    store = pltpu.VMEM((2, 32, 8, LANE), jnp.float32)
    blocks = on_chip(blocks_kernel, (pltpu.VMEM((16, 8, 4 * 256), jnp.bfloat16),), [store, store], "blocks", lined)
    returned = exchange(blocks, SECOND)
    behind = on_chip(
        behind_kernel, (pltpu.VMEM((32, 8, 2 * LANE), jnp.bfloat16),), [], "behind", returned, behind_table, twist
    )
    home = exchange(behind, FIRST)
    return pl.pallas_call(
        gate_kernel,
        in_specs=[near] * 4,
        out_shape=jax.ShapeDtypeStruct((seg, channels), jnp.float32),
        scratch_shapes=[pltpu.VMEM((2, 256, LANE), jnp.float32)],
        name="gate",
    )(*[pltpu.with_memory_space_constraint(arg, pltpu.VMEM) for arg in (queries, direct, fixed, home)])


def solution(mesh):
    fine = Mesh(mesh.devices.reshape(SPLIT), EVERY)
    placed = (P(EVERY, None), P(), P(), P(EVERY))
    return jax.shard_map(on_device, mesh=fine, in_specs=placed, out_specs=P(EVERY, None), check_vma=False)
```

```python
import numpy as np

import jax
import jax.numpy as jnp
from jax import lax
from jax.experimental import pallas as pl
from jax.experimental.pallas import tpu as pltpu
from jax.sharding import Mesh, PartitionSpec as P

LANE = 128
FIRST = ("zh", "y", "zl")
SECOND = ("core", "x")
EVERY = ("zh", "y", "core", "x", "zl")
SPLIT = (2, 8, 2, 4, 4)
PEERS = 64
BLOCKS = 16
PLANES = 8
HIGH = 4
RUN = 4
SPAN = 2048
LINES = 16
KQ = 2
WAVES = 256


def turn_of(phase):
    turn = 2.0 * np.pi * np.asarray(phase, np.float64)
    return np.cos(turn), np.sin(turn)


def halves(table):
    table = np.asarray(table, np.float32)
    upper = table.astype(jnp.bfloat16)
    lower = (table - upper.astype(np.float32)).astype(jnp.bfloat16)
    return np.stack([upper, lower])


def tables():
    line = np.arange(LINES)
    same = np.eye(BLOCKS)
    cos, sin = turn_of(np.outer(line + 0.25, line) / LINES)

    def forward(part):
        small = part.reshape(PLANES, KQ, RUN, HIGH)
        return np.einsum("jkzr,bc->kjbczr", small, same).reshape(256, 256)

    def backward(part):
        small = part.reshape(PLANES, KQ, RUN, HIGH) / SPAN
        return np.einsum("jkzr,bc->rczkjb", small, same).reshape(256, 256)

    first = np.concatenate([forward(cos), forward(sin)], axis=0)
    first_back = np.concatenate([backward(cos), backward(sin)], axis=1)
    cos, sin = turn_of(np.outer(line + 0.25, np.arange(LANE)) / SPAN)
    rows = np.broadcast_to(line.reshape(PLANES, KQ).T[:, :, None], (KQ, PLANES, BLOCKS)).reshape(-1)
    twist = np.concatenate([cos[rows], sin[rows]], axis=1).astype(np.float32)
    cos, sin = turn_of(np.outer(np.arange(LANE), np.arange(LANE)) / LANE)
    second = np.block([[cos, sin], [-sin, cos]])
    block = (np.arange(BLOCKS)[None, :] * PLANES + np.arange(PLANES)[:, None]).reshape(-1)
    wave = np.arange(WAVES)
    cos, sin = turn_of(np.outer(wave, block) / WAVES)
    over = np.block([[cos, sin], [-sin, cos]])
    cos_before, sin_before = turn_of(np.outer(wave, block - 1) / WAVES)
    real = (cos + sin_before).T / WAVES
    imag = (sin - cos_before).T / WAVES
    under = np.block([[real, -imag], [imag, real]])
    ahead = halves(np.concatenate([first, second], axis=0))
    behind = halves(np.concatenate([first_back, second.T], axis=1))
    return ahead, behind, halves(over), halves(under), twist


def mxu(left, right):
    return jnp.dot(left, right, preferred_element_type=jnp.float32)


def cut(value):
    upper = value.astype(jnp.bfloat16)
    return upper, (value - upper.astype(jnp.float32)).astype(jnp.bfloat16)


def short_filter(ext_ref, taps, seg):
    total = taps[0:1, :] * ext_ref[8 : 8 + seg, :]
    for tap in range(1, taps.shape[0]):
        total = total + taps[tap : tap + 1, :] * ext_ref[8 - tap : 8 - tap + seg, :]
    return total


def mix_of(filtered):
    width = filtered.shape[1] // 3
    mixture = (filtered[:, width : 2 * width] * filtered[:, 2 * width :]).astype(jnp.bfloat16)
    return mixture.astype(jnp.float32)


def pack_kernel(
    projected_ref, taps_ref, gain_ref, filter_ref, rows_ref, queries_ref, direct_ref, head_ref, ext_ref
):
    seg = projected_ref.shape[0]
    ext_ref[0:8, :] = jnp.zeros((8, 3 * LANE), jnp.float32)
    ext_ref[8 : 8 + seg, :] = projected_ref[...].astype(jnp.float32)
    head_ref[0:8, :] = ext_ref[8:16, :]
    head_ref[8:11, :] = taps_ref[...]
    head_ref[16:17, 0:LANE] = gain_ref[...]
    filtered = short_filter(ext_ref, taps_ref[...], seg)
    mixture = mix_of(filtered)
    queries_ref[...] = filtered[:, :LANE]
    direct_ref[...] = gain_ref[...] * mixture
    for hi in range(HIGH):
        flipped = mixture[hi * LANE : (hi + 1) * LANE, :].T
        where = pl.ds(hi, PEERS, stride=HIGH)
        for ch in range(2):
            rows_ref[ch, where, :] = flipped[ch * PEERS : (ch + 1) * PEERS, :]
        taps = filter_ref[hi : hi + 1, :].astype(jnp.float32)
        rows_ref[2, where, :] = jnp.broadcast_to(taps, (PEERS, LANE))


def mend_kernel(rows_ref, head_ref, earlier_ref, out_ref, fixed_ref, ext_ref, block_ref):
    ext_ref[0:8, :] = earlier_ref[...].astype(jnp.float32)
    ext_ref[8:16, :] = head_ref[0:8, :]
    filtered = short_filter(ext_ref, head_ref[8:11, :], 8)
    mixture = mix_of(filtered)
    fixed_ref[0:8, :] = filtered[:, :LANE]
    fixed_ref[8:16, :] = head_ref[16:17, 0:LANE] * mixture
    block_ref[...] = rows_ref[...]
    flipped = jnp.concatenate([mixture, jnp.zeros((LANE - 8, LANE), jnp.float32)], axis=0).T
    fresh = lax.broadcasted_iota(jnp.int32, (PEERS, LANE), 1) < 8
    where = pl.ds(0, PEERS, stride=HIGH)
    for ch in range(2):
        block_ref[ch, where, :] = jnp.where(fresh, flipped[ch * PEERS : (ch + 1) * PEERS, :], block_ref[ch, where, :])
    for at in range(3):
        out_ref[:, :, at * LANE : (at + 1) * LANE] = block_ref[at].reshape(PEERS, HIGH, LANE).astype(jnp.bfloat16)


def ahead_kernel(data_ref, table_ref, twist_ref, out_ref):
    data = data_ref[...].astype(jnp.float32).reshape(256, 3 * LANE).astype(jnp.bfloat16)
    waves = mxu(table_ref[0, :512, :], data) + mxu(table_ref[1, :512, :], data)
    cos = twist_ref[:, :LANE]
    sin = twist_ref[:, LANE:]
    for number in range(3):
        real = waves[:256, number * LANE : (number + 1) * LANE]
        imag = waves[256:, number * LANE : (number + 1) * LANE]
        upper, lower = cut(jnp.concatenate([real * cos - imag * sin, real * sin + imag * cos], axis=1))
        second = table_ref[0, 512:, :]
        freq = mxu(upper, second) + (mxu(lower, second) + mxu(upper, table_ref[1, 512:, :]))
        for kq in range(KQ):
            at = (kq * 3 + number) * 256
            value = freq[kq * 128 : (kq + 1) * 128, :].reshape(PLANES, BLOCKS, 256)
            out_ref[:, :, at : at + 256] = value.astype(jnp.bfloat16)


def blocks_kernel(data_ref, over_ref, under_ref, out_ref):
    def piece(kq, number, part):
        at = ((kq * 3 + number) * 2 + part) * LANE
        return data_ref[:, :, at : at + LANE].astype(jnp.float32).reshape(128, LANE)

    columns = []
    for kq in range(KQ):
        for number in range(3):
            columns.append(jnp.concatenate([piece(kq, number, 0), piece(kq, number, 1)], axis=0))
    data = jnp.concatenate(columns, axis=1).astype(jnp.bfloat16)
    waves = mxu(over_ref[0], data) + mxu(over_ref[1], data)
    products = []
    for kq in range(KQ):
        at = (kq * 3 + 2) * LANE
        tap_real = waves[:WAVES, at : at + LANE]
        tap_imag = waves[WAVES:, at : at + LANE]
        for ch in range(2):
            at = (kq * 3 + ch) * LANE
            real = waves[:WAVES, at : at + LANE]
            imag = waves[WAVES:, at : at + LANE]
            both = [real * tap_real - imag * tap_imag, real * tap_imag + imag * tap_real]
            products.append(jnp.concatenate(both, axis=0))
    upper, lower = cut(jnp.concatenate(products, axis=1))
    sums = mxu(under_ref[0], upper) + (mxu(under_ref[0], lower) + mxu(under_ref[1], upper))
    for kq in range(KQ):
        for ch in range(2):
            for part in range(2):
                at = (kq * 2 + ch) * LANE
                value = sums[part * 128 : (part + 1) * 128, at : at + LANE].reshape(PLANES, BLOCKS, LANE)
                to = (at // LANE * 2 + part) * LANE
                out_ref[:, :, to : to + LANE] = value.astype(jnp.bfloat16)


def behind_kernel(data_ref, table_ref, twist_ref, out_ref, rows_ref):
    columns = []
    for ch in range(2):
        parts = [[], []]
        for kq in range(KQ):
            at = (kq * 2 + ch) * 256
            block = data_ref[:, :, at : at + 256].astype(jnp.float32).reshape(128, 256).astype(jnp.bfloat16)
            lines = mxu(block, table_ref[0, :, 512:]) + mxu(block, table_ref[1, :, 512:])
            cos = twist_ref[kq * 128 : (kq + 1) * 128, :LANE]
            sin = twist_ref[kq * 128 : (kq + 1) * 128, LANE:]
            real = lines[:, :LANE]
            imag = lines[:, LANE:]
            parts[0].append(real * cos + imag * sin)
            parts[1].append(imag * cos - real * sin)
        columns.append(jnp.concatenate(parts[0] + parts[1], axis=0))
    upper, lower = cut(jnp.concatenate(columns, axis=1))
    first = table_ref[0, :, :512]
    value = mxu(first, upper) + (mxu(first, lower) + mxu(table_ref[1, :, :512], upper))
    for hi in range(HIGH):
        for ch in range(2):
            where = pl.ds(ch * HIGH + hi, PEERS, stride=8)
            rows_ref[where, :] = value[hi * PEERS : (hi + 1) * PEERS, ch * LANE : (ch + 1) * LANE]
    out_ref[...] = rows_ref[...].reshape(PEERS, 8, LANE).astype(jnp.bfloat16)


def gate_kernel(queries_ref, direct_ref, fixed_ref, data_ref, out_ref, rows_ref):
    rows_ref[...] = data_ref[...].astype(jnp.float32).reshape(8 * PEERS, LANE)
    for hi in range(HIGH):
        rows = [rows_ref[pl.ds(ch * HIGH + hi, PEERS, stride=8), :] for ch in range(2)]
        convolved = jnp.concatenate(rows, axis=0).T
        span = slice(hi * LANE, (hi + 1) * LANE)
        out_ref[span, :] = queries_ref[span, :] * (convolved + direct_ref[span, :])
        if hi == 0:
            out_ref[0:8, :] = fixed_ref[0:8, :] * (convolved[0:8, :] + fixed_ref[8:16, :])


def exchange(value, axis):
    return lax.all_to_all(value, axis, split_axis=0, concat_axis=0, tiled=True)


def on_chip(kernel, outs, scratch, name, *args):
    near = pl.BlockSpec(memory_space=pltpu.VMEM)
    return pl.pallas_call(
        kernel,
        in_specs=[near] * len(args),
        out_specs=tuple(near for _ in outs) if len(outs) > 1 else near,
        out_shape=outs if len(outs) > 1 else outs[0],
        scratch_shapes=scratch,
        name=name,
    )(*[pltpu.with_memory_space_constraint(arg, pltpu.VMEM) for arg in args])


def on_device(projected, short_taps, skip_gain, long_filter):
    seg, wide = projected.shape
    channels = skip_gain.shape[0]
    count = lax.axis_size(EVERY)
    near = pl.BlockSpec(memory_space=pltpu.VMEM)
    ahead_table, behind_table, over, under, twist = tables()
    earlier = lax.ppermute(projected[seg - 8 :], EVERY, [(s, s + 1) for s in range(count - 1)])
    plane = pltpu.VMEM((seg, channels), jnp.float32)
    stack = pltpu.VMEM((3, 256, LANE), jnp.float32)
    rows, queries, direct, head = pl.pallas_call(
        pack_kernel,
        out_specs=(near, near, near, near),
        out_shape=(stack, plane, plane, pltpu.VMEM((24, wide), jnp.float32)),
        scratch_shapes=[pltpu.VMEM((seg + 8, wide), jnp.float32)],
        name="pack",
    )(projected, short_taps, skip_gain.reshape(1, channels), long_filter.reshape(HIGH, LANE))
    packed, fixed = on_chip(
        mend_kernel,
        (pltpu.VMEM((PEERS, HIGH, 3 * LANE), jnp.bfloat16), pltpu.VMEM((16, channels), jnp.float32)),
        [pltpu.VMEM((16, wide), jnp.float32), stack],
        "mend",
        rows,
        head,
        earlier,
    )
    arrived = exchange(packed, FIRST)
    ahead = on_chip(
        ahead_kernel,
        (pltpu.VMEM((PLANES, BLOCKS, KQ * 3 * 256), jnp.bfloat16),),
        [],
        "ahead",
        arrived,
        ahead_table,
        twist,
    )
    lined = exchange(ahead, SECOND)
    blocks = on_chip(
        blocks_kernel,
        (pltpu.VMEM((PLANES, BLOCKS, KQ * 2 * 256), jnp.bfloat16),),
        [],
        "blocks",
        lined,
        over,
        under,
    )
    returned = exchange(blocks, SECOND)
    behind = on_chip(
        behind_kernel,
        (pltpu.VMEM((PEERS, 8, LANE), jnp.bfloat16),),
        [pltpu.VMEM((8 * PEERS, LANE), jnp.float32)],
        "behind",
        returned,
        behind_table,
        twist,
    )
    home = exchange(behind, FIRST)
    return pl.pallas_call(
        gate_kernel,
        in_specs=[near] * 4,
        out_shape=jax.ShapeDtypeStruct((seg, channels), jnp.float32),
        scratch_shapes=[pltpu.VMEM((8 * PEERS, LANE), jnp.float32)],
        name="gate",
    )(*[pltpu.with_memory_space_constraint(arg, pltpu.VMEM) for arg in (queries, direct, fixed, home)])


def solution(mesh):
    fine = Mesh(mesh.devices.reshape(SPLIT), EVERY)
    placed = (P(EVERY, None), P(), P(), P(EVERY))
    return jax.shard_map(on_device, mesh=fine, in_specs=placed, out_specs=P(EVERY, None), check_vma=False)
```

```python
import numpy as np

import jax
import jax.numpy as jnp
from jax import lax
from jax.experimental import pallas as pl
from jax.experimental.pallas import tpu as pltpu
from jax.sharding import Mesh, PartitionSpec as P

LANE = 128
FIRST = ("zh", "y", "zl")
SECOND = ("core", "x")
EVERY = ("zh", "y", "core", "x", "zl")
SPLIT = (2, 8, 2, 4, 4)
PEERS = 64
BLOCKS = 16
PLANES = 8
HIGH = 4
RUN = 4
SPAN = 2048
LINES = 16
KQ = 2
WAVES = 256
EDGE = ((0, 0), (1, 0), (0, 1), (1, 1), (2, 0), (3, 0), (2, 1), (3, 1))


def turn_of(phase):
    turn = 2.0 * np.pi * np.asarray(phase, np.float64)
    return np.cos(turn), np.sin(turn)


def halves(table):
    table = np.asarray(table, np.float32)
    upper = table.astype(jnp.bfloat16)
    lower = (table - upper.astype(np.float32)).astype(jnp.bfloat16)
    return np.stack([upper, lower])


def tables():
    line = np.arange(LINES)
    same = np.eye(BLOCKS)
    cos, sin = turn_of(np.outer(line + 0.25, line) / LINES)

    def forward(part):
        small = part.reshape(PLANES, KQ, RUN, HIGH)
        return np.einsum("jkzr,bc->kjbczr", small, same).reshape(256, 256)

    def backward(part):
        small = part.reshape(PLANES, KQ, RUN, HIGH) / SPAN
        return np.einsum("jkzr,bc->rczkjb", small, same).reshape(256, 256)

    first = np.concatenate([forward(cos), forward(sin)], axis=0)
    first_back = np.concatenate([backward(cos), backward(sin)], axis=1)
    cos, sin = turn_of(np.outer(line + 0.25, np.arange(LANE)) / SPAN)
    rows = np.broadcast_to(line.reshape(PLANES, KQ).T[:, :, None], (KQ, PLANES, BLOCKS)).reshape(-1)
    twist = np.concatenate([cos[rows], sin[rows]], axis=1).astype(np.float32)
    cos, sin = turn_of(np.outer(np.arange(LANE), np.arange(LANE)) / LANE)
    second = np.block([[cos, sin], [-sin, cos]])
    block = (np.arange(BLOCKS)[None, :] * PLANES + np.arange(PLANES)[:, None]).reshape(-1)
    wave = np.arange(WAVES)
    cos, sin = turn_of(np.outer(wave, block) / WAVES)
    over = np.block([[cos, sin], [-sin, cos]])
    cos_before, sin_before = turn_of(np.outer(wave, block - 1) / WAVES)
    real = (cos + sin_before).T / WAVES
    imag = (sin - cos_before).T / WAVES
    under = np.block([[real, -imag], [imag, real]])
    spot = line.reshape(PLANES, KQ, 1) + LINES * np.arange(LANE) + 0.25
    omega = np.stack(turn_of(spot / SPAN), axis=2).reshape(PLANES, 2 * KQ, LANE)
    omega = np.concatenate([omega, np.zeros_like(omega)], axis=1).astype(np.float32)
    ahead = halves(np.concatenate([first, second], axis=0))
    behind = halves(np.concatenate([first_back, second.T], axis=1))
    return ahead, behind, halves(over), halves(under), twist, omega


def mxu(left, right):
    return jnp.dot(left, right, preferred_element_type=jnp.float32)


def cut(value):
    upper = value.astype(jnp.bfloat16)
    return upper, (value - upper.astype(jnp.float32)).astype(jnp.bfloat16)


def short_filter(ext_ref, taps, seg):
    total = taps[0:1, :] * ext_ref[8 : 8 + seg, :]
    for tap in range(1, taps.shape[0]):
        total = total + taps[tap : tap + 1, :] * ext_ref[8 - tap : 8 - tap + seg, :]
    return total


def pack_kernel(projected_ref, taps_ref, filter_ref, out_ref, ext_ref, rows_ref):
    seg = projected_ref.shape[0]
    ext_ref[0:8, :] = jnp.zeros((8, 2 * LANE), jnp.float32)
    ext_ref[8 : 8 + seg, :] = projected_ref[:, LANE:].astype(jnp.float32)
    taps = taps_ref[:, LANE:]
    filtered = short_filter(ext_ref, taps, seg)
    mixture = (filtered[:, :LANE] * filtered[:, LANE:]).astype(jnp.bfloat16).astype(jnp.float32)
    last = ext_ref[7 + seg : 8 + seg, :]
    carry = taps[1:2, :] * last + taps[2:3, :] * ext_ref[6 + seg : 7 + seg, :]
    ends = [filtered[0:1, :], filtered[1:2, :], carry, taps[2:3, :] * last]
    ends = [ends[row][:, half * LANE : (half + 1) * LANE] for row, half in EDGE]
    upper, lower = cut(jnp.concatenate(ends, axis=0))
    pad = jnp.zeros((LANE - 16, LANE), jnp.float32)
    flipped = jnp.concatenate([upper.astype(jnp.float32), lower.astype(jnp.float32), pad], axis=0).T
    lane = lax.broadcasted_iota(jnp.int32, (PEERS, LANE), 1)
    edges = jnp.where(lane < 16, flipped[:PEERS, :], pltpu.roll(flipped[PEERS:, :], 16, 1))
    for hi in range(HIGH):
        flipped = mixture[hi * LANE : (hi + 1) * LANE, :].T
        where = pl.ds(hi, PEERS, stride=HIGH)
        for ch in range(2):
            rows_ref[ch, where, :] = flipped[ch * PEERS : (ch + 1) * PEERS, :]
        taps_row = filter_ref[hi : hi + 1, :].astype(jnp.float32)
        rows_ref[2, where, :] = jnp.broadcast_to(taps_row, (PEERS, LANE))
        rows_ref[3, where, :] = edges
    for at in range(4):
        out_ref[:, :, at * LANE : (at + 1) * LANE] = rows_ref[at].reshape(PEERS, HIGH, LANE).astype(jnp.bfloat16)


def plan_kernel(projected_ref, earlier_ref, taps_ref, gain_ref, queries_ref, direct_ref, ext_ref):
    seg = projected_ref.shape[0]
    ext_ref[0:8, :] = earlier_ref[...].astype(jnp.float32)
    ext_ref[8 : 8 + seg, :] = projected_ref[...].astype(jnp.float32)
    filtered = short_filter(ext_ref, taps_ref[...], seg)
    mixture = (filtered[:, LANE : 2 * LANE] * filtered[:, 2 * LANE :]).astype(jnp.bfloat16)
    queries_ref[...] = filtered[:, :LANE]
    direct_ref[...] = gain_ref[...] * mixture.astype(jnp.float32)


def back(value, lanes):
    return pltpu.roll(value, LANE - lanes, 1)


def whole_edges(edges):
    return edges + back(edges, 8)


def rows_of(own, before):
    total = own + before
    return (total * back(total, 2)).astype(jnp.bfloat16).astype(jnp.float32)


def ahead_kernel(data_ref, table_ref, twist_ref, out_ref, rows_ref, edge_ref):
    for at in range(4):
        block = data_ref[:, :, at * LANE : (at + 1) * LANE].astype(jnp.float32)
        rows_ref[at] = block.reshape(256, LANE)
    where = pl.ds(0, PEERS, stride=HIGH)
    edges = rows_ref[3, where, :]
    edge_ref[...] = edges
    own = whole_edges(edges)
    mixture = rows_of(own, pltpu.roll(back(own, 4), 1, 0))
    inside = (lax.broadcasted_iota(jnp.int32, (PEERS, LANE), 0) & (RUN - 1)) != 0
    lane = lax.broadcasted_iota(jnp.int32, (PEERS, LANE), 1)
    mixture = jnp.where(inside, mixture, 0.0)
    for ch in range(2):
        fresh = back(mixture, 16 * ch) if ch else mixture
        rows_ref[ch, where, :] = jnp.where(lane < 2, fresh, rows_ref[ch, where, :])
    opening = edge_ref[pl.ds(0, BLOCKS, stride=RUN), :]
    closing = edge_ref[pl.ds(RUN - 1, BLOCKS, stride=RUN), :]
    outside = jnp.where((lane[:BLOCKS, :] & 4) == 0, opening, closing).astype(jnp.bfloat16)
    for plane in range(PLANES):
        out_ref[plane, :, KQ * 3 * 256 :] = outside
    data = jnp.concatenate([rows_ref[0], rows_ref[1], rows_ref[2]], axis=1).astype(jnp.bfloat16)
    waves = mxu(table_ref[0, :512, :], data) + mxu(table_ref[1, :512, :], data)
    cos = twist_ref[:, :LANE]
    sin = twist_ref[:, LANE:]
    for number in range(3):
        real = waves[:256, number * LANE : (number + 1) * LANE]
        imag = waves[256:, number * LANE : (number + 1) * LANE]
        upper, lower = cut(jnp.concatenate([real * cos - imag * sin, real * sin + imag * cos], axis=1))
        second = table_ref[0, 512:, :]
        freq = mxu(upper, second) + (mxu(lower, second) + mxu(upper, table_ref[1, 512:, :]))
        for kq in range(KQ):
            at = (kq * 3 + number) * 256
            value = freq[kq * 128 : (kq + 1) * 128, :].reshape(PLANES, BLOCKS, 256)
            out_ref[:, :, at : at + 256] = value.astype(jnp.bfloat16)


def blocks_kernel(data_ref, over_ref, under_ref, omega_ref, out_ref):
    omega = omega_ref[lax.axis_index(SECOND)]
    owns = [whole_edges(data_ref[plane, :, KQ * 3 * 256 :].astype(jnp.float32)) for plane in range(PLANES)]
    row = lax.broadcasted_iota(jnp.int32, (BLOCKS, LANE), 0)
    wrapped = jnp.where(row == 0, 0.0, pltpu.roll(back(owns[PLANES - 1], 4), 1, 0))
    befores = [wrapped] + [back(own, 4) for own in owns[:-1]]
    opening = jnp.concatenate([rows_of(own, before) for own, before in zip(owns, befores)], axis=0)

    def piece(kq, number, part):
        at = ((kq * 3 + number) * 2 + part) * LANE
        value = data_ref[:, :, at : at + LANE].astype(jnp.float32).reshape(128, LANE)
        if number == 2:
            return value
        second = opening[:, 16 * number + 1 : 16 * number + 2] * omega[2 * kq + part : 2 * kq + part + 1, :]
        if part == 0:
            second = second + opening[:, 16 * number : 16 * number + 1]
        return value + second

    columns = []
    for kq in range(KQ):
        for number in range(3):
            columns.append(jnp.concatenate([piece(kq, number, 0), piece(kq, number, 1)], axis=0))
    upper, lower = cut(jnp.concatenate(columns, axis=1))
    waves = mxu(over_ref[0], upper) + (mxu(over_ref[0], lower) + mxu(over_ref[1], upper))
    products = []
    for kq in range(KQ):
        at = (kq * 3 + 2) * LANE
        tap_real = waves[:WAVES, at : at + LANE]
        tap_imag = waves[WAVES:, at : at + LANE]
        for ch in range(2):
            at = (kq * 3 + ch) * LANE
            real = waves[:WAVES, at : at + LANE]
            imag = waves[WAVES:, at : at + LANE]
            both = [real * tap_real - imag * tap_imag, real * tap_imag + imag * tap_real]
            products.append(jnp.concatenate(both, axis=0))
    upper, lower = cut(jnp.concatenate(products, axis=1))
    sums = mxu(under_ref[0], upper) + (mxu(under_ref[0], lower) + mxu(under_ref[1], upper))
    for kq in range(KQ):
        for ch in range(2):
            for part in range(2):
                at = (kq * 2 + ch) * LANE
                value = sums[part * 128 : (part + 1) * 128, at : at + LANE].reshape(PLANES, BLOCKS, LANE)
                to = (at // LANE * 2 + part) * LANE
                out_ref[:, :, to : to + LANE] = value.astype(jnp.bfloat16)


def behind_kernel(data_ref, table_ref, twist_ref, out_ref, rows_ref):
    columns = []
    for ch in range(2):
        parts = [[], []]
        for kq in range(KQ):
            at = (kq * 2 + ch) * 256
            block = data_ref[:, :, at : at + 256].astype(jnp.float32).reshape(128, 256).astype(jnp.bfloat16)
            lines = mxu(block, table_ref[0, :, 512:]) + mxu(block, table_ref[1, :, 512:])
            cos = twist_ref[kq * 128 : (kq + 1) * 128, :LANE]
            sin = twist_ref[kq * 128 : (kq + 1) * 128, LANE:]
            real = lines[:, :LANE]
            imag = lines[:, LANE:]
            parts[0].append(real * cos + imag * sin)
            parts[1].append(imag * cos - real * sin)
        columns.append(jnp.concatenate(parts[0] + parts[1], axis=0))
    upper, lower = cut(jnp.concatenate(columns, axis=1))
    first = table_ref[0, :, :512]
    value = mxu(first, upper) + (mxu(first, lower) + mxu(table_ref[1, :, :512], upper))
    for hi in range(HIGH):
        for ch in range(2):
            where = pl.ds(ch * HIGH + hi, PEERS, stride=8)
            rows_ref[where, :] = value[hi * PEERS : (hi + 1) * PEERS, ch * LANE : (ch + 1) * LANE]
    out_ref[...] = rows_ref[...].reshape(PEERS, 8, LANE).astype(jnp.bfloat16)


def gate_kernel(queries_ref, direct_ref, data_ref, out_ref, rows_ref):
    rows_ref[...] = data_ref[...].astype(jnp.float32).reshape(8 * PEERS, LANE)
    for hi in range(HIGH):
        rows = [rows_ref[pl.ds(ch * HIGH + hi, PEERS, stride=8), :] for ch in range(2)]
        convolved = jnp.concatenate(rows, axis=0).T
        span = slice(hi * LANE, (hi + 1) * LANE)
        out_ref[span, :] = queries_ref[span, :] * (convolved + direct_ref[span, :])


def exchange(value, axis):
    return lax.all_to_all(value, axis, split_axis=0, concat_axis=0, tiled=True)


def on_chip(kernel, outs, scratch, name, *args):
    near = pl.BlockSpec(memory_space=pltpu.VMEM)
    return pl.pallas_call(
        kernel,
        in_specs=[near] * len(args),
        out_specs=tuple(near for _ in outs) if len(outs) > 1 else near,
        out_shape=outs if len(outs) > 1 else outs[0],
        scratch_shapes=scratch,
        name=name,
    )(*[pltpu.with_memory_space_constraint(arg, pltpu.VMEM) for arg in args])


def on_device(projected, short_taps, skip_gain, long_filter):
    seg, wide = projected.shape
    channels = skip_gain.shape[0]
    count = lax.axis_size(EVERY)
    near = pl.BlockSpec(memory_space=pltpu.VMEM)
    ahead_table, behind_table, over, under, twist, omega = tables()
    earlier = lax.ppermute(projected[seg - 8 :], EVERY, [(s, s + 1) for s in range(count - 1)])
    plane = pltpu.VMEM((seg, channels), jnp.float32)
    stack = pltpu.VMEM((4, 256, LANE), jnp.float32)
    packed = pl.pallas_call(
        pack_kernel,
        out_specs=near,
        out_shape=pltpu.VMEM((PEERS, HIGH, 4 * LANE), jnp.bfloat16),
        scratch_shapes=[pltpu.VMEM((seg + 8, 2 * LANE), jnp.float32), stack],
        name="pack",
    )(projected, short_taps, long_filter.reshape(HIGH, LANE))
    queries, direct = pl.pallas_call(
        plan_kernel,
        out_specs=(near, near),
        out_shape=(plane, plane),
        scratch_shapes=[pltpu.VMEM((seg + 8, wide), jnp.float32)],
        name="plan",
    )(projected, earlier, short_taps, skip_gain.reshape(1, channels))
    arrived = exchange(packed, FIRST)
    ahead = on_chip(
        ahead_kernel,
        (pltpu.VMEM((PLANES, BLOCKS, KQ * 3 * 256 + LANE), jnp.bfloat16),),
        [stack, pltpu.VMEM((PEERS, LANE), jnp.float32)],
        "ahead",
        arrived,
        ahead_table,
        twist,
    )
    lined = exchange(ahead, SECOND)
    blocks = on_chip(
        blocks_kernel,
        (pltpu.VMEM((PLANES, BLOCKS, KQ * 2 * 256), jnp.bfloat16),),
        [],
        "blocks",
        lined,
        over,
        under,
        omega,
    )
    returned = exchange(blocks, SECOND)
    behind = on_chip(
        behind_kernel,
        (pltpu.VMEM((PEERS, 8, LANE), jnp.bfloat16),),
        [pltpu.VMEM((8 * PEERS, LANE), jnp.float32)],
        "behind",
        returned,
        behind_table,
        twist,
    )
    home = exchange(behind, FIRST)
    return pl.pallas_call(
        gate_kernel,
        in_specs=[near] * 3,
        out_shape=jax.ShapeDtypeStruct((seg, channels), jnp.float32),
        scratch_shapes=[pltpu.VMEM((8 * PEERS, LANE), jnp.float32)],
        name="gate",
    )(*[pltpu.with_memory_space_constraint(arg, pltpu.VMEM) for arg in (queries, direct, home)])


def solution(mesh):
    fine = Mesh(mesh.devices.reshape(SPLIT), EVERY)
    placed = (P(EVERY, None), P(), P(), P(EVERY))
    return jax.shard_map(on_device, mesh=fine, in_specs=placed, out_specs=P(EVERY, None), check_vma=False)
```

```python
import numpy as np

import jax
import jax.numpy as jnp
from jax import lax
from jax.experimental import pallas as pl
from jax.experimental.pallas import tpu as pltpu
from jax.sharding import Mesh, PartitionSpec as P

LANE = 128
FIRST = ("zh", "y", "zl")
SECOND = ("core", "x")
EVERY = ("zh", "y", "core", "x", "zl")
SPLIT = (2, 8, 2, 4, 4)
PEERS = 64
BLOCKS = 16
PLANES = 8
HIGH = 4
RUN = 4
SPAN = 2048
LINES = 16
KQ = 2
WAVES = 256
GRANT = pltpu.CompilerParams(vmem_limit_bytes=12 * 2**20)
EDGE = ((0, 0), (1, 0), (0, 1), (1, 1), (2, 0), (3, 0), (2, 1), (3, 1))


def turn_of(phase):
    turn = 2.0 * np.pi * np.asarray(phase, np.float64)
    return np.cos(turn), np.sin(turn)


def halves(table):
    table = np.asarray(table, np.float32)
    upper = table.astype(jnp.bfloat16)
    lower = (table - upper.astype(np.float32)).astype(jnp.bfloat16)
    return np.stack([upper, lower])


def tables():
    line = np.arange(LINES)
    same = np.eye(BLOCKS)
    cos, sin = turn_of(np.outer(line + 0.25, line) / LINES)

    def forward(part):
        small = part.reshape(PLANES, KQ, RUN, HIGH)
        return np.einsum("jkzr,bc->kjbczr", small, same).reshape(256, 256)

    def backward(part):
        small = part.reshape(PLANES, KQ, RUN, HIGH) / SPAN
        return np.einsum("jkzr,bc->rczkjb", small, same).reshape(256, 256)

    first = np.concatenate([forward(cos), forward(sin)], axis=0)
    first_back = np.concatenate([backward(cos), backward(sin)], axis=1)
    cos, sin = turn_of(np.outer(line + 0.25, np.arange(LANE)) / SPAN)
    rows = np.broadcast_to(line.reshape(PLANES, KQ).T[:, :, None], (KQ, PLANES, BLOCKS)).reshape(-1)
    twist = np.concatenate([cos[rows], sin[rows]], axis=1)
    cos, sin = turn_of(np.outer(np.arange(LANE), np.arange(LANE)) / LANE)
    second = np.block([[cos, sin], [-sin, cos]])
    block = (np.arange(BLOCKS)[None, :] * PLANES + np.arange(PLANES)[:, None]).reshape(-1)
    wave = np.arange(WAVES)
    cos, sin = turn_of(np.outer(wave, block) / WAVES)
    over = np.block([[cos, sin], [-sin, cos]])
    cos_before, sin_before = turn_of(np.outer(wave, block - 1) / WAVES)
    real = (cos + sin_before).T / WAVES
    imag = (sin - cos_before).T / WAVES
    under = np.block([[real, -imag], [imag, real]])
    spot = line.reshape(PLANES, KQ, 1) + LINES * np.arange(LANE) + 0.25
    omega = np.stack(turn_of(spot / SPAN), axis=2).reshape(PLANES, 2 * KQ, LANE)
    omega = np.concatenate([omega, np.zeros_like(omega)], axis=1).reshape(8 * PLANES, LANE)
    twist = np.concatenate([twist, np.concatenate([omega, np.zeros_like(omega)], axis=1)], axis=0).astype(np.float32)
    ahead = halves(np.concatenate([first, second], axis=0))
    behind = halves(np.concatenate([first_back, second.T], axis=1))
    return ahead, behind, halves(over), halves(under), twist


def mxu(left, right):
    return jnp.dot(left, right, preferred_element_type=jnp.float32)


def cut(value):
    upper = value.astype(jnp.bfloat16)
    return upper, (value - upper.astype(jnp.float32)).astype(jnp.bfloat16)


def short_filter(ext_ref, taps, seg):
    total = taps[0:1, :] * ext_ref[8 : 8 + seg, :]
    for tap in range(1, taps.shape[0]):
        total = total + taps[tap : tap + 1, :] * ext_ref[8 - tap : 8 - tap + seg, :]
    return total


def pack_kernel(projected_ref, taps_ref, filter_ref, out_ref, tail_ref, ext_ref, rows_ref):
    seg = projected_ref.shape[0]
    tail_ref[...] = projected_ref[seg - 8 :, :]
    ext_ref[0:8, :] = jnp.zeros((8, 2 * LANE), jnp.float32)
    ext_ref[8 : 8 + seg, :] = projected_ref[:, LANE:].astype(jnp.float32)
    taps = taps_ref[:, LANE:]
    filtered = short_filter(ext_ref, taps, seg)
    mixture = (filtered[:, :LANE] * filtered[:, LANE:]).astype(jnp.bfloat16).astype(jnp.float32)
    last = ext_ref[7 + seg : 8 + seg, :]
    carry = taps[1:2, :] * last + taps[2:3, :] * ext_ref[6 + seg : 7 + seg, :]
    ends = [filtered[0:1, :], filtered[1:2, :], carry, taps[2:3, :] * last]
    ends = [ends[row][:, half * LANE : (half + 1) * LANE] for row, half in EDGE]
    upper, lower = cut(jnp.concatenate(ends, axis=0))
    pad = jnp.zeros((LANE - 16, LANE), jnp.float32)
    flipped = jnp.concatenate([upper.astype(jnp.float32), lower.astype(jnp.float32), pad], axis=0).T
    lane = lax.broadcasted_iota(jnp.int32, (PEERS, LANE), 1)
    edges = jnp.where(lane < 16, flipped[:PEERS, :], pltpu.roll(flipped[PEERS:, :], 16, 1))
    for hi in range(HIGH):
        flipped = mixture[hi * LANE : (hi + 1) * LANE, :].T
        where = pl.ds(hi, PEERS, stride=HIGH)
        for ch in range(2):
            rows_ref[ch, where, :] = flipped[ch * PEERS : (ch + 1) * PEERS, :]
        taps_row = filter_ref[hi : hi + 1, :].astype(jnp.float32)
        rows_ref[2, where, :] = jnp.broadcast_to(taps_row, (PEERS, LANE))
        rows_ref[3, where, :] = edges
    for at in range(4):
        out_ref[:, :, at * LANE : (at + 1) * LANE] = rows_ref[at].reshape(PEERS, HIGH, LANE).astype(jnp.bfloat16)


def plan_kernel(projected_ref, earlier_ref, taps_ref, gain_ref, queries_ref, direct_ref, ext_ref):
    seg = projected_ref.shape[0]
    ext_ref[0:8, :] = earlier_ref[...].astype(jnp.float32)
    ext_ref[8 : 8 + seg, :] = projected_ref[...].astype(jnp.float32)
    filtered = short_filter(ext_ref, taps_ref[...], seg)
    mixture = (filtered[:, LANE : 2 * LANE] * filtered[:, 2 * LANE :]).astype(jnp.bfloat16)
    queries_ref[...] = filtered[:, :LANE]
    direct_ref[...] = gain_ref[...] * mixture.astype(jnp.float32)


def back(value, lanes):
    return pltpu.roll(value, LANE - lanes, 1)


def whole_edges(edges):
    return edges + back(edges, 8)


def rows_of(own, before):
    total = own + before
    return (total * back(total, 2)).astype(jnp.bfloat16).astype(jnp.float32)


def ahead_kernel(data_ref, table_ref, twist_ref, out_ref, rows_ref, edge_ref):
    for at in range(4):
        block = data_ref[:, :, at * LANE : (at + 1) * LANE].astype(jnp.float32)
        rows_ref[at] = block.reshape(256, LANE)
    where = pl.ds(0, PEERS, stride=HIGH)
    edges = rows_ref[3, where, :]
    edge_ref[...] = edges
    own = whole_edges(edges)
    mixture = rows_of(own, pltpu.roll(back(own, 4), 1, 0))
    inside = (lax.broadcasted_iota(jnp.int32, (PEERS, LANE), 0) & (RUN - 1)) != 0
    lane = lax.broadcasted_iota(jnp.int32, (PEERS, LANE), 1)
    mixture = jnp.where(inside, mixture, 0.0)
    for ch in range(2):
        fresh = back(mixture, 16 * ch) if ch else mixture
        rows_ref[ch, where, :] = jnp.where(lane < 2, fresh, rows_ref[ch, where, :])
    opening = edge_ref[pl.ds(0, BLOCKS, stride=RUN), :]
    closing = edge_ref[pl.ds(RUN - 1, BLOCKS, stride=RUN), :]
    outside = jnp.where((lane[:BLOCKS, :] & 4) == 0, opening, closing).astype(jnp.bfloat16)
    for plane in range(PLANES):
        out_ref[plane, :, KQ * 3 * 256 :] = outside
    data = jnp.concatenate([rows_ref[0], rows_ref[1], rows_ref[2]], axis=1).astype(jnp.bfloat16)
    waves = mxu(table_ref[0, :512, :], data) + mxu(table_ref[1, :512, :], data)
    cos = twist_ref[:256, :LANE]
    sin = twist_ref[:256, LANE:]
    for number in range(3):
        real = waves[:256, number * LANE : (number + 1) * LANE]
        imag = waves[256:, number * LANE : (number + 1) * LANE]
        upper, lower = cut(jnp.concatenate([real * cos - imag * sin, real * sin + imag * cos], axis=1))
        second = table_ref[0, 512:, :]
        freq = mxu(upper, second) + (mxu(lower, second) + mxu(upper, table_ref[1, 512:, :]))
        for kq in range(KQ):
            at = (kq * 3 + number) * 256
            value = freq[kq * 128 : (kq + 1) * 128, :].reshape(PLANES, BLOCKS, 256)
            out_ref[:, :, at : at + 256] = value.astype(jnp.bfloat16)


def blocks_kernel(data_ref, over_ref, under_ref, twist_ref, out_ref):
    omega = twist_ref[pl.ds(256 + 8 * lax.axis_index(SECOND), 8), :LANE]
    owns = [whole_edges(data_ref[plane, :, KQ * 3 * 256 :].astype(jnp.float32)) for plane in range(PLANES)]
    row = lax.broadcasted_iota(jnp.int32, (BLOCKS, LANE), 0)
    wrapped = jnp.where(row == 0, 0.0, pltpu.roll(back(owns[PLANES - 1], 4), 1, 0))
    befores = [wrapped] + [back(own, 4) for own in owns[:-1]]
    opening = jnp.concatenate([rows_of(own, before) for own, before in zip(owns, befores)], axis=0)

    def piece(kq, number, part):
        at = ((kq * 3 + number) * 2 + part) * LANE
        value = data_ref[:, :, at : at + LANE].astype(jnp.float32).reshape(128, LANE)
        if number == 2:
            return value
        second = opening[:, 16 * number + 1 : 16 * number + 2] * omega[2 * kq + part : 2 * kq + part + 1, :]
        if part == 0:
            second = second + opening[:, 16 * number : 16 * number + 1]
        return value + second

    columns = []
    for kq in range(KQ):
        for number in range(3):
            columns.append(jnp.concatenate([piece(kq, number, 0), piece(kq, number, 1)], axis=0))
    upper, lower = cut(jnp.concatenate(columns, axis=1))
    waves = mxu(over_ref[0], upper) + (mxu(over_ref[0], lower) + mxu(over_ref[1], upper))
    products = []
    for kq in range(KQ):
        at = (kq * 3 + 2) * LANE
        tap_real = waves[:WAVES, at : at + LANE]
        tap_imag = waves[WAVES:, at : at + LANE]
        for ch in range(2):
            at = (kq * 3 + ch) * LANE
            real = waves[:WAVES, at : at + LANE]
            imag = waves[WAVES:, at : at + LANE]
            both = [real * tap_real - imag * tap_imag, real * tap_imag + imag * tap_real]
            products.append(jnp.concatenate(both, axis=0))
    upper, lower = cut(jnp.concatenate(products, axis=1))
    sums = mxu(under_ref[0], upper) + (mxu(under_ref[0], lower) + mxu(under_ref[1], upper))
    for kq in range(KQ):
        for ch in range(2):
            for part in range(2):
                at = (kq * 2 + ch) * LANE
                value = sums[part * 128 : (part + 1) * 128, at : at + LANE].reshape(PLANES, BLOCKS, LANE)
                to = (at // LANE * 2 + part) * LANE
                out_ref[:, :, to : to + LANE] = value.astype(jnp.bfloat16)


def behind_kernel(data_ref, table_ref, twist_ref, out_ref, rows_ref):
    columns = []
    for ch in range(2):
        parts = [[], []]
        for kq in range(KQ):
            at = (kq * 2 + ch) * 256
            block = data_ref[:, :, at : at + 256].astype(jnp.float32).reshape(128, 256).astype(jnp.bfloat16)
            lines = mxu(block, table_ref[0, :, 512:]) + mxu(block, table_ref[1, :, 512:])
            cos = twist_ref[kq * 128 : (kq + 1) * 128, :LANE]
            sin = twist_ref[kq * 128 : (kq + 1) * 128, LANE:]
            real = lines[:, :LANE]
            imag = lines[:, LANE:]
            parts[0].append(real * cos + imag * sin)
            parts[1].append(imag * cos - real * sin)
        columns.append(jnp.concatenate(parts[0] + parts[1], axis=0))
    upper, lower = cut(jnp.concatenate(columns, axis=1))
    first = table_ref[0, :, :512]
    value = mxu(first, upper) + (mxu(first, lower) + mxu(table_ref[1, :, :512], upper))
    for hi in range(HIGH):
        for ch in range(2):
            where = pl.ds(ch * HIGH + hi, PEERS, stride=8)
            rows_ref[where, :] = value[hi * PEERS : (hi + 1) * PEERS, ch * LANE : (ch + 1) * LANE]
    out_ref[...] = rows_ref[...].reshape(PEERS, 8, LANE).astype(jnp.bfloat16)


def gate_kernel(queries_ref, direct_ref, data_ref, out_ref, rows_ref):
    rows_ref[...] = data_ref[...].astype(jnp.float32).reshape(8 * PEERS, LANE)
    for hi in range(HIGH):
        rows = [rows_ref[pl.ds(ch * HIGH + hi, PEERS, stride=8), :] for ch in range(2)]
        convolved = jnp.concatenate(rows, axis=0).T
        span = slice(hi * LANE, (hi + 1) * LANE)
        out_ref[span, :] = queries_ref[span, :] * (convolved + direct_ref[span, :])


def exchange(value, axis):
    return lax.all_to_all(value, axis, split_axis=0, concat_axis=0, tiled=True)


def on_chip(kernel, outs, scratch, name, *args):
    near = pl.BlockSpec(memory_space=pltpu.VMEM)
    return pl.pallas_call(
        kernel,
        in_specs=[near] * len(args),
        out_specs=tuple(near for _ in outs) if len(outs) > 1 else near,
        out_shape=outs if len(outs) > 1 else outs[0],
        scratch_shapes=scratch,
        name=name,
        compiler_params=GRANT,
    )(*[pltpu.with_memory_space_constraint(arg, pltpu.VMEM) for arg in args])


def on_device(projected, short_taps, skip_gain, long_filter):
    seg, wide = projected.shape
    channels = skip_gain.shape[0]
    count = lax.axis_size(EVERY)
    near = pl.BlockSpec(memory_space=pltpu.VMEM)
    ahead_table, behind_table, over, under, twist = tables()
    plane = pltpu.VMEM((seg, channels), jnp.float32)
    stack = pltpu.VMEM((4, 256, LANE), jnp.float32)
    packed, tail = pl.pallas_call(
        pack_kernel,
        out_specs=(near, near),
        out_shape=(jax.ShapeDtypeStruct((PEERS, HIGH, 4 * LANE), jnp.bfloat16), pltpu.VMEM((8, wide), jnp.bfloat16)),
        scratch_shapes=[pltpu.VMEM((seg + 8, 2 * LANE), jnp.float32), stack],
        name="pack",
    )(projected, short_taps, long_filter.reshape(HIGH, LANE))
    earlier = lax.ppermute(tail, EVERY, [(s, s + 1) for s in range(count - 1)])
    queries, direct = pl.pallas_call(
        plan_kernel,
        out_specs=(near, near),
        out_shape=(plane, plane),
        scratch_shapes=[pltpu.VMEM((seg + 8, wide), jnp.float32)],
        name="plan",
    )(
        projected,
        pltpu.with_memory_space_constraint(earlier, pltpu.VMEM),
        short_taps,
        skip_gain.reshape(1, channels),
    )
    arrived = exchange(packed, FIRST)
    arrived, queries, direct = lax.optimization_barrier((arrived, queries, direct))
    ahead = on_chip(
        ahead_kernel,
        (pltpu.VMEM((PLANES, BLOCKS, KQ * 3 * 256 + LANE), jnp.bfloat16),),
        [stack, pltpu.VMEM((PEERS, LANE), jnp.float32)],
        "ahead",
        arrived,
        ahead_table,
        twist,
    )
    lined = exchange(ahead, SECOND)
    blocks = on_chip(
        blocks_kernel,
        (pltpu.VMEM((PLANES, BLOCKS, KQ * 2 * 256), jnp.bfloat16),),
        [],
        "blocks",
        lined,
        over,
        under,
        twist,
    )
    returned = exchange(blocks, SECOND)
    behind = on_chip(
        behind_kernel,
        (pltpu.VMEM((PEERS, 8, LANE), jnp.bfloat16),),
        [pltpu.VMEM((8 * PEERS, LANE), jnp.float32)],
        "behind",
        returned,
        behind_table,
        twist,
    )
    home = exchange(behind, FIRST)
    return pl.pallas_call(
        gate_kernel,
        in_specs=[near] * 3,
        out_shape=jax.ShapeDtypeStruct((seg, channels), jnp.float32),
        scratch_shapes=[pltpu.VMEM((8 * PEERS, LANE), jnp.float32)],
        name="gate",
        compiler_params=GRANT,
    )(*[pltpu.with_memory_space_constraint(arg, pltpu.VMEM) for arg in (queries, direct, home)])


def solution(mesh):
    fine = Mesh(mesh.devices.reshape(SPLIT), EVERY)
    placed = (P(EVERY, None), P(), P(), P(EVERY))
    return jax.shard_map(on_device, mesh=fine, in_specs=placed, out_specs=P(EVERY, None), check_vma=False)
```

```python
import numpy as np

import jax
import jax.numpy as jnp
from jax import lax
from jax.experimental import pallas as pl
from jax.experimental.pallas import tpu as pltpu
from jax.sharding import Mesh, PartitionSpec as P

LANE = 128
FIRST = ("zh", "y", "zl")
SECOND = ("core", "x")
EVERY = ("zh", "y", "core", "x", "zl")
SPLIT = (2, 8, 2, 4, 4)
PEERS = 64
BLOCKS = 16
PLANES = 8
HIGH = 4
RUN = 4
SPAN = 2048
LINES = 16
KQ = 2
WAVES = 256
GRANT = pltpu.CompilerParams(vmem_limit_bytes=12 * 2**20)
EDGE = ((0, 0), (1, 0), (0, 1), (1, 1), (2, 0), (3, 0), (2, 1), (3, 1))


def turn_of(phase):
    turn = 2.0 * np.pi * np.asarray(phase, np.float64)
    return np.cos(turn), np.sin(turn)


def halves(table):
    table = np.asarray(table, np.float32)
    upper = table.astype(jnp.bfloat16)
    lower = (table - upper.astype(np.float32)).astype(jnp.bfloat16)
    return np.stack([upper, lower])


def tables():
    line = np.arange(LINES)
    same = np.eye(BLOCKS)
    cos, sin = turn_of(np.outer(line + 0.25, line) / LINES)

    def forward(part):
        small = part.reshape(PLANES, KQ, RUN, HIGH)
        return np.einsum("jkzr,bc->kjbczr", small, same).reshape(256, 256)

    def backward(part):
        small = part.reshape(PLANES, KQ, RUN, HIGH) / SPAN
        return np.einsum("jkzr,bc->rczkjb", small, same).reshape(256, 256)

    first = np.concatenate([forward(cos), forward(sin)], axis=0)
    first_back = np.concatenate([backward(cos), backward(sin)], axis=1)
    cos, sin = turn_of(np.outer(line + 0.25, np.arange(LANE)) / SPAN)
    rows = np.broadcast_to(line.reshape(PLANES, KQ).T[:, :, None], (KQ, PLANES, BLOCKS)).reshape(-1)
    twist = np.concatenate([cos[rows], sin[rows]], axis=1)
    cos, sin = turn_of(np.outer(np.arange(LANE), np.arange(LANE)) / LANE)
    second = np.block([[cos, sin], [-sin, cos]])
    block = (np.arange(BLOCKS)[None, :] * PLANES + np.arange(PLANES)[:, None]).reshape(-1)
    wave = np.arange(WAVES)
    cos, sin = turn_of(np.outer(wave, block) / WAVES)
    over = np.block([[cos, sin], [-sin, cos]])
    cos_before, sin_before = turn_of(np.outer(wave, block - 1) / WAVES)
    real = (cos + sin_before).T / WAVES
    imag = (sin - cos_before).T / WAVES
    under = np.block([[real, -imag], [imag, real]])
    spot = line.reshape(PLANES, KQ, 1) + LINES * np.arange(LANE) + 0.25
    omega = np.stack(turn_of(spot / SPAN), axis=2).reshape(PLANES, 2 * KQ, LANE)
    omega = np.concatenate([omega, np.zeros_like(omega)], axis=1).reshape(8 * PLANES, LANE)
    twist = np.concatenate([twist, np.concatenate([omega, np.zeros_like(omega)], axis=1)], axis=0).astype(np.float32)
    ahead = halves(np.concatenate([first, second], axis=0))
    behind = halves(np.concatenate([first_back, second.T], axis=1))
    return ahead, behind, halves(over), halves(under), twist


def mxu(left, right):
    return jnp.dot(left, right, preferred_element_type=jnp.float32)


def cut(value):
    upper = value.astype(jnp.bfloat16)
    return upper, (value - upper.astype(jnp.float32)).astype(jnp.bfloat16)


def short_filter(ext_ref, taps, seg):
    total = taps[0:1, :] * ext_ref[8 : 8 + seg, :]
    for tap in range(1, taps.shape[0]):
        total = total + taps[tap : tap + 1, :] * ext_ref[8 - tap : 8 - tap + seg, :]
    return total


def pack_kernel(projected_ref, taps_ref, filter_ref, out_ref, tail_ref, ext_ref, rows_ref):
    seg = projected_ref.shape[0]
    tail_ref[...] = projected_ref[seg - 8 :, :]
    ext_ref[0:8, :] = jnp.zeros((8, 2 * LANE), jnp.float32)
    ext_ref[8 : 8 + seg, :] = projected_ref[:, LANE:].astype(jnp.float32)
    taps = taps_ref[:, LANE:]
    filtered = short_filter(ext_ref, taps, seg)
    mixture = (filtered[:, :LANE] * filtered[:, LANE:]).astype(jnp.bfloat16).astype(jnp.float32)
    last = ext_ref[7 + seg : 8 + seg, :]
    carry = taps[1:2, :] * last + taps[2:3, :] * ext_ref[6 + seg : 7 + seg, :]
    ends = [filtered[0:1, :], filtered[1:2, :], carry, taps[2:3, :] * last]
    ends = [ends[row][:, half * LANE : (half + 1) * LANE] for row, half in EDGE]
    upper, lower = cut(jnp.concatenate(ends, axis=0))
    pad = jnp.zeros((LANE - 16, LANE), jnp.float32)
    flipped = jnp.concatenate([upper.astype(jnp.float32), lower.astype(jnp.float32), pad], axis=0).T
    lane = lax.broadcasted_iota(jnp.int32, (PEERS, LANE), 1)
    edges = jnp.where(lane < 16, flipped[:PEERS, :], pltpu.roll(flipped[PEERS:, :], 16, 1))
    for hi in range(HIGH):
        flipped = mixture[hi * LANE : (hi + 1) * LANE, :].T
        where = pl.ds(hi, PEERS, stride=HIGH)
        for ch in range(2):
            rows_ref[ch, where, :] = flipped[ch * PEERS : (ch + 1) * PEERS, :]
        taps_row = filter_ref[hi : hi + 1, :].astype(jnp.float32)
        rows_ref[2, where, :] = jnp.broadcast_to(taps_row, (PEERS, LANE))
        rows_ref[3, where, :] = edges
    for at in range(4):
        out_ref[:, :, at * LANE : (at + 1) * LANE] = rows_ref[at].reshape(PEERS, HIGH, LANE).astype(jnp.bfloat16)


def plan_kernel(projected_ref, earlier_ref, taps_ref, gain_ref, queries_ref, direct_ref, ext_ref):
    seg = projected_ref.shape[0]
    ext_ref[0:8, :] = earlier_ref[...].astype(jnp.float32)
    ext_ref[8 : 8 + seg, :] = projected_ref[...].astype(jnp.float32)
    filtered = short_filter(ext_ref, taps_ref[...], seg)
    mixture = (filtered[:, LANE : 2 * LANE] * filtered[:, 2 * LANE :]).astype(jnp.bfloat16)
    queries_ref[...] = filtered[:, :LANE]
    direct_ref[...] = gain_ref[...] * mixture.astype(jnp.float32)


def back(value, lanes):
    return pltpu.roll(value, LANE - lanes, 1)


def whole_edges(edges):
    return edges + back(edges, 8)


def rows_of(own, before):
    total = own + before
    return (total * back(total, 2)).astype(jnp.bfloat16).astype(jnp.float32)


def ahead_kernel(data_ref, table_ref, twist_ref, out_ref, rows_ref, edge_ref):
    for at in range(4):
        block = data_ref[:, :, at * LANE : (at + 1) * LANE].astype(jnp.float32)
        rows_ref[at] = block.reshape(256, LANE)
    where = pl.ds(0, PEERS, stride=HIGH)
    edges = rows_ref[3, where, :]
    edge_ref[...] = edges
    own = whole_edges(edges)
    mixture = rows_of(own, pltpu.roll(back(own, 4), 1, 0))
    inside = (lax.broadcasted_iota(jnp.int32, (PEERS, LANE), 0) & (RUN - 1)) != 0
    lane = lax.broadcasted_iota(jnp.int32, (PEERS, LANE), 1)
    mixture = jnp.where(inside, mixture, 0.0)
    for ch in range(2):
        fresh = back(mixture, 16 * ch) if ch else mixture
        rows_ref[ch, where, :] = jnp.where(lane < 2, fresh, rows_ref[ch, where, :])
    opening = edge_ref[pl.ds(0, BLOCKS, stride=RUN), :]
    closing = edge_ref[pl.ds(RUN - 1, BLOCKS, stride=RUN), :]
    outside = jnp.where((lane[:BLOCKS, :] & 4) == 0, opening, closing).astype(jnp.bfloat16)
    for plane in range(PLANES):
        out_ref[plane, :, KQ * 3 * 256 :] = outside
    data = jnp.concatenate([rows_ref[0], rows_ref[1], rows_ref[2]], axis=1).astype(jnp.bfloat16)
    waves = mxu(table_ref[0, :512, :], data) + mxu(table_ref[1, :512, :], data)
    cos = twist_ref[:256, :LANE]
    sin = twist_ref[:256, LANE:]
    for number in range(3):
        real = waves[:256, number * LANE : (number + 1) * LANE]
        imag = waves[256:, number * LANE : (number + 1) * LANE]
        upper, lower = cut(jnp.concatenate([real * cos - imag * sin, real * sin + imag * cos], axis=1))
        second = table_ref[0, 512:, :]
        freq = mxu(upper, second) + (mxu(lower, second) + mxu(upper, table_ref[1, 512:, :]))
        for kq in range(KQ):
            at = (kq * 3 + number) * 256
            value = freq[kq * 128 : (kq + 1) * 128, :].reshape(PLANES, BLOCKS, 256)
            out_ref[:, :, at : at + 256] = value.astype(jnp.bfloat16)


def blocks_kernel(data_ref, over_ref, under_ref, twist_ref, out_ref):
    omega = twist_ref[pl.ds(256 + 8 * lax.axis_index(SECOND), 8), :LANE]
    owns = [whole_edges(data_ref[plane, :, KQ * 3 * 256 :].astype(jnp.float32)) for plane in range(PLANES)]
    row = lax.broadcasted_iota(jnp.int32, (BLOCKS, LANE), 0)
    wrapped = jnp.where(row == 0, 0.0, pltpu.roll(back(owns[PLANES - 1], 4), 1, 0))
    befores = [wrapped] + [back(own, 4) for own in owns[:-1]]
    opening = jnp.concatenate([rows_of(own, before) for own, before in zip(owns, befores)], axis=0)

    def piece(kq, number, part):
        at = ((kq * 3 + number) * 2 + part) * LANE
        value = data_ref[:, :, at : at + LANE].astype(jnp.float32).reshape(128, LANE)
        if number == 2:
            return value
        second = opening[:, 16 * number + 1 : 16 * number + 2] * omega[2 * kq + part : 2 * kq + part + 1, :]
        if part == 0:
            second = second + opening[:, 16 * number : 16 * number + 1]
        return value + second

    columns = []
    for kq in range(KQ):
        for number in range(3):
            columns.append(jnp.concatenate([piece(kq, number, 0), piece(kq, number, 1)], axis=0))
    upper, lower = cut(jnp.concatenate(columns, axis=1))
    waves = mxu(over_ref[0], upper) + (mxu(over_ref[0], lower) + mxu(over_ref[1], upper))
    products = []
    for kq in range(KQ):
        at = (kq * 3 + 2) * LANE
        tap_real = waves[:WAVES, at : at + LANE]
        tap_imag = waves[WAVES:, at : at + LANE]
        for ch in range(2):
            at = (kq * 3 + ch) * LANE
            real = waves[:WAVES, at : at + LANE]
            imag = waves[WAVES:, at : at + LANE]
            both = [real * tap_real - imag * tap_imag, real * tap_imag + imag * tap_real]
            products.append(jnp.concatenate(both, axis=0))
    upper, lower = cut(jnp.concatenate(products, axis=1))
    sums = mxu(under_ref[0], upper) + (mxu(under_ref[0], lower) + mxu(under_ref[1], upper))
    for kq in range(KQ):
        for ch in range(2):
            for part in range(2):
                at = (kq * 2 + ch) * LANE
                value = sums[part * 128 : (part + 1) * 128, at : at + LANE].reshape(PLANES, BLOCKS, LANE)
                to = (at // LANE * 2 + part) * LANE
                out_ref[:, :, to : to + LANE] = value.astype(jnp.bfloat16)


def behind_kernel(data_ref, table_ref, twist_ref, out_ref, rows_ref):
    columns = []
    for ch in range(2):
        parts = [[], []]
        for kq in range(KQ):
            at = (kq * 2 + ch) * 256
            block = data_ref[:, :, at : at + 256].astype(jnp.float32).reshape(128, 256).astype(jnp.bfloat16)
            lines = mxu(block, table_ref[0, :, 512:]) + mxu(block, table_ref[1, :, 512:])
            cos = twist_ref[kq * 128 : (kq + 1) * 128, :LANE]
            sin = twist_ref[kq * 128 : (kq + 1) * 128, LANE:]
            real = lines[:, :LANE]
            imag = lines[:, LANE:]
            parts[0].append(real * cos + imag * sin)
            parts[1].append(imag * cos - real * sin)
        columns.append(jnp.concatenate(parts[0] + parts[1], axis=0))
    upper, lower = cut(jnp.concatenate(columns, axis=1))
    first = table_ref[0, :, :512]
    value = mxu(first, upper) + (mxu(first, lower) + mxu(table_ref[1, :, :512], upper))
    for hi in range(HIGH):
        for ch in range(2):
            where = pl.ds(ch * HIGH + hi, PEERS, stride=8)
            rows_ref[where, :] = value[hi * PEERS : (hi + 1) * PEERS, ch * LANE : (ch + 1) * LANE]
    out_ref[...] = rows_ref[...].reshape(PEERS, 8, LANE).astype(jnp.bfloat16)


def gate_kernel(queries_ref, direct_ref, data_ref, out_ref, rows_ref):
    rows_ref[...] = data_ref[...].astype(jnp.float32).reshape(8 * PEERS, LANE)
    for hi in range(HIGH):
        rows = [rows_ref[pl.ds(ch * HIGH + hi, PEERS, stride=8), :] for ch in range(2)]
        convolved = jnp.concatenate(rows, axis=0).T
        span = slice(hi * LANE, (hi + 1) * LANE)
        out_ref[span, :] = queries_ref[span, :] * (convolved + direct_ref[span, :])


def exchange(value, axis):
    return lax.all_to_all(value, axis, split_axis=0, concat_axis=0, tiled=True)


def far(value):
    return pltpu.with_memory_space_constraint(value, pltpu.HBM)


def on_chip(kernel, outs, scratch, name, *args):
    near = pl.BlockSpec(memory_space=pltpu.VMEM)
    return pl.pallas_call(
        kernel,
        in_specs=[near] * len(args),
        out_specs=tuple(near for _ in outs) if len(outs) > 1 else near,
        out_shape=outs if len(outs) > 1 else outs[0],
        scratch_shapes=scratch,
        name=name,
        compiler_params=GRANT,
    )(*[pltpu.with_memory_space_constraint(arg, pltpu.VMEM) for arg in args])


def on_device(projected, short_taps, skip_gain, long_filter):
    seg, wide = projected.shape
    channels = skip_gain.shape[0]
    count = lax.axis_size(EVERY)
    near = pl.BlockSpec(memory_space=pltpu.VMEM)
    ahead_table, behind_table, over, under, twist = tables()
    plane = pltpu.VMEM((seg, channels), jnp.float32)
    stack = pltpu.VMEM((4, 256, LANE), jnp.float32)
    packed, tail = pl.pallas_call(
        pack_kernel,
        out_specs=(near, near),
        out_shape=(pltpu.VMEM((PEERS, HIGH, 4 * LANE), jnp.bfloat16), pltpu.VMEM((8, wide), jnp.bfloat16)),
        scratch_shapes=[pltpu.VMEM((seg + 8, 2 * LANE), jnp.float32), stack],
        name="pack",
        cost_estimate=pl.CostEstimate(flops=200000000, bytes_accessed=800000, transcendentals=0),
        compiler_params=GRANT,
    )(far(projected), far(short_taps), far(long_filter.reshape(HIGH, LANE)))
    earlier = lax.ppermute(tail, EVERY, [(s, s + 1) for s in range(count - 1)])
    queries, direct = pl.pallas_call(
        plan_kernel,
        out_specs=(near, near),
        out_shape=(plane, plane),
        scratch_shapes=[pltpu.VMEM((seg + 8, wide), jnp.float32)],
        name="plan",
        compiler_params=GRANT,
    )(
        far(projected),
        pltpu.with_memory_space_constraint(earlier, pltpu.VMEM),
        far(short_taps),
        far(skip_gain.reshape(1, channels)),
    )
    arrived = exchange(packed, FIRST)
    ahead = on_chip(
        ahead_kernel,
        (pltpu.VMEM((PLANES, BLOCKS, KQ * 3 * 256 + LANE), jnp.bfloat16),),
        [stack, pltpu.VMEM((PEERS, LANE), jnp.float32)],
        "ahead",
        arrived,
        ahead_table,
        twist,
    )
    lined = exchange(ahead, SECOND)
    blocks = on_chip(
        blocks_kernel,
        (pltpu.VMEM((PLANES, BLOCKS, KQ * 2 * 256), jnp.bfloat16),),
        [],
        "blocks",
        lined,
        over,
        under,
        twist,
    )
    returned = exchange(blocks, SECOND)
    behind = on_chip(
        behind_kernel,
        (pltpu.VMEM((PEERS, 8, LANE), jnp.bfloat16),),
        [pltpu.VMEM((8 * PEERS, LANE), jnp.float32)],
        "behind",
        returned,
        behind_table,
        twist,
    )
    home = exchange(behind, FIRST)
    return pl.pallas_call(
        gate_kernel,
        in_specs=[near] * 3,
        out_shape=jax.ShapeDtypeStruct((seg, channels), jnp.float32),
        scratch_shapes=[pltpu.VMEM((8 * PEERS, LANE), jnp.float32)],
        name="gate",
        compiler_params=GRANT,
    )(*[pltpu.with_memory_space_constraint(arg, pltpu.VMEM) for arg in (queries, direct, home)])


def solution(mesh):
    fine = Mesh(mesh.devices.reshape(SPLIT), EVERY)
    placed = (P(EVERY, None), P(), P(), P(EVERY))
    return jax.shard_map(on_device, mesh=fine, in_specs=placed, out_specs=P(EVERY, None), check_vma=False)
```

```python
import numpy as np

import jax
import jax.numpy as jnp
from jax import lax
from jax.experimental import pallas as pl
from jax.experimental.pallas import tpu as pltpu
from jax.sharding import Mesh, PartitionSpec as P

LANE = 128
FIRST = ("zh", "y", "zl")
SECOND = ("core", "x")
EVERY = ("zh", "y", "core", "x", "zl")
SPLIT = (2, 8, 2, 4, 4)
PEERS = 64
BLOCKS = 16
PLANES = 8
HIGH = 4
RUN = 4
SPAN = 2048
LINES = 16
KQ = 2
WAVES = 256
GRANT = pltpu.CompilerParams(vmem_limit_bytes=12 * 2**20)
EDGE = ((0, 0), (1, 0), (0, 1), (1, 1), (2, 0), (3, 0), (2, 1), (3, 1))


def turn_of(phase):
    turn = 2.0 * np.pi * np.asarray(phase, np.float64)
    return np.cos(turn), np.sin(turn)


def halves(table):
    table = np.asarray(table, np.float32)
    upper = table.astype(jnp.bfloat16)
    lower = (table - upper.astype(np.float32)).astype(jnp.bfloat16)
    return np.stack([upper, lower])


def tables():
    line = np.arange(LINES)
    same = np.eye(BLOCKS)
    cos, sin = turn_of(np.outer(line + 0.25, line) / LINES)

    def forward(part):
        small = part.reshape(PLANES, KQ, RUN, HIGH)
        return np.einsum("jkzr,bc->kjbczr", small, same).reshape(256, 256)

    def backward(part):
        small = part.reshape(PLANES, KQ, RUN, HIGH) / SPAN
        return np.einsum("jkzr,bc->rczkjb", small, same).reshape(256, 256)

    first = np.concatenate([forward(cos), forward(sin)], axis=0)
    first_back = np.concatenate([backward(cos), backward(sin)], axis=1)
    cos, sin = turn_of(np.outer(line + 0.25, np.arange(LANE)) / SPAN)
    rows = np.broadcast_to(line.reshape(PLANES, KQ).T[:, :, None], (KQ, PLANES, BLOCKS)).reshape(-1)
    twist = np.concatenate([cos[rows], sin[rows]], axis=1)
    cos, sin = turn_of(np.outer(np.arange(LANE), np.arange(LANE)) / LANE)
    second = np.block([[cos, sin], [-sin, cos]])
    block = (np.arange(BLOCKS)[None, :] * PLANES + np.arange(PLANES)[:, None]).reshape(-1)
    wave = np.arange(WAVES)
    cos, sin = turn_of(np.outer(wave, block) / WAVES)
    over = np.block([[cos, sin], [-sin, cos]])
    cos_before, sin_before = turn_of(np.outer(wave, block - 1) / WAVES)
    real = (cos + sin_before).T / WAVES
    imag = (sin - cos_before).T / WAVES
    under = np.block([[real, -imag], [imag, real]])
    spot = line.reshape(PLANES, KQ, 1) + LINES * np.arange(LANE) + 0.25
    omega = np.stack(turn_of(spot / SPAN), axis=2).reshape(PLANES, 2 * KQ, LANE)
    omega = np.concatenate([omega, np.zeros_like(omega)], axis=1).reshape(8 * PLANES, LANE)
    twist = np.concatenate([twist, np.concatenate([omega, np.zeros_like(omega)], axis=1)], axis=0).astype(np.float32)
    ahead = halves(np.concatenate([first, second], axis=0))
    behind = halves(np.concatenate([first_back, second.T], axis=1))
    return ahead, behind, halves(over), halves(under), twist


def mxu(left, right):
    return jnp.dot(left, right, preferred_element_type=jnp.float32)


def cut(value):
    upper = value.astype(jnp.bfloat16)
    return upper, (value - upper.astype(jnp.float32)).astype(jnp.bfloat16)


def short_filter(ext_ref, taps, seg):
    total = taps[0:1, :] * ext_ref[8 : 8 + seg, :]
    for tap in range(1, taps.shape[0]):
        total = total + taps[tap : tap + 1, :] * ext_ref[8 - tap : 8 - tap + seg, :]
    return total


def pack_kernel(projected_ref, taps_ref, filter_ref, out_ref, tail_ref, ext_ref, rows_ref):
    seg = projected_ref.shape[0]
    tail_ref[...] = projected_ref[seg - 8 :, :]
    ext_ref[0:8, :] = jnp.zeros((8, 2 * LANE), jnp.float32)
    ext_ref[8 : 8 + seg, :] = projected_ref[:, LANE:].astype(jnp.float32)
    taps = taps_ref[:, LANE:]
    filtered = short_filter(ext_ref, taps, seg)
    mixture = (filtered[:, :LANE] * filtered[:, LANE:]).astype(jnp.bfloat16).astype(jnp.float32)
    last = ext_ref[7 + seg : 8 + seg, :]
    carry = taps[1:2, :] * last + taps[2:3, :] * ext_ref[6 + seg : 7 + seg, :]
    ends = [filtered[0:1, :], filtered[1:2, :], carry, taps[2:3, :] * last]
    ends = [ends[row][:, half * LANE : (half + 1) * LANE] for row, half in EDGE]
    upper, lower = cut(jnp.concatenate(ends, axis=0))
    pad = jnp.zeros((LANE - 16, LANE), jnp.float32)
    flipped = jnp.concatenate([upper.astype(jnp.float32), lower.astype(jnp.float32), pad], axis=0).T
    lane = lax.broadcasted_iota(jnp.int32, (PEERS, LANE), 1)
    edges = jnp.where(lane < 16, flipped[:PEERS, :], pltpu.roll(flipped[PEERS:, :], 16, 1))
    for hi in range(HIGH):
        flipped = mixture[hi * LANE : (hi + 1) * LANE, :].T
        where = pl.ds(hi, PEERS, stride=HIGH)
        for ch in range(2):
            rows_ref[ch, where, :] = flipped[ch * PEERS : (ch + 1) * PEERS, :]
        taps_row = filter_ref[hi : hi + 1, :].astype(jnp.float32)
        rows_ref[2, where, :] = jnp.broadcast_to(taps_row, (PEERS, LANE))
        rows_ref[3, where, :] = edges
    for at in range(4):
        out_ref[:, :, at * LANE : (at + 1) * LANE] = rows_ref[at].reshape(PEERS, HIGH, LANE).astype(jnp.bfloat16)


def plan_kernel(projected_ref, taps_ref, gain_ref, queries_ref, direct_ref, head_ref, ext_ref):
    seg = projected_ref.shape[0]
    ext_ref[0:8, :] = jnp.zeros((8, 3 * LANE), jnp.float32)
    ext_ref[8 : 8 + seg, :] = projected_ref[...].astype(jnp.float32)
    head_ref[0:8, :] = ext_ref[8:16, :]
    head_ref[8:11, :] = taps_ref[...]
    head_ref[16:17, 0:LANE] = gain_ref[...]
    filtered = short_filter(ext_ref, taps_ref[...], seg)
    queries_ref[...] = filtered[:, :LANE]
    direct_ref[...] = gain_ref[...] * mix_of(filtered)


def mix_of(filtered):
    mixture = (filtered[:, LANE : 2 * LANE] * filtered[:, 2 * LANE :]).astype(jnp.bfloat16)
    return mixture.astype(jnp.float32)


def back(value, lanes):
    return pltpu.roll(value, LANE - lanes, 1)


def whole_edges(edges):
    return edges + back(edges, 8)


def rows_of(own, before):
    total = own + before
    return (total * back(total, 2)).astype(jnp.bfloat16).astype(jnp.float32)


def ahead_kernel(data_ref, table_ref, twist_ref, out_ref, rows_ref, edge_ref):
    for at in range(4):
        block = data_ref[:, :, at * LANE : (at + 1) * LANE].astype(jnp.float32)
        rows_ref[at] = block.reshape(256, LANE)
    where = pl.ds(0, PEERS, stride=HIGH)
    edges = rows_ref[3, where, :]
    edge_ref[...] = edges
    own = whole_edges(edges)
    mixture = rows_of(own, pltpu.roll(back(own, 4), 1, 0))
    inside = (lax.broadcasted_iota(jnp.int32, (PEERS, LANE), 0) & (RUN - 1)) != 0
    lane = lax.broadcasted_iota(jnp.int32, (PEERS, LANE), 1)
    mixture = jnp.where(inside, mixture, 0.0)
    for ch in range(2):
        fresh = back(mixture, 16 * ch) if ch else mixture
        rows_ref[ch, where, :] = jnp.where(lane < 2, fresh, rows_ref[ch, where, :])
    opening = edge_ref[pl.ds(0, BLOCKS, stride=RUN), :]
    closing = edge_ref[pl.ds(RUN - 1, BLOCKS, stride=RUN), :]
    outside = jnp.where((lane[:BLOCKS, :] & 4) == 0, opening, closing).astype(jnp.bfloat16)
    for plane in range(PLANES):
        out_ref[plane, :, KQ * 3 * 256 :] = outside
    data = jnp.concatenate([rows_ref[0], rows_ref[1], rows_ref[2]], axis=1).astype(jnp.bfloat16)
    waves = mxu(table_ref[0, :512, :], data) + mxu(table_ref[1, :512, :], data)
    cos = twist_ref[:256, :LANE]
    sin = twist_ref[:256, LANE:]
    for number in range(3):
        real = waves[:256, number * LANE : (number + 1) * LANE]
        imag = waves[256:, number * LANE : (number + 1) * LANE]
        upper, lower = cut(jnp.concatenate([real * cos - imag * sin, real * sin + imag * cos], axis=1))
        second = table_ref[0, 512:, :]
        freq = mxu(upper, second) + (mxu(lower, second) + mxu(upper, table_ref[1, 512:, :]))
        for kq in range(KQ):
            at = (kq * 3 + number) * 256
            value = freq[kq * 128 : (kq + 1) * 128, :].reshape(PLANES, BLOCKS, 256)
            out_ref[:, :, at : at + 256] = value.astype(jnp.bfloat16)


def blocks_kernel(data_ref, over_ref, under_ref, twist_ref, out_ref):
    omega = twist_ref[pl.ds(256 + 8 * lax.axis_index(SECOND), 8), :LANE]
    owns = [whole_edges(data_ref[plane, :, KQ * 3 * 256 :].astype(jnp.float32)) for plane in range(PLANES)]
    row = lax.broadcasted_iota(jnp.int32, (BLOCKS, LANE), 0)
    wrapped = jnp.where(row == 0, 0.0, pltpu.roll(back(owns[PLANES - 1], 4), 1, 0))
    befores = [wrapped] + [back(own, 4) for own in owns[:-1]]
    opening = jnp.concatenate([rows_of(own, before) for own, before in zip(owns, befores)], axis=0)

    def piece(kq, number, part):
        at = ((kq * 3 + number) * 2 + part) * LANE
        return data_ref[:, :, at : at + LANE].astype(jnp.float32).reshape(128, LANE)

    columns = []
    for ch in range(2):
        zeroth = jnp.broadcast_to(opening[:, 16 * ch : 16 * ch + 1], (128, LANE))
        second = jnp.broadcast_to(opening[:, 16 * ch + 1 : 16 * ch + 2], (128, LANE))
        for kq in range(KQ):
            real = piece(kq, ch, 0) + (zeroth + second * omega[2 * kq : 2 * kq + 1, :])
            imag = piece(kq, ch, 1) + second * omega[2 * kq + 1 : 2 * kq + 2, :]
            columns.append(jnp.concatenate([real, imag], axis=0))
    upper, lower = cut(jnp.concatenate(columns, axis=1))
    waves = mxu(over_ref[0], upper) + (mxu(over_ref[0], lower) + mxu(over_ref[1], upper))
    taps = [jnp.concatenate([piece(kq, 2, 0), piece(kq, 2, 1)], axis=0) for kq in range(KQ)]
    taps = jnp.concatenate(taps, axis=1).astype(jnp.bfloat16)
    taps = mxu(over_ref[0], taps) + mxu(over_ref[1], taps)
    products = []
    for kq in range(KQ):
        tap_real = taps[:WAVES, kq * LANE : (kq + 1) * LANE]
        tap_imag = taps[WAVES:, kq * LANE : (kq + 1) * LANE]
        for ch in range(2):
            at = (ch * KQ + kq) * LANE
            real = waves[:WAVES, at : at + LANE]
            imag = waves[WAVES:, at : at + LANE]
            both = [real * tap_real - imag * tap_imag, real * tap_imag + imag * tap_real]
            products.append(jnp.concatenate(both, axis=0))
    upper, lower = cut(jnp.concatenate(products, axis=1))
    sums = mxu(under_ref[0], upper) + (mxu(under_ref[0], lower) + mxu(under_ref[1], upper))
    for kq in range(KQ):
        for ch in range(2):
            for part in range(2):
                at = (kq * 2 + ch) * LANE
                value = sums[part * 128 : (part + 1) * 128, at : at + LANE].reshape(PLANES, BLOCKS, LANE)
                to = (at // LANE * 2 + part) * LANE
                out_ref[:, :, to : to + LANE] = value.astype(jnp.bfloat16)


def behind_kernel(data_ref, table_ref, twist_ref, out_ref, rows_ref):
    columns = []
    for ch in range(2):
        parts = [[], []]
        for kq in range(KQ):
            at = (kq * 2 + ch) * 256
            block = data_ref[:, :, at : at + 256].astype(jnp.float32).reshape(128, 256).astype(jnp.bfloat16)
            lines = mxu(block, table_ref[0, :, 512:]) + mxu(block, table_ref[1, :, 512:])
            cos = twist_ref[kq * 128 : (kq + 1) * 128, :LANE]
            sin = twist_ref[kq * 128 : (kq + 1) * 128, LANE:]
            real = lines[:, :LANE]
            imag = lines[:, LANE:]
            parts[0].append(real * cos + imag * sin)
            parts[1].append(imag * cos - real * sin)
        columns.append(jnp.concatenate(parts[0] + parts[1], axis=0))
    upper, lower = cut(jnp.concatenate(columns, axis=1))
    first = table_ref[0, :, :512]
    value = mxu(first, upper) + (mxu(first, lower) + mxu(table_ref[1, :, :512], upper))
    for hi in range(HIGH):
        for ch in range(2):
            where = pl.ds(ch * HIGH + hi, PEERS, stride=8)
            rows_ref[where, :] = value[hi * PEERS : (hi + 1) * PEERS, ch * LANE : (ch + 1) * LANE]
    out_ref[...] = rows_ref[...].reshape(PEERS, 8, LANE).astype(jnp.bfloat16)


def gate_kernel(queries_ref, direct_ref, head_ref, earlier_ref, data_ref, out_ref, rows_ref, ext_ref):
    ext_ref[0:8, :] = earlier_ref[...].astype(jnp.float32)
    ext_ref[8:16, :] = head_ref[0:8, :]
    filtered = short_filter(ext_ref, head_ref[8:11, :], 8)
    rows_ref[...] = data_ref[...].astype(jnp.float32).reshape(8 * PEERS, LANE)
    for hi in range(HIGH):
        rows = [rows_ref[pl.ds(ch * HIGH + hi, PEERS, stride=8), :] for ch in range(2)]
        convolved = jnp.concatenate(rows, axis=0).T
        span = slice(hi * LANE, (hi + 1) * LANE)
        out_ref[span, :] = queries_ref[span, :] * (convolved + direct_ref[span, :])
        if hi == 0:
            direct = head_ref[16:17, 0:LANE] * mix_of(filtered)
            out_ref[0:8, :] = filtered[:, :LANE] * (convolved[0:8, :] + direct)


def exchange(value, axis):
    return lax.all_to_all(value, axis, split_axis=0, concat_axis=0, tiled=True)


def far(value):
    return pltpu.with_memory_space_constraint(value, pltpu.HBM)


def on_chip(kernel, outs, scratch, name, *args):
    near = pl.BlockSpec(memory_space=pltpu.VMEM)
    return pl.pallas_call(
        kernel,
        in_specs=[near] * len(args),
        out_specs=tuple(near for _ in outs) if len(outs) > 1 else near,
        out_shape=outs if len(outs) > 1 else outs[0],
        scratch_shapes=scratch,
        name=name,
        compiler_params=GRANT,
    )(*[pltpu.with_memory_space_constraint(arg, pltpu.VMEM) for arg in args])


def on_device(projected, short_taps, skip_gain, long_filter):
    seg, wide = projected.shape
    channels = skip_gain.shape[0]
    count = lax.axis_size(EVERY)
    near = pl.BlockSpec(memory_space=pltpu.VMEM)
    ahead_table, behind_table, over, under, twist = tables()
    plane = pltpu.VMEM((seg, channels), jnp.float32)
    stack = pltpu.VMEM((4, 256, LANE), jnp.float32)
    packed, tail = pl.pallas_call(
        pack_kernel,
        out_specs=(near, near),
        out_shape=(pltpu.VMEM((PEERS, HIGH, 4 * LANE), jnp.bfloat16), pltpu.VMEM((8, wide), jnp.bfloat16)),
        scratch_shapes=[pltpu.VMEM((seg + 8, 2 * LANE), jnp.float32), stack],
        name="pack",
        cost_estimate=pl.CostEstimate(flops=200000000, bytes_accessed=800000, transcendentals=0),
        compiler_params=GRANT,
    )(far(projected), far(short_taps), far(long_filter.reshape(HIGH, LANE)))
    earlier = lax.ppermute(tail, EVERY, [(s, s + 1) for s in range(count - 1)])
    queries, direct, head = pl.pallas_call(
        plan_kernel,
        out_specs=(near, near, near),
        out_shape=(plane, plane, pltpu.VMEM((24, wide), jnp.float32)),
        scratch_shapes=[pltpu.VMEM((seg + 8, wide), jnp.float32)],
        name="plan",
        compiler_params=GRANT,
    )(far(projected), far(short_taps), far(skip_gain.reshape(1, channels)))
    arrived = exchange(packed, FIRST)
    ahead = on_chip(
        ahead_kernel,
        (pltpu.VMEM((PLANES, BLOCKS, KQ * 3 * 256 + LANE), jnp.bfloat16),),
        [stack, pltpu.VMEM((PEERS, LANE), jnp.float32)],
        "ahead",
        arrived,
        ahead_table,
        twist,
    )
    lined = exchange(ahead, SECOND)
    blocks = on_chip(
        blocks_kernel,
        (pltpu.VMEM((PLANES, BLOCKS, KQ * 2 * 256), jnp.bfloat16),),
        [],
        "blocks",
        lined,
        over,
        under,
        twist,
    )
    returned = exchange(blocks, SECOND)
    behind = on_chip(
        behind_kernel,
        (pltpu.VMEM((PEERS, 8, LANE), jnp.bfloat16),),
        [pltpu.VMEM((8 * PEERS, LANE), jnp.float32)],
        "behind",
        returned,
        behind_table,
        twist,
    )
    home = exchange(behind, FIRST)
    return pl.pallas_call(
        gate_kernel,
        in_specs=[near] * 5,
        out_shape=jax.ShapeDtypeStruct((seg, channels), jnp.float32),
        scratch_shapes=[pltpu.VMEM((8 * PEERS, LANE), jnp.float32), pltpu.VMEM((16, wide), jnp.float32)],
        name="gate",
        compiler_params=GRANT,
    )(*[pltpu.with_memory_space_constraint(arg, pltpu.VMEM) for arg in (queries, direct, head, earlier, home)])


def solution(mesh):
    fine = Mesh(mesh.devices.reshape(SPLIT), EVERY)
    placed = (P(EVERY, None), P(), P(), P(EVERY))
    return jax.shard_map(on_device, mesh=fine, in_specs=placed, out_specs=P(EVERY, None), check_vma=False)
```

```python
import numpy as np

import jax
import jax.numpy as jnp
from jax import lax
from jax.experimental import pallas as pl
from jax.experimental.pallas import tpu as pltpu
from jax.sharding import Mesh, PartitionSpec as P

LANE = 128
FIRST = ("zh", "y", "zl")
SECOND = ("core", "x")
EVERY = ("zh", "y", "core", "x", "zl")
SPLIT = (2, 8, 2, 4, 4)
PEERS = 64
BLOCKS = 16
PLANES = 8
HIGH = 4
RUN = 4
SPAN = 2048
LINES = 16
KQ = 2
WAVES = 256
GRANT = pltpu.CompilerParams(vmem_limit_bytes=12 * 2**20)
EDGE = ((0, 0), (1, 0), (0, 1), (1, 1), (2, 0), (3, 0), (2, 1), (3, 1))


def turn_of(phase):
    turn = 2.0 * np.pi * np.asarray(phase, np.float64)
    return np.cos(turn), np.sin(turn)


def halves(table):
    table = np.asarray(table, np.float32)
    upper = table.astype(jnp.bfloat16)
    lower = (table - upper.astype(np.float32)).astype(jnp.bfloat16)
    return np.stack([upper, lower])


def tables():
    line = np.arange(LINES)
    same = np.eye(BLOCKS)
    cos, sin = turn_of(np.outer(line + 0.25, line) / LINES)

    def forward(part):
        small = part.reshape(PLANES, KQ, RUN, HIGH)
        return np.einsum("jkzr,bc->kjbczr", small, same).reshape(256, 256)

    def backward(part):
        small = part.reshape(PLANES, KQ, RUN, HIGH) / SPAN
        return np.einsum("jkzr,bc->rczkjb", small, same).reshape(256, 256)

    first = np.concatenate([forward(cos), forward(sin)], axis=0)
    first_back = np.concatenate([backward(cos), backward(sin)], axis=1)
    cos, sin = turn_of(np.outer(line + 0.25, np.arange(LANE)) / SPAN)
    rows = np.broadcast_to(line.reshape(PLANES, KQ).T[:, :, None], (KQ, PLANES, BLOCKS)).reshape(-1)
    twist = np.concatenate([cos[rows], sin[rows]], axis=1)
    cos, sin = turn_of(np.outer(np.arange(LANE), np.arange(LANE)) / LANE)
    second = np.block([[cos, sin], [-sin, cos]])
    block = (np.arange(BLOCKS)[None, :] * PLANES + np.arange(PLANES)[:, None]).reshape(-1)
    wave = np.arange(WAVES)
    cos, sin = turn_of(np.outer(wave, block) / WAVES)
    over = np.block([[cos, sin], [-sin, cos]])
    cos_before, sin_before = turn_of(np.outer(wave, block - 1) / WAVES)
    real = (cos + sin_before).T / WAVES
    imag = (sin - cos_before).T / WAVES
    under = np.block([[real, -imag], [imag, real]])
    spot = line.reshape(PLANES, KQ, 1) + LINES * np.arange(LANE) + 0.25
    omega = np.stack(turn_of(spot / SPAN), axis=2).reshape(PLANES, 2 * KQ, LANE)
    omega = np.concatenate([omega, np.zeros_like(omega)], axis=1).reshape(8 * PLANES, LANE)
    twist = np.concatenate([twist, np.concatenate([omega, np.zeros_like(omega)], axis=1)], axis=0).astype(np.float32)
    ahead = halves(np.concatenate([first, second], axis=0))
    behind = halves(np.concatenate([first_back, second.T], axis=1))
    return ahead, behind, halves(over), halves(under), twist


def mxu(left, right):
    return jnp.dot(left, right, preferred_element_type=jnp.float32)


def cut(value):
    upper = value.astype(jnp.bfloat16)
    return upper, (value - upper.astype(jnp.float32)).astype(jnp.bfloat16)


def short_filter(ext_ref, taps, seg):
    total = taps[0:1, :] * ext_ref[8 : 8 + seg, :]
    for tap in range(1, taps.shape[0]):
        total = total + taps[tap : tap + 1, :] * ext_ref[8 - tap : 8 - tap + seg, :]
    return total


def mix_of(filtered):
    mixture = (filtered[:, LANE : 2 * LANE] * filtered[:, 2 * LANE :]).astype(jnp.bfloat16)
    return mixture.astype(jnp.float32)


def pack_kernel(
    projected_ref, taps_ref, gain_ref, filter_ref, out_ref, queries_ref, direct_ref, head_ref, ext_ref, rows_ref
):
    seg = projected_ref.shape[0]
    ext_ref[0:8, :] = jnp.zeros((8, 3 * LANE), jnp.float32)
    ext_ref[8 : 8 + seg, :] = projected_ref[...].astype(jnp.float32)
    head_ref[0:8, :] = ext_ref[8:16, :LANE]
    head_ref[8:11, :] = taps_ref[:, :LANE]
    head_ref[16:17, :] = gain_ref[...]
    filtered = short_filter(ext_ref, taps_ref[...], seg)
    mixture = mix_of(filtered)
    queries_ref[...] = filtered[:, :LANE]
    direct = gain_ref[...] * mixture
    direct_ref[...] = direct
    direct_ref[0:8, :] = jnp.where(lax.broadcasted_iota(jnp.int32, (8, LANE), 0) < 2, 0.0, direct[0:8, :])
    taps = taps_ref[:, LANE:]
    last = ext_ref[7 + seg : 8 + seg, LANE:]
    carry = taps[1:2, :] * last + taps[2:3, :] * ext_ref[6 + seg : 7 + seg, LANE:]
    ends = [filtered[0:1, LANE:], filtered[1:2, LANE:], carry, taps[2:3, :] * last]
    ends = [ends[row][:, half * LANE : (half + 1) * LANE] for row, half in EDGE]
    upper, lower = cut(jnp.concatenate(ends, axis=0))
    pad = jnp.zeros((LANE - 16, LANE), jnp.float32)
    flipped = jnp.concatenate([upper.astype(jnp.float32), lower.astype(jnp.float32), pad], axis=0).T
    lane = lax.broadcasted_iota(jnp.int32, (PEERS, LANE), 1)
    edges = jnp.where(lane < 16, flipped[:PEERS, :], pltpu.roll(flipped[PEERS:, :], 16, 1))
    extra = [edges]
    for row in (6 + seg, 7 + seg):
        extra.append(jnp.broadcast_to(ext_ref[row : row + 1, :LANE], (PEERS, LANE)))
    extra.append(jnp.zeros((PEERS, LANE), jnp.float32))
    for hi in range(HIGH):
        flipped = mixture[hi * LANE : (hi + 1) * LANE, :].T
        where = pl.ds(hi, PEERS, stride=HIGH)
        for ch in range(2):
            rows_ref[ch, where, :] = flipped[ch * PEERS : (ch + 1) * PEERS, :]
        taps_row = filter_ref[hi : hi + 1, :].astype(jnp.float32)
        rows_ref[2, where, :] = jnp.broadcast_to(taps_row, (PEERS, LANE))
        rows_ref[3, where, :] = extra[hi]
    for at in range(4):
        out_ref[:, :, at * LANE : (at + 1) * LANE] = rows_ref[at].reshape(PEERS, HIGH, LANE).astype(jnp.bfloat16)


def back(value, lanes):
    return pltpu.roll(value, LANE - lanes, 1)


def whole_edges(edges):
    return edges + back(edges, 8)


def rows_of(own, before):
    total = own + before
    return (total * back(total, 2)).astype(jnp.bfloat16).astype(jnp.float32)


def ahead_kernel(data_ref, table_ref, twist_ref, out_ref, mix_ref, tail_ref, rows_ref, edge_ref):
    for at in range(4):
        block = data_ref[:, :, at * LANE : (at + 1) * LANE].astype(jnp.float32)
        rows_ref[at] = block.reshape(256, LANE)
    where = pl.ds(0, PEERS, stride=HIGH)
    edges = rows_ref[3, where, :]
    edge_ref[...] = edges
    own = whole_edges(edges)
    mixture = rows_of(own, pltpu.roll(back(own, 4), 1, 0))
    inside = (lax.broadcasted_iota(jnp.int32, (PEERS, LANE), 0) & (RUN - 1)) != 0
    lane = lax.broadcasted_iota(jnp.int32, (PEERS, LANE), 1)
    mixture = jnp.where(inside, mixture, 0.0)
    mix_ref[...] = mixture
    own_place = lax.axis_index(FIRST)
    before = jnp.maximum(own_place - 1, 0)
    ending = jnp.where(lax.axis_index(SECOND) == PLANES - 1, before, jnp.minimum(own_place + RUN - 1, PEERS - 1))
    for row in range(2):
        tail_ref[row : row + 1, :] = rows_ref[3, pl.ds(before * HIGH + 1 + row, 1), :]
    relay = []
    for row in range(2):
        value = rows_ref[3, pl.ds(ending * HIGH + 1 + row, 1), :]
        relay += [pltpu.roll(value, LANE // 2, 1), value]
    relay = jnp.concatenate(relay + [jnp.zeros((BLOCKS - 4, LANE), jnp.float32)], axis=0)
    for ch in range(2):
        fresh = back(mixture, 16 * ch) if ch else mixture
        rows_ref[ch, where, :] = jnp.where(lane < 2, fresh, rows_ref[ch, where, :])
    opening = edge_ref[pl.ds(0, BLOCKS, stride=RUN), :]
    closing = edge_ref[pl.ds(RUN - 1, BLOCKS, stride=RUN), :]
    outside = jnp.where((lane[:BLOCKS, :] & 4) == 0, opening, closing)
    outside = jnp.where(lane[:BLOCKS, :] < LANE // 2, outside, relay).astype(jnp.bfloat16)
    for plane in range(PLANES):
        out_ref[plane, :, KQ * 3 * 256 :] = outside
    data = jnp.concatenate([rows_ref[0], rows_ref[1], rows_ref[2]], axis=1).astype(jnp.bfloat16)
    waves = mxu(table_ref[0, :512, :], data) + mxu(table_ref[1, :512, :], data)
    cos = twist_ref[:256, :LANE]
    sin = twist_ref[:256, LANE:]
    for number in range(3):
        real = waves[:256, number * LANE : (number + 1) * LANE]
        imag = waves[256:, number * LANE : (number + 1) * LANE]
        upper, lower = cut(jnp.concatenate([real * cos - imag * sin, real * sin + imag * cos], axis=1))
        second = table_ref[0, 512:, :]
        freq = mxu(upper, second) + (mxu(lower, second) + mxu(upper, table_ref[1, 512:, :]))
        for kq in range(KQ):
            at = (kq * 3 + number) * 256
            value = freq[kq * 128 : (kq + 1) * 128, :].reshape(PLANES, BLOCKS, 256)
            out_ref[:, :, at : at + 256] = value.astype(jnp.bfloat16)


def blocks_kernel(data_ref, over_ref, under_ref, twist_ref, out_ref, start_ref, tail_ref, open_ref):
    plane = lax.axis_index(SECOND)
    omega = twist_ref[pl.ds(256 + 8 * plane, 8), :LANE]
    before = jnp.where(plane == 0, PLANES - 1, plane - 1)
    relay = data_ref[pl.ds(before, 1), :, KQ * 3 * 256 :].astype(jnp.float32).reshape(BLOCKS, LANE)
    low = lax.broadcasted_iota(jnp.int32, (1, LANE), 1) < LANE // 2
    for row in range(2):
        value = pltpu.roll(relay[2 * row : 2 * row + 1, :], LANE // 2, 1)
        tail_ref[row : row + 1, :] = jnp.where(low, value, relay[2 * row + 1 : 2 * row + 2, :])
    owns = [whole_edges(data_ref[plane, :, KQ * 3 * 256 :].astype(jnp.float32)) for plane in range(PLANES)]
    row = lax.broadcasted_iota(jnp.int32, (BLOCKS, LANE), 0)
    wrapped = jnp.where(row == 0, 0.0, pltpu.roll(back(owns[PLANES - 1], 4), 1, 0))
    befores = [wrapped] + [back(own, 4) for own in owns[:-1]]
    opening = jnp.concatenate([rows_of(own, before) for own, before in zip(owns, befores)], axis=0)
    open_ref[...] = opening
    start_ref[...] = open_ref[pl.ds(pl.multiple_of(plane * BLOCKS, BLOCKS), BLOCKS), :]

    def piece(kq, number, part):
        at = ((kq * 3 + number) * 2 + part) * LANE
        return data_ref[:, :, at : at + LANE].astype(jnp.float32).reshape(128, LANE)

    columns = []
    for ch in range(2):
        zeroth = jnp.broadcast_to(opening[:, 16 * ch : 16 * ch + 1], (128, LANE))
        second = jnp.broadcast_to(opening[:, 16 * ch + 1 : 16 * ch + 2], (128, LANE))
        for kq in range(KQ):
            real = piece(kq, ch, 0) + (zeroth + second * omega[2 * kq : 2 * kq + 1, :])
            imag = piece(kq, ch, 1) + second * omega[2 * kq + 1 : 2 * kq + 2, :]
            columns.append(jnp.concatenate([real, imag], axis=0))
    upper, lower = cut(jnp.concatenate(columns, axis=1))
    waves = mxu(over_ref[0], upper) + (mxu(over_ref[0], lower) + mxu(over_ref[1], upper))
    taps = [jnp.concatenate([piece(kq, 2, 0), piece(kq, 2, 1)], axis=0) for kq in range(KQ)]
    taps = jnp.concatenate(taps, axis=1).astype(jnp.bfloat16)
    taps = mxu(over_ref[0], taps) + mxu(over_ref[1], taps)
    products = []
    for kq in range(KQ):
        tap_real = taps[:WAVES, kq * LANE : (kq + 1) * LANE]
        tap_imag = taps[WAVES:, kq * LANE : (kq + 1) * LANE]
        for ch in range(2):
            at = (ch * KQ + kq) * LANE
            real = waves[:WAVES, at : at + LANE]
            imag = waves[WAVES:, at : at + LANE]
            both = [real * tap_real - imag * tap_imag, real * tap_imag + imag * tap_real]
            products.append(jnp.concatenate(both, axis=0))
    upper, lower = cut(jnp.concatenate(products, axis=1))
    sums = mxu(under_ref[0], upper) + (mxu(under_ref[0], lower) + mxu(under_ref[1], upper))
    for kq in range(KQ):
        for ch in range(2):
            for part in range(2):
                at = (kq * 2 + ch) * LANE
                value = sums[part * 128 : (part + 1) * 128, at : at + LANE].reshape(PLANES, BLOCKS, LANE)
                to = (at // LANE * 2 + part) * LANE
                out_ref[:, :, to : to + LANE] = value.astype(jnp.bfloat16)


def behind_kernel(data_ref, table_ref, twist_ref, head_ref, mix_ref, start_ref, out_ref, rows_ref, fix_ref):
    columns = []
    for ch in range(2):
        parts = [[], []]
        for kq in range(KQ):
            at = (kq * 2 + ch) * 256
            block = data_ref[:, :, at : at + 256].astype(jnp.float32).reshape(128, 256).astype(jnp.bfloat16)
            lines = mxu(block, table_ref[0, :, 512:]) + mxu(block, table_ref[1, :, 512:])
            cos = twist_ref[kq * 128 : (kq + 1) * 128, :LANE]
            sin = twist_ref[kq * 128 : (kq + 1) * 128, LANE:]
            real = lines[:, :LANE]
            imag = lines[:, LANE:]
            parts[0].append(real * cos + imag * sin)
            parts[1].append(imag * cos - real * sin)
        columns.append(jnp.concatenate(parts[0] + parts[1], axis=0))
    upper, lower = cut(jnp.concatenate(columns, axis=1))
    first = table_ref[0, :, :512]
    value = mxu(first, upper) + (mxu(first, lower) + mxu(table_ref[1, :, :512], upper))
    for hi in range(HIGH):
        for ch in range(2):
            where = pl.ds(ch * HIGH + hi, PEERS, stride=8)
            rows_ref[where, :] = value[hi * PEERS : (hi + 1) * PEERS, ch * LANE : (ch + 1) * LANE]
    fix_ref[...] = mix_ref[...]
    fix_ref[pl.ds(0, BLOCKS, stride=RUN), :] = start_ref[...]
    mixture = fix_ref[...]
    lane = lax.broadcasted_iota(jnp.int32, (PEERS, LANE), 1)
    for ch in range(2):
        mine = lane[0:1, :] == ch * PEERS + lax.axis_index(FIRST)
        gain = jnp.sum(jnp.where(mine, head_ref[16:17, :], 0.0), axis=1, keepdims=True)
        fresh = back(mixture, 16 * ch) if ch else mixture
        where = pl.ds(ch * HIGH, PEERS, stride=8)
        rows_ref[where, :] = rows_ref[where, :] + jnp.where(lane < 2, gain * fresh, 0.0)
    out_ref[...] = rows_ref[...].reshape(PEERS, 8, LANE).astype(jnp.bfloat16)


def gate_kernel(queries_ref, direct_ref, head_ref, inside_ref, outside_ref, data_ref, out_ref, rows_ref, ext_ref):
    place = lax.axis_index(FIRST)
    ext_ref[0:8, :] = jnp.zeros((8, LANE), jnp.float32)

    @pl.when((place & (RUN - 1)) != 0)
    def _():
        ext_ref[6:8, :] = inside_ref[0:2, :]

    @pl.when(((place & (RUN - 1)) == 0) & (place + lax.axis_index(SECOND) > 0))
    def _():
        ext_ref[6:8, :] = outside_ref[0:2, :]

    ext_ref[8:16, :] = head_ref[0:8, :]
    queries = short_filter(ext_ref, head_ref[8:11, :], 8)
    rows_ref[...] = data_ref[...].astype(jnp.float32).reshape(8 * PEERS, LANE)
    for hi in range(HIGH):
        rows = [rows_ref[pl.ds(ch * HIGH + hi, PEERS, stride=8), :] for ch in range(2)]
        convolved = jnp.concatenate(rows, axis=0).T
        span = slice(hi * LANE, (hi + 1) * LANE)
        out_ref[span, :] = queries_ref[span, :] * (convolved + direct_ref[span, :])
        if hi == 0:
            out_ref[0:8, :] = queries * (convolved[0:8, :] + direct_ref[0:8, :])


def exchange(value, axis):
    return lax.all_to_all(value, axis, split_axis=0, concat_axis=0, tiled=True)


def far(value):
    return pltpu.with_memory_space_constraint(value, pltpu.HBM)


def on_chip(kernel, outs, scratch, name, *args):
    near = pl.BlockSpec(memory_space=pltpu.VMEM)
    return pl.pallas_call(
        kernel,
        in_specs=[near] * len(args),
        out_specs=tuple(near for _ in outs) if len(outs) > 1 else near,
        out_shape=outs if len(outs) > 1 else outs[0],
        scratch_shapes=scratch,
        name=name,
        compiler_params=GRANT,
    )(*[pltpu.with_memory_space_constraint(arg, pltpu.VMEM) for arg in args])


def on_device(projected, short_taps, skip_gain, long_filter):
    seg, wide = projected.shape
    channels = skip_gain.shape[0]
    near = pl.BlockSpec(memory_space=pltpu.VMEM)
    ahead_table, behind_table, over, under, twist = tables()
    plane = pltpu.VMEM((seg, channels), jnp.float32)
    stack = pltpu.VMEM((4, 256, LANE), jnp.float32)
    corner = pltpu.VMEM((8, LANE), jnp.float32)
    wide_rows = pltpu.VMEM((PEERS, LANE), jnp.float32)
    packed, queries, direct, head = pl.pallas_call(
        pack_kernel,
        out_specs=(near,) * 4,
        out_shape=(
            pltpu.VMEM((PEERS, HIGH, 4 * LANE), jnp.bfloat16),
            plane,
            plane,
            pltpu.VMEM((24, LANE), jnp.float32),
        ),
        scratch_shapes=[pltpu.VMEM((seg + 8, wide), jnp.float32), stack],
        name="pack",
        cost_estimate=pl.CostEstimate(flops=200000000, bytes_accessed=800000, transcendentals=0),
        compiler_params=GRANT,
    )(
        far(projected),
        far(short_taps),
        far(skip_gain.reshape(1, channels)),
        far(long_filter.reshape(HIGH, LANE)),
    )
    arrived = exchange(packed, FIRST)
    ahead, mixture, inside = on_chip(
        ahead_kernel,
        (pltpu.VMEM((PLANES, BLOCKS, KQ * 3 * 256 + LANE), jnp.bfloat16), wide_rows, corner),
        [stack, wide_rows],
        "ahead",
        arrived,
        ahead_table,
        twist,
    )
    lined = exchange(ahead, SECOND)
    blocks, start, outside = on_chip(
        blocks_kernel,
        (
            pltpu.VMEM((PLANES, BLOCKS, KQ * 2 * 256), jnp.bfloat16),
            pltpu.VMEM((BLOCKS, LANE), jnp.float32),
            corner,
        ),
        [pltpu.VMEM((128, LANE), jnp.float32)],
        "blocks",
        lined,
        over,
        under,
        twist,
    )
    returned = exchange(blocks, SECOND)
    behind = on_chip(
        behind_kernel,
        (pltpu.VMEM((PEERS, 8, LANE), jnp.bfloat16),),
        [pltpu.VMEM((8 * PEERS, LANE), jnp.float32), wide_rows],
        "behind",
        returned,
        behind_table,
        twist,
        head,
        mixture,
        start,
    )
    home = exchange(behind, FIRST)
    return pl.pallas_call(
        gate_kernel,
        in_specs=[near] * 6,
        out_shape=jax.ShapeDtypeStruct((seg, channels), jnp.float32),
        scratch_shapes=[pltpu.VMEM((8 * PEERS, LANE), jnp.float32), pltpu.VMEM((16, LANE), jnp.float32)],
        name="gate",
        compiler_params=GRANT,
    )(*[pltpu.with_memory_space_constraint(arg, pltpu.VMEM) for arg in (queries, direct, head, inside, outside, home)])


def solution(mesh):
    fine = Mesh(mesh.devices.reshape(SPLIT), EVERY)
    placed = (P(EVERY, None), P(), P(), P(EVERY))
    return jax.shard_map(on_device, mesh=fine, in_specs=placed, out_specs=P(EVERY, None), check_vma=False)
```

```python
import numpy as np

import jax
import jax.numpy as jnp
from jax import lax
from jax.experimental import pallas as pl
from jax.experimental.pallas import tpu as pltpu
from jax.sharding import Mesh, PartitionSpec as P

LANE = 128
FIRST = ("zh", "y", "zl")
SECOND = ("core", "x")
EVERY = ("zh", "y", "core", "x", "zl")
SPLIT = (2, 8, 2, 4, 4)
PEERS = 64
BLOCKS = 16
PLANES = 8
HIGH = 4
RUN = 4
SPAN = 2048
LINES = 16
KQ = 2
WAVES = 256
GRANT = pltpu.CompilerParams(vmem_limit_bytes=12 * 2**20)
EDGE = ((0, 0), (1, 0), (0, 1), (1, 1), (2, 0), (3, 0), (2, 1), (3, 1))


def turn_of(phase):
    turn = 2.0 * np.pi * np.asarray(phase, np.float64)
    return np.cos(turn), np.sin(turn)


def halves(table):
    table = np.asarray(table, np.float32)
    upper = table.astype(jnp.bfloat16)
    lower = (table - upper.astype(np.float32)).astype(jnp.bfloat16)
    return np.stack([upper, lower])


def tables():
    line = np.arange(LINES)
    same = np.eye(BLOCKS)
    cos, sin = turn_of(np.outer(line + 0.25, line) / LINES)

    def forward(part):
        small = part.reshape(PLANES, KQ, RUN, HIGH)
        return np.einsum("jkzr,bc->kjbczr", small, same).reshape(256, 256)

    def backward(part):
        small = part.reshape(PLANES, KQ, RUN, HIGH) / SPAN
        return np.einsum("jkzr,bc->rczkjb", small, same).reshape(256, 256)

    first = np.concatenate([forward(cos), forward(sin)], axis=0)
    first_back = np.concatenate([backward(cos), backward(sin)], axis=1)
    cos, sin = turn_of(np.outer(line + 0.25, np.arange(LANE)) / SPAN)
    rows = np.broadcast_to(line.reshape(PLANES, KQ).T[:, :, None], (KQ, PLANES, BLOCKS)).reshape(-1)
    twist = np.concatenate([cos[rows], sin[rows]], axis=1)
    cos, sin = turn_of(np.outer(np.arange(LANE), np.arange(LANE)) / LANE)
    second = np.block([[cos, sin], [-sin, cos]])
    block = (np.arange(BLOCKS)[None, :] * PLANES + np.arange(PLANES)[:, None]).reshape(-1)
    wave = np.arange(WAVES)
    cos, sin = turn_of(np.outer(wave, block) / WAVES)
    over = np.block([[cos, sin], [-sin, cos]])
    cos_before, sin_before = turn_of(np.outer(wave, block - 1) / WAVES)
    real = (cos + sin_before).T / WAVES
    imag = (sin - cos_before).T / WAVES
    under = np.block([[real, -imag], [imag, real]])
    spot = line.reshape(PLANES, KQ, 1) + LINES * np.arange(LANE) + 0.25
    omega = np.stack(turn_of(spot / SPAN), axis=2).reshape(PLANES, 2 * KQ, LANE)
    omega = np.concatenate([omega, np.zeros_like(omega)], axis=1).reshape(8 * PLANES, LANE)
    twist = np.concatenate([twist, np.concatenate([omega, np.zeros_like(omega)], axis=1)], axis=0).astype(np.float32)
    ahead = halves(np.concatenate([first, second], axis=0))
    behind = halves(np.concatenate([first_back, second.T], axis=1))
    return ahead, behind, halves(over), halves(under), twist


def mxu(left, right):
    return jnp.dot(left, right, preferred_element_type=jnp.float32)


def cut(value):
    upper = value.astype(jnp.bfloat16)
    return upper, (value - upper.astype(jnp.float32)).astype(jnp.bfloat16)


def short_filter(ext_ref, taps, seg):
    total = taps[0:1, :] * ext_ref[8 : 8 + seg, :]
    for tap in range(1, taps.shape[0]):
        total = total + taps[tap : tap + 1, :] * ext_ref[8 - tap : 8 - tap + seg, :]
    return total


def mix_of(filtered):
    mixture = (filtered[:, LANE : 2 * LANE] * filtered[:, 2 * LANE :]).astype(jnp.bfloat16)
    return mixture.astype(jnp.float32)


def pack_kernel(
    projected_ref, taps_ref, gain_ref, filter_ref, out_ref, queries_ref, direct_ref, head_ref, ext_ref, rows_ref
):
    seg = projected_ref.shape[0]
    ext_ref[0:8, :] = jnp.zeros((8, 3 * LANE), jnp.float32)
    ext_ref[8 : 8 + seg, :] = projected_ref[...].astype(jnp.float32)
    head_ref[0:8, :] = ext_ref[8:16, :LANE]
    head_ref[8:11, :] = taps_ref[:, :LANE]
    head_ref[16:17, :] = gain_ref[...]
    filtered = short_filter(ext_ref, taps_ref[...], seg)
    mixture = mix_of(filtered)
    queries_ref[...] = filtered[:, :LANE]
    direct = gain_ref[...] * mixture
    direct_ref[...] = direct
    direct_ref[0:8, :] = jnp.where(lax.broadcasted_iota(jnp.int32, (8, LANE), 0) < 2, 0.0, direct[0:8, :])
    taps = taps_ref[:, LANE:]
    last = ext_ref[7 + seg : 8 + seg, LANE:]
    carry = taps[1:2, :] * last + taps[2:3, :] * ext_ref[6 + seg : 7 + seg, LANE:]
    ends = [filtered[0:1, LANE:], filtered[1:2, LANE:], carry, taps[2:3, :] * last]
    ends = [ends[row][:, half * LANE : (half + 1) * LANE] for row, half in EDGE]
    upper, lower = cut(jnp.concatenate(ends, axis=0))
    pad = jnp.zeros((LANE - 16, LANE), jnp.float32)
    flipped = jnp.concatenate([upper.astype(jnp.float32), lower.astype(jnp.float32), pad], axis=0).T
    lane = lax.broadcasted_iota(jnp.int32, (PEERS, LANE), 1)
    edges = jnp.where(lane < 16, flipped[:PEERS, :], pltpu.roll(flipped[PEERS:, :], 16, 1))
    extra = [edges]
    for row in (6 + seg, 7 + seg):
        extra.append(jnp.broadcast_to(ext_ref[row : row + 1, :LANE], (PEERS, LANE)))
    extra.append(jnp.zeros((PEERS, LANE), jnp.float32))
    for hi in range(HIGH):
        flipped = mixture[hi * LANE : (hi + 1) * LANE, :].T
        where = pl.ds(hi, PEERS, stride=HIGH)
        for ch in range(2):
            rows_ref[ch, where, :] = flipped[ch * PEERS : (ch + 1) * PEERS, :]
        taps_row = filter_ref[hi : hi + 1, :].astype(jnp.float32)
        rows_ref[2, where, :] = jnp.broadcast_to(taps_row, (PEERS, LANE))
        rows_ref[3, where, :] = extra[hi]
    for at in range(4):
        out_ref[:, :, at * LANE : (at + 1) * LANE] = rows_ref[at].reshape(PEERS, HIGH, LANE).astype(jnp.bfloat16)


def back(value, lanes):
    return pltpu.roll(value, LANE - lanes, 1)


def whole_edges(edges):
    return edges + back(edges, 8)


def rows_of(own, before):
    total = own + before
    return (total * back(total, 2)).astype(jnp.bfloat16).astype(jnp.float32)


def ahead_kernel(data_ref, table_ref, twist_ref, out_ref, mix_ref, tail_ref, rows_ref, edge_ref):
    for at in range(4):
        block = data_ref[:, :, at * LANE : (at + 1) * LANE].astype(jnp.float32)
        rows_ref[at] = block.reshape(256, LANE)
    where = pl.ds(0, PEERS, stride=HIGH)
    edges = rows_ref[3, where, :]
    edge_ref[...] = edges
    own = whole_edges(edges)
    mixture = rows_of(own, pltpu.roll(back(own, 4), 1, 0))
    inside = (lax.broadcasted_iota(jnp.int32, (PEERS, LANE), 0) & (RUN - 1)) != 0
    lane = lax.broadcasted_iota(jnp.int32, (PEERS, LANE), 1)
    mixture = jnp.where(inside, mixture, 0.0)
    mix_ref[...] = mixture
    own_place = lax.axis_index(FIRST)
    before = jnp.maximum(own_place - 1, 0)
    ending = jnp.where(lax.axis_index(SECOND) == PLANES - 1, before, jnp.minimum(own_place + RUN - 1, PEERS - 1))
    for row in range(2):
        tail_ref[row : row + 1, :] = rows_ref[3, pl.ds(before * HIGH + 1 + row, 1), :]
    relay = []
    for row in range(2):
        value = rows_ref[3, pl.ds(ending * HIGH + 1 + row, 1), :]
        relay += [pltpu.roll(value, LANE // 2, 1), value]
    relay = jnp.concatenate(relay + [jnp.zeros((BLOCKS - 4, LANE), jnp.float32)], axis=0)
    for ch in range(2):
        fresh = back(mixture, 16 * ch) if ch else mixture
        rows_ref[ch, where, :] = jnp.where(lane < 2, fresh, rows_ref[ch, where, :])
    opening = edge_ref[pl.ds(0, BLOCKS, stride=RUN), :]
    closing = edge_ref[pl.ds(RUN - 1, BLOCKS, stride=RUN), :]
    outside = jnp.where((lane[:BLOCKS, :] & 4) == 0, opening, closing)
    outside = jnp.where(lane[:BLOCKS, :] < LANE // 2, outside, relay).astype(jnp.bfloat16)
    for plane in range(PLANES):
        out_ref[plane, :, KQ * 3 * 256 :] = outside
    data = jnp.concatenate([rows_ref[0], rows_ref[1], rows_ref[2]], axis=1).astype(jnp.bfloat16)
    waves = mxu(table_ref[0, :512, :], data) + mxu(table_ref[1, :512, :], data)
    cos = twist_ref[:256, :LANE]
    sin = twist_ref[:256, LANE:]
    for number in range(3):
        real = waves[:256, number * LANE : (number + 1) * LANE]
        imag = waves[256:, number * LANE : (number + 1) * LANE]
        upper, lower = cut(jnp.concatenate([real * cos - imag * sin, real * sin + imag * cos], axis=1))
        second = table_ref[0, 512:, :]
        freq = mxu(upper, second) + (mxu(lower, second) + mxu(upper, table_ref[1, 512:, :]))
        for kq in range(KQ):
            at = (kq * 3 + number) * 256
            value = freq[kq * 128 : (kq + 1) * 128, :].reshape(PLANES, BLOCKS, 256)
            out_ref[:, :, at : at + 256] = value.astype(jnp.bfloat16)


def blocks_kernel(data_ref, over_ref, under_ref, twist_ref, out_ref, start_ref, tail_ref, open_ref):
    plane = lax.axis_index(SECOND)
    omega = twist_ref[pl.ds(256 + 8 * plane, 8), :LANE]
    before = jnp.where(plane == 0, PLANES - 1, plane - 1)
    relay = data_ref[pl.ds(before, 1), :, KQ * 3 * 256 :].astype(jnp.float32).reshape(BLOCKS, LANE)
    low = lax.broadcasted_iota(jnp.int32, (1, LANE), 1) < LANE // 2
    for row in range(2):
        value = pltpu.roll(relay[2 * row : 2 * row + 1, :], LANE // 2, 1)
        tail_ref[row : row + 1, :] = jnp.where(low, value, relay[2 * row + 1 : 2 * row + 2, :])
    owns = [whole_edges(data_ref[plane, :, KQ * 3 * 256 :].astype(jnp.float32)) for plane in range(PLANES)]
    row = lax.broadcasted_iota(jnp.int32, (BLOCKS, LANE), 0)
    wrapped = jnp.where(row == 0, 0.0, pltpu.roll(back(owns[PLANES - 1], 4), 1, 0))
    befores = [wrapped] + [back(own, 4) for own in owns[:-1]]
    opening = jnp.concatenate([rows_of(own, before) for own, before in zip(owns, befores)], axis=0)
    open_ref[...] = opening
    start_ref[...] = open_ref[pl.ds(pl.multiple_of(plane * BLOCKS, BLOCKS), BLOCKS), :]

    def piece(kq, number, part):
        at = ((kq * 3 + number) * 2 + part) * LANE
        return data_ref[:, :, at : at + LANE].astype(jnp.float32).reshape(128, LANE)

    taps = [jnp.concatenate([piece(kq, 2, 0), piece(kq, 2, 1)], axis=0) for kq in range(KQ)]
    taps = jnp.concatenate(taps, axis=1).astype(jnp.bfloat16)
    taps = mxu(over_ref[0], taps) + mxu(over_ref[1], taps)
    for ch in range(2):
        zeroth = jnp.broadcast_to(opening[:, 16 * ch : 16 * ch + 1], (128, LANE))
        second = jnp.broadcast_to(opening[:, 16 * ch + 1 : 16 * ch + 2], (128, LANE))
        columns = []
        for kq in range(KQ):
            real = piece(kq, ch, 0) + (zeroth + second * omega[2 * kq : 2 * kq + 1, :])
            imag = piece(kq, ch, 1) + second * omega[2 * kq + 1 : 2 * kq + 2, :]
            columns.append(jnp.concatenate([real, imag], axis=0))
        upper, lower = cut(jnp.concatenate(columns, axis=1))
        real, imag = (
            mxu(over_ref[0, half], upper) + (mxu(over_ref[0, half], lower) + mxu(over_ref[1, half], upper))
            for half in (slice(0, WAVES), slice(WAVES, 2 * WAVES))
        )
        tap_real, tap_imag = taps[:WAVES], taps[WAVES:]
        both = [real * tap_real - imag * tap_imag, real * tap_imag + imag * tap_real]
        upper, lower = cut(jnp.concatenate(both, axis=0))
        for part in range(2):
            half = slice(part * 128, (part + 1) * 128)
            sums = mxu(under_ref[0, half], upper) + (mxu(under_ref[0, half], lower) + mxu(under_ref[1, half], upper))
            for kq in range(KQ):
                value = sums[:, kq * LANE : (kq + 1) * LANE]
                to = ((kq * 2 + ch) * 2 + part) * LANE
                out_ref[:, :, to : to + LANE] = value.reshape(PLANES, BLOCKS, LANE).astype(jnp.bfloat16)


def behind_kernel(data_ref, table_ref, twist_ref, head_ref, mix_ref, start_ref, out_ref, rows_ref, fix_ref):
    columns = []
    for ch in range(2):
        parts = [[], []]
        for kq in range(KQ):
            at = (kq * 2 + ch) * 256
            block = data_ref[:, :, at : at + 256].astype(jnp.float32).reshape(128, 256).astype(jnp.bfloat16)
            lines = mxu(block, table_ref[0, :, 512:]) + mxu(block, table_ref[1, :, 512:])
            cos = twist_ref[kq * 128 : (kq + 1) * 128, :LANE]
            sin = twist_ref[kq * 128 : (kq + 1) * 128, LANE:]
            real = lines[:, :LANE]
            imag = lines[:, LANE:]
            parts[0].append(real * cos + imag * sin)
            parts[1].append(imag * cos - real * sin)
        columns.append(jnp.concatenate(parts[0] + parts[1], axis=0))
    upper, lower = cut(jnp.concatenate(columns, axis=1))
    first = table_ref[0, :, :512]
    value = mxu(first, upper) + (mxu(first, lower) + mxu(table_ref[1, :, :512], upper))
    for hi in range(HIGH):
        for ch in range(2):
            where = pl.ds(ch * HIGH + hi, PEERS, stride=8)
            rows_ref[where, :] = value[hi * PEERS : (hi + 1) * PEERS, ch * LANE : (ch + 1) * LANE]
    fix_ref[...] = mix_ref[...]
    fix_ref[pl.ds(0, BLOCKS, stride=RUN), :] = start_ref[...]
    mixture = fix_ref[...]
    lane = lax.broadcasted_iota(jnp.int32, (PEERS, LANE), 1)
    for ch in range(2):
        mine = lane[0:1, :] == ch * PEERS + lax.axis_index(FIRST)
        gain = jnp.sum(jnp.where(mine, head_ref[16:17, :], 0.0), axis=1, keepdims=True)
        fresh = back(mixture, 16 * ch) if ch else mixture
        where = pl.ds(ch * HIGH, PEERS, stride=8)
        rows_ref[where, :] = rows_ref[where, :] + jnp.where(lane < 2, gain * fresh, 0.0)
    out_ref[...] = rows_ref[...].reshape(PEERS, 8, LANE).astype(jnp.bfloat16)


def gate_kernel(queries_ref, direct_ref, head_ref, inside_ref, outside_ref, data_ref, out_ref, rows_ref, ext_ref):
    place = lax.axis_index(FIRST)
    ext_ref[0:8, :] = jnp.zeros((8, LANE), jnp.float32)

    @pl.when((place & (RUN - 1)) != 0)
    def _():
        ext_ref[6:8, :] = inside_ref[0:2, :]

    @pl.when(((place & (RUN - 1)) == 0) & (place + lax.axis_index(SECOND) > 0))
    def _():
        ext_ref[6:8, :] = outside_ref[0:2, :]

    ext_ref[8:16, :] = head_ref[0:8, :]
    queries = short_filter(ext_ref, head_ref[8:11, :], 8)
    rows_ref[...] = data_ref[...].astype(jnp.float32).reshape(8 * PEERS, LANE)
    for hi in range(HIGH):
        rows = [rows_ref[pl.ds(ch * HIGH + hi, PEERS, stride=8), :] for ch in range(2)]
        convolved = jnp.concatenate(rows, axis=0).T
        span = slice(hi * LANE, (hi + 1) * LANE)
        out_ref[span, :] = queries_ref[span, :] * (convolved + direct_ref[span, :])
        if hi == 0:
            out_ref[0:8, :] = queries * (convolved[0:8, :] + direct_ref[0:8, :])


def exchange(value, axis):
    return lax.all_to_all(value, axis, split_axis=0, concat_axis=0, tiled=True)


def far(value):
    return pltpu.with_memory_space_constraint(value, pltpu.HBM)


def on_chip(kernel, outs, scratch, name, *args):
    near = pl.BlockSpec(memory_space=pltpu.VMEM)
    return pl.pallas_call(
        kernel,
        in_specs=[near] * len(args),
        out_specs=tuple(near for _ in outs) if len(outs) > 1 else near,
        out_shape=outs if len(outs) > 1 else outs[0],
        scratch_shapes=scratch,
        name=name,
        compiler_params=GRANT,
    )(*[pltpu.with_memory_space_constraint(arg, pltpu.VMEM) for arg in args])


def on_device(projected, short_taps, skip_gain, long_filter):
    seg, wide = projected.shape
    channels = skip_gain.shape[0]
    near = pl.BlockSpec(memory_space=pltpu.VMEM)
    ahead_table, behind_table, over, under, twist = tables()
    plane = pltpu.VMEM((seg, channels), jnp.float32)
    stack = pltpu.VMEM((4, 256, LANE), jnp.float32)
    corner = pltpu.VMEM((8, LANE), jnp.float32)
    wide_rows = pltpu.VMEM((PEERS, LANE), jnp.float32)
    packed, queries, direct, head = pl.pallas_call(
        pack_kernel,
        out_specs=(near,) * 4,
        out_shape=(
            pltpu.VMEM((PEERS, HIGH, 4 * LANE), jnp.bfloat16),
            plane,
            plane,
            pltpu.VMEM((24, LANE), jnp.float32),
        ),
        scratch_shapes=[pltpu.VMEM((seg + 8, wide), jnp.float32), stack],
        name="pack",
        cost_estimate=pl.CostEstimate(flops=200000000, bytes_accessed=800000, transcendentals=0),
        compiler_params=GRANT,
    )(
        far(projected),
        far(short_taps),
        far(skip_gain.reshape(1, channels)),
        far(long_filter.reshape(HIGH, LANE)),
    )
    arrived = exchange(packed, FIRST)
    ahead, mixture, inside = on_chip(
        ahead_kernel,
        (pltpu.VMEM((PLANES, BLOCKS, KQ * 3 * 256 + LANE), jnp.bfloat16), wide_rows, corner),
        [stack, wide_rows],
        "ahead",
        arrived,
        ahead_table,
        twist,
    )
    lined = exchange(ahead, SECOND)
    blocks, start, outside = on_chip(
        blocks_kernel,
        (
            pltpu.VMEM((PLANES, BLOCKS, KQ * 2 * 256), jnp.bfloat16),
            pltpu.VMEM((BLOCKS, LANE), jnp.float32),
            corner,
        ),
        [pltpu.VMEM((128, LANE), jnp.float32)],
        "blocks",
        lined,
        over,
        under,
        twist,
    )
    returned = exchange(blocks, SECOND)
    behind = on_chip(
        behind_kernel,
        (pltpu.VMEM((PEERS, 8, LANE), jnp.bfloat16),),
        [pltpu.VMEM((8 * PEERS, LANE), jnp.float32), wide_rows],
        "behind",
        returned,
        behind_table,
        twist,
        head,
        mixture,
        start,
    )
    home = exchange(behind, FIRST)
    return pl.pallas_call(
        gate_kernel,
        in_specs=[near] * 6,
        out_shape=jax.ShapeDtypeStruct((seg, channels), jnp.float32),
        scratch_shapes=[pltpu.VMEM((8 * PEERS, LANE), jnp.float32), pltpu.VMEM((16, LANE), jnp.float32)],
        name="gate",
        compiler_params=GRANT,
    )(*[pltpu.with_memory_space_constraint(arg, pltpu.VMEM) for arg in (queries, direct, head, inside, outside, home)])


def solution(mesh):
    fine = Mesh(mesh.devices.reshape(SPLIT), EVERY)
    placed = (P(EVERY, None), P(), P(), P(EVERY))
    return jax.shard_map(on_device, mesh=fine, in_specs=placed, out_specs=P(EVERY, None), check_vma=False)
```

```python
import numpy as np

import jax
import jax.numpy as jnp
from jax import lax
from jax.experimental import pallas as pl
from jax.experimental.pallas import tpu as pltpu
from jax.sharding import Mesh, PartitionSpec as P

LANE = 128
FIRST = ("zh", "y", "zl")
SECOND = ("core", "x")
EVERY = ("zh", "y", "core", "x", "zl")
SPLIT = (2, 8, 2, 4, 4)
PEERS = 64
BLOCKS = 16
PLANES = 8
HIGH = 4
RUN = 4
SPAN = 2048
LINES = 16
KQ = 2
WAVES = 256
GRANT = pltpu.CompilerParams(vmem_limit_bytes=12 * 2**20)
EDGE = ((0, 0), (1, 0), (0, 1), (1, 1), (2, 0), (3, 0), (2, 1), (3, 1))


def turn_of(phase):
    turn = 2.0 * np.pi * np.asarray(phase, np.float64)
    return np.cos(turn), np.sin(turn)


def halves(table):
    table = np.asarray(table, np.float32)
    upper = table.astype(jnp.bfloat16)
    lower = (table - upper.astype(np.float32)).astype(jnp.bfloat16)
    return np.stack([upper, lower])


def tables():
    line = np.arange(LINES)
    same = np.eye(BLOCKS)
    cos, sin = turn_of(np.outer(line + 0.25, line) / LINES)

    def forward(part):
        small = part.reshape(PLANES, KQ, RUN, HIGH)
        return np.einsum("jkzr,bc->kjbczr", small, same).reshape(256, 256)

    def backward(part):
        small = part.reshape(PLANES, KQ, RUN, HIGH) / SPAN
        return np.einsum("jkzr,bc->rczkjb", small, same).reshape(256, 256)

    first = np.concatenate([forward(cos), forward(sin)], axis=0)
    first_back = np.concatenate([backward(cos), backward(sin)], axis=1)
    cos, sin = turn_of(np.outer(line + 0.25, np.arange(LANE)) / SPAN)
    rows = np.broadcast_to(line.reshape(PLANES, KQ).T[:, :, None], (KQ, PLANES, BLOCKS)).reshape(-1)
    twist = np.concatenate([cos[rows], sin[rows]], axis=1)
    cos, sin = turn_of(np.outer(np.arange(LANE), np.arange(LANE)) / LANE)
    second = np.block([[cos, sin], [-sin, cos]])
    block = (np.arange(BLOCKS)[None, :] * PLANES + np.arange(PLANES)[:, None]).reshape(-1)
    wave = np.arange(WAVES)
    cos, sin = turn_of(np.outer(wave, block) / WAVES)
    over = np.block([[cos, sin], [-sin, cos]])
    cos_before, sin_before = turn_of(np.outer(wave, block - 1) / WAVES)
    real = (cos + sin_before).T / WAVES
    imag = (sin - cos_before).T / WAVES
    under = np.block([[real, -imag], [imag, real]])
    spot = line.reshape(PLANES, KQ, 1) + LINES * np.arange(LANE) + 0.25
    omega = np.stack(turn_of(spot / SPAN), axis=2).reshape(PLANES, 2 * KQ, LANE)
    omega = np.concatenate([omega, np.zeros_like(omega)], axis=1).reshape(8 * PLANES, LANE)
    twist = np.concatenate([twist, np.concatenate([omega, np.zeros_like(omega)], axis=1)], axis=0).astype(np.float32)
    ahead = halves(np.concatenate([first, second], axis=0))
    behind = halves(np.concatenate([first_back, second.T], axis=1))
    return ahead, behind, halves(over), halves(under), twist


def mxu(left, right):
    return jnp.dot(left, right, preferred_element_type=jnp.float32)


def cut(value):
    upper = value.astype(jnp.bfloat16)
    return upper, (value - upper.astype(jnp.float32)).astype(jnp.bfloat16)


def short_filter(ext_ref, taps, seg):
    total = taps[0:1, :] * ext_ref[8 : 8 + seg, :]
    for tap in range(1, taps.shape[0]):
        total = total + taps[tap : tap + 1, :] * ext_ref[8 - tap : 8 - tap + seg, :]
    return total


def mix_of(filtered):
    mixture = (filtered[:, LANE : 2 * LANE] * filtered[:, 2 * LANE :]).astype(jnp.bfloat16)
    return mixture.astype(jnp.float32)


def pack_kernel(
    projected_ref, taps_ref, gain_ref, filter_ref, out_ref, queries_ref, direct_ref, head_ref, ext_ref, rows_ref
):
    seg = projected_ref.shape[0]
    ext_ref[0:8, :] = jnp.zeros((8, 3 * LANE), jnp.float32)
    ext_ref[8 : 8 + seg, :] = projected_ref[...].astype(jnp.float32)
    head_ref[0:8, :] = ext_ref[8:16, :LANE]
    head_ref[8:11, :] = taps_ref[:, :LANE]
    head_ref[16:17, :] = gain_ref[...]
    filtered = short_filter(ext_ref, taps_ref[...], seg)
    mixture = mix_of(filtered)
    queries_ref[...] = filtered[:, :LANE]
    direct = gain_ref[...] * mixture
    direct_ref[...] = direct
    direct_ref[0:8, :] = jnp.where(lax.broadcasted_iota(jnp.int32, (8, LANE), 0) < 2, 0.0, direct[0:8, :])
    taps = taps_ref[:, LANE:]
    last = ext_ref[7 + seg : 8 + seg, LANE:]
    carry = taps[1:2, :] * last + taps[2:3, :] * ext_ref[6 + seg : 7 + seg, LANE:]
    ends = [filtered[0:1, LANE:], filtered[1:2, LANE:], carry, taps[2:3, :] * last]
    ends = [ends[row][:, half * LANE : (half + 1) * LANE] for row, half in EDGE]
    upper, lower = cut(jnp.concatenate(ends, axis=0))
    pad = jnp.zeros((LANE - 16, LANE), jnp.float32)
    flipped = jnp.concatenate([upper.astype(jnp.float32), lower.astype(jnp.float32), pad], axis=0).T
    lane = lax.broadcasted_iota(jnp.int32, (PEERS, LANE), 1)
    edges = jnp.where(lane < 16, flipped[:PEERS, :], pltpu.roll(flipped[PEERS:, :], 16, 1))
    extra = [edges]
    for row in (6 + seg, 7 + seg):
        extra.append(jnp.broadcast_to(ext_ref[row : row + 1, :LANE], (PEERS, LANE)))
    extra.append(jnp.zeros((PEERS, LANE), jnp.float32))
    for hi in range(HIGH):
        flipped = mixture[hi * LANE : (hi + 1) * LANE, :].T
        where = pl.ds(hi, PEERS, stride=HIGH)
        for ch in range(2):
            rows_ref[ch, where, :] = flipped[ch * PEERS : (ch + 1) * PEERS, :]
        taps_row = filter_ref[hi : hi + 1, :].astype(jnp.float32)
        rows_ref[2, where, :] = jnp.broadcast_to(taps_row, (PEERS, LANE))
        rows_ref[3, where, :] = extra[hi]
    for at in range(4):
        out_ref[:, :, at * LANE : (at + 1) * LANE] = rows_ref[at].reshape(PEERS, HIGH, LANE).astype(jnp.bfloat16)


def back(value, lanes):
    return pltpu.roll(value, LANE - lanes, 1)


def whole_edges(edges):
    return edges + back(edges, 8)


def rows_of(own, before):
    total = own + before
    return (total * back(total, 2)).astype(jnp.bfloat16).astype(jnp.float32)


def ahead_kernel(data_ref, table_ref, twist_ref, out_ref, mix_ref, tail_ref, rows_ref, edge_ref):
    def lines_of(at):
        return data_ref[:, :, at * LANE : (at + 1) * LANE].astype(jnp.float32).reshape(256, LANE)

    cos = twist_ref[:256, :LANE]
    sin = twist_ref[:256, LANE:]

    def transform(numbers, data):
        data = data.astype(jnp.bfloat16)
        waves = [
            mxu(table_ref[0, half, :], data) + mxu(table_ref[1, half, :], data)
            for half in (slice(0, 256), slice(256, 512))
        ]
        for spot, number in enumerate(numbers):
            real = waves[0][:, spot * LANE : (spot + 1) * LANE]
            imag = waves[1][:, spot * LANE : (spot + 1) * LANE]
            upper, lower = cut(jnp.concatenate([real * cos - imag * sin, real * sin + imag * cos], axis=1))
            second = table_ref[0, 512:, :]
            for kq in range(KQ):
                rows = slice(kq * 128, (kq + 1) * 128)
                freq = mxu(upper[rows], second) + (mxu(lower[rows], second) + mxu(upper[rows], table_ref[1, 512:, :]))
                at = (kq * 3 + number) * 256
                out_ref[:, :, at : at + 256] = freq.reshape(PLANES, BLOCKS, 256).astype(jnp.bfloat16)

    transform((2,), lines_of(2))
    for at in (0, 1, 3):
        rows_ref[at] = lines_of(at)
    where = pl.ds(0, PEERS, stride=HIGH)
    edges = rows_ref[3, where, :]
    edge_ref[...] = edges
    own = whole_edges(edges)
    mixture = rows_of(own, pltpu.roll(back(own, 4), 1, 0))
    inside = (lax.broadcasted_iota(jnp.int32, (PEERS, LANE), 0) & (RUN - 1)) != 0
    lane = lax.broadcasted_iota(jnp.int32, (PEERS, LANE), 1)
    mixture = jnp.where(inside, mixture, 0.0)
    mix_ref[...] = mixture
    own_place = lax.axis_index(FIRST)
    before = jnp.maximum(own_place - 1, 0)
    ending = jnp.where(lax.axis_index(SECOND) == PLANES - 1, before, jnp.minimum(own_place + RUN - 1, PEERS - 1))
    for row in range(2):
        tail_ref[row : row + 1, :] = rows_ref[3, pl.ds(before * HIGH + 1 + row, 1), :]
    relay = []
    for row in range(2):
        value = rows_ref[3, pl.ds(ending * HIGH + 1 + row, 1), :]
        relay += [pltpu.roll(value, LANE // 2, 1), value]
    relay = jnp.concatenate(relay + [jnp.zeros((BLOCKS - 4, LANE), jnp.float32)], axis=0)
    for ch in range(2):
        fresh = back(mixture, 16 * ch) if ch else mixture
        rows_ref[ch, where, :] = jnp.where(lane < 2, fresh, rows_ref[ch, where, :])
    opening = edge_ref[pl.ds(0, BLOCKS, stride=RUN), :]
    closing = edge_ref[pl.ds(RUN - 1, BLOCKS, stride=RUN), :]
    outside = jnp.where((lane[:BLOCKS, :] & 4) == 0, opening, closing)
    outside = jnp.where(lane[:BLOCKS, :] < LANE // 2, outside, relay).astype(jnp.bfloat16)
    for plane in range(PLANES):
        out_ref[plane, :, KQ * 3 * 256 :] = outside
    transform((0, 1), jnp.concatenate([rows_ref[0], rows_ref[1]], axis=1))


def blocks_kernel(data_ref, over_ref, under_ref, twist_ref, out_ref, start_ref, tail_ref, open_ref):
    def piece(kq, number, part):
        at = ((kq * 3 + number) * 2 + part) * LANE
        return data_ref[:, :, at : at + LANE].astype(jnp.float32).reshape(128, LANE)

    taps = [jnp.concatenate([piece(kq, 2, 0), piece(kq, 2, 1)], axis=0) for kq in range(KQ)]
    taps = jnp.concatenate(taps, axis=1).astype(jnp.bfloat16)
    tap_real, tap_imag = (
        mxu(over_ref[0, half], taps) + mxu(over_ref[1, half], taps) for half in (slice(0, WAVES), slice(WAVES, 2 * WAVES))
    )
    plane = lax.axis_index(SECOND)
    omega = twist_ref[pl.ds(256 + 8 * plane, 8), :LANE]
    before = jnp.where(plane == 0, PLANES - 1, plane - 1)
    relay = data_ref[pl.ds(before, 1), :, KQ * 3 * 256 :].astype(jnp.float32).reshape(BLOCKS, LANE)
    low = lax.broadcasted_iota(jnp.int32, (1, LANE), 1) < LANE // 2
    for row in range(2):
        value = pltpu.roll(relay[2 * row : 2 * row + 1, :], LANE // 2, 1)
        tail_ref[row : row + 1, :] = jnp.where(low, value, relay[2 * row + 1 : 2 * row + 2, :])
    owns = [whole_edges(data_ref[plane, :, KQ * 3 * 256 :].astype(jnp.float32)) for plane in range(PLANES)]
    row = lax.broadcasted_iota(jnp.int32, (BLOCKS, LANE), 0)
    wrapped = jnp.where(row == 0, 0.0, pltpu.roll(back(owns[PLANES - 1], 4), 1, 0))
    befores = [wrapped] + [back(own, 4) for own in owns[:-1]]
    opening = jnp.concatenate([rows_of(own, before) for own, before in zip(owns, befores)], axis=0)
    open_ref[...] = opening
    start_ref[...] = open_ref[pl.ds(pl.multiple_of(plane * BLOCKS, BLOCKS), BLOCKS), :]

    for ch in range(2):
        zeroth = jnp.broadcast_to(opening[:, 16 * ch : 16 * ch + 1], (128, LANE))
        second = jnp.broadcast_to(opening[:, 16 * ch + 1 : 16 * ch + 2], (128, LANE))
        columns = []
        for kq in range(KQ):
            real = piece(kq, ch, 0) + (zeroth + second * omega[2 * kq : 2 * kq + 1, :])
            imag = piece(kq, ch, 1) + second * omega[2 * kq + 1 : 2 * kq + 2, :]
            columns.append(jnp.concatenate([real, imag], axis=0))
        upper, lower = cut(jnp.concatenate(columns, axis=1))
        real, imag = (
            mxu(over_ref[0, half], upper) + (mxu(over_ref[0, half], lower) + mxu(over_ref[1, half], upper))
            for half in (slice(0, WAVES), slice(WAVES, 2 * WAVES))
        )
        both = [real * tap_real - imag * tap_imag, real * tap_imag + imag * tap_real]
        upper, lower = cut(jnp.concatenate(both, axis=0))
        for part in range(2):
            half = slice(part * 128, (part + 1) * 128)
            sums = mxu(under_ref[0, half], upper) + (mxu(under_ref[0, half], lower) + mxu(under_ref[1, half], upper))
            for kq in range(KQ):
                value = sums[:, kq * LANE : (kq + 1) * LANE]
                to = ((kq * 2 + ch) * 2 + part) * LANE
                out_ref[:, :, to : to + LANE] = value.reshape(PLANES, BLOCKS, LANE).astype(jnp.bfloat16)


def behind_kernel(data_ref, table_ref, twist_ref, head_ref, mix_ref, start_ref, out_ref, rows_ref, fix_ref):
    columns = []
    for ch in range(2):
        parts = [[], []]
        for kq in range(KQ):
            at = (kq * 2 + ch) * 256
            block = data_ref[:, :, at : at + 256].astype(jnp.float32).reshape(128, 256).astype(jnp.bfloat16)
            lines = mxu(block, table_ref[0, :, 512:]) + mxu(block, table_ref[1, :, 512:])
            cos = twist_ref[kq * 128 : (kq + 1) * 128, :LANE]
            sin = twist_ref[kq * 128 : (kq + 1) * 128, LANE:]
            real = lines[:, :LANE]
            imag = lines[:, LANE:]
            parts[0].append(real * cos + imag * sin)
            parts[1].append(imag * cos - real * sin)
        columns.append(jnp.concatenate(parts[0] + parts[1], axis=0))
    upper, lower = cut(jnp.concatenate(columns, axis=1))
    first = table_ref[0, :, :512]
    value = mxu(first, upper) + (mxu(first, lower) + mxu(table_ref[1, :, :512], upper))
    for hi in range(HIGH):
        for ch in range(2):
            where = pl.ds(ch * HIGH + hi, PEERS, stride=8)
            rows_ref[where, :] = value[hi * PEERS : (hi + 1) * PEERS, ch * LANE : (ch + 1) * LANE]
    fix_ref[...] = mix_ref[...]
    fix_ref[pl.ds(0, BLOCKS, stride=RUN), :] = start_ref[...]
    mixture = fix_ref[...]
    lane = lax.broadcasted_iota(jnp.int32, (PEERS, LANE), 1)
    for ch in range(2):
        mine = lane[0:1, :] == ch * PEERS + lax.axis_index(FIRST)
        gain = jnp.sum(jnp.where(mine, head_ref[16:17, :], 0.0), axis=1, keepdims=True)
        fresh = back(mixture, 16 * ch) if ch else mixture
        where = pl.ds(ch * HIGH, PEERS, stride=8)
        rows_ref[where, :] = rows_ref[where, :] + jnp.where(lane < 2, gain * fresh, 0.0)
    out_ref[...] = rows_ref[...].reshape(PEERS, 8, LANE).astype(jnp.bfloat16)


def gate_kernel(queries_ref, direct_ref, head_ref, inside_ref, outside_ref, data_ref, out_ref, rows_ref, ext_ref):
    place = lax.axis_index(FIRST)
    ext_ref[0:8, :] = jnp.zeros((8, LANE), jnp.float32)

    @pl.when((place & (RUN - 1)) != 0)
    def _():
        ext_ref[6:8, :] = inside_ref[0:2, :]

    @pl.when(((place & (RUN - 1)) == 0) & (place + lax.axis_index(SECOND) > 0))
    def _():
        ext_ref[6:8, :] = outside_ref[0:2, :]

    ext_ref[8:16, :] = head_ref[0:8, :]
    queries = short_filter(ext_ref, head_ref[8:11, :], 8)
    rows_ref[...] = data_ref[...].astype(jnp.float32).reshape(8 * PEERS, LANE)
    for hi in range(HIGH):
        rows = [rows_ref[pl.ds(ch * HIGH + hi, PEERS, stride=8), :] for ch in range(2)]
        convolved = jnp.concatenate(rows, axis=0).T
        span = slice(hi * LANE, (hi + 1) * LANE)
        out_ref[span, :] = queries_ref[span, :] * (convolved + direct_ref[span, :])
        if hi == 0:
            out_ref[0:8, :] = queries * (convolved[0:8, :] + direct_ref[0:8, :])


def exchange(value, axis):
    return lax.all_to_all(value, axis, split_axis=0, concat_axis=0, tiled=True)


def far(value):
    return pltpu.with_memory_space_constraint(value, pltpu.HBM)


def on_chip(kernel, outs, scratch, name, *args):
    near = pl.BlockSpec(memory_space=pltpu.VMEM)
    return pl.pallas_call(
        kernel,
        in_specs=[near] * len(args),
        out_specs=tuple(near for _ in outs) if len(outs) > 1 else near,
        out_shape=outs if len(outs) > 1 else outs[0],
        scratch_shapes=scratch,
        name=name,
        compiler_params=GRANT,
    )(*[pltpu.with_memory_space_constraint(arg, pltpu.VMEM) for arg in args])


def on_device(projected, short_taps, skip_gain, long_filter):
    seg, wide = projected.shape
    channels = skip_gain.shape[0]
    near = pl.BlockSpec(memory_space=pltpu.VMEM)
    ahead_table, behind_table, over, under, twist = tables()
    plane = pltpu.VMEM((seg, channels), jnp.float32)
    stack = pltpu.VMEM((4, 256, LANE), jnp.float32)
    corner = pltpu.VMEM((8, LANE), jnp.float32)
    wide_rows = pltpu.VMEM((PEERS, LANE), jnp.float32)
    packed, queries, direct, head = pl.pallas_call(
        pack_kernel,
        out_specs=(near,) * 4,
        out_shape=(
            pltpu.VMEM((PEERS, HIGH, 4 * LANE), jnp.bfloat16),
            plane,
            plane,
            pltpu.VMEM((24, LANE), jnp.float32),
        ),
        scratch_shapes=[pltpu.VMEM((seg + 8, wide), jnp.float32), stack],
        name="pack",
        cost_estimate=pl.CostEstimate(flops=200000000, bytes_accessed=800000, transcendentals=0),
        compiler_params=GRANT,
    )(
        far(projected),
        far(short_taps),
        far(skip_gain.reshape(1, channels)),
        far(long_filter.reshape(HIGH, LANE)),
    )
    arrived = exchange(packed, FIRST)
    ahead, mixture, inside = on_chip(
        ahead_kernel,
        (pltpu.VMEM((PLANES, BLOCKS, KQ * 3 * 256 + LANE), jnp.bfloat16), wide_rows, corner),
        [stack, wide_rows],
        "ahead",
        arrived,
        ahead_table,
        twist,
    )
    lined = exchange(ahead, SECOND)
    blocks, start, outside = on_chip(
        blocks_kernel,
        (
            pltpu.VMEM((PLANES, BLOCKS, KQ * 2 * 256), jnp.bfloat16),
            pltpu.VMEM((BLOCKS, LANE), jnp.float32),
            corner,
        ),
        [pltpu.VMEM((128, LANE), jnp.float32)],
        "blocks",
        lined,
        over,
        under,
        twist,
    )
    returned = exchange(blocks, SECOND)
    behind = on_chip(
        behind_kernel,
        (pltpu.VMEM((PEERS, 8, LANE), jnp.bfloat16),),
        [pltpu.VMEM((8 * PEERS, LANE), jnp.float32), wide_rows],
        "behind",
        returned,
        behind_table,
        twist,
        head,
        mixture,
        start,
    )
    home = exchange(behind, FIRST)
    return pl.pallas_call(
        gate_kernel,
        in_specs=[near] * 6,
        out_shape=jax.ShapeDtypeStruct((seg, channels), jnp.float32),
        scratch_shapes=[pltpu.VMEM((8 * PEERS, LANE), jnp.float32), pltpu.VMEM((16, LANE), jnp.float32)],
        name="gate",
        compiler_params=GRANT,
    )(*[pltpu.with_memory_space_constraint(arg, pltpu.VMEM) for arg in (queries, direct, head, inside, outside, home)])


def solution(mesh):
    fine = Mesh(mesh.devices.reshape(SPLIT), EVERY)
    placed = (P(EVERY, None), P(), P(), P(EVERY))
    return jax.shard_map(on_device, mesh=fine, in_specs=placed, out_specs=P(EVERY, None), check_vma=False)
```

```python
import numpy as np

import jax
import jax.numpy as jnp
from jax import lax
from jax.experimental import pallas as pl
from jax.experimental.pallas import tpu as pltpu
from jax.sharding import Mesh, PartitionSpec as P

LANE = 128
FIRST = ("zh", "y", "zl")
SECOND = ("core", "x")
EVERY = ("zh", "y", "core", "x", "zl")
SPLIT = (2, 8, 2, 4, 4)
PEERS = 64
BLOCKS = 16
PLANES = 8
HIGH = 4
RUN = 4
SPAN = 2048
LINES = 16
KQ = 2
WAVES = 256
GRANT = pltpu.CompilerParams(vmem_limit_bytes=12 * 2**20)
EDGE = ((0, 0), (1, 0), (0, 1), (1, 1), (2, 0), (3, 0), (2, 1), (3, 1))


def turn_of(phase):
    turn = 2.0 * np.pi * np.asarray(phase, np.float64)
    return np.cos(turn), np.sin(turn)


def halves(table):
    table = np.asarray(table, np.float32)
    upper = table.astype(jnp.bfloat16)
    lower = (table - upper.astype(np.float32)).astype(jnp.bfloat16)
    return np.stack([upper, lower])


def tables():
    line = np.arange(LINES)
    same = np.eye(BLOCKS)
    cos, sin = turn_of(np.outer(line + 0.25, line) / LINES)

    def forward(part):
        small = part.reshape(PLANES, KQ, RUN, HIGH)
        return np.einsum("jkzr,bc->kjbczr", small, same).reshape(256, 256)

    def backward(part):
        small = part.reshape(PLANES, KQ, RUN, HIGH) / SPAN
        return np.einsum("jkzr,bc->rczkjb", small, same).reshape(256, 256)

    first = np.concatenate([forward(cos), forward(sin)], axis=0)
    first_back = np.concatenate([backward(cos), backward(sin)], axis=1)
    cos, sin = turn_of(np.outer(line + 0.25, np.arange(LANE)) / SPAN)
    rows = np.broadcast_to(line.reshape(PLANES, KQ).T[:, :, None], (KQ, PLANES, BLOCKS)).reshape(-1)
    twist = np.concatenate([cos[rows], sin[rows]], axis=1)
    cos, sin = turn_of(np.outer(np.arange(LANE), np.arange(LANE)) / LANE)
    second = np.block([[cos, sin], [-sin, cos]])
    block = (np.arange(BLOCKS)[None, :] * PLANES + np.arange(PLANES)[:, None]).reshape(-1)
    wave = np.arange(WAVES)
    cos, sin = turn_of(np.outer(wave, block) / WAVES)
    over = np.block([[cos, sin], [-sin, cos]])
    cos_before, sin_before = turn_of(np.outer(wave, block - 1) / WAVES)
    real = (cos + sin_before).T / WAVES
    imag = (sin - cos_before).T / WAVES
    under = np.block([[real, -imag], [imag, real]])
    spot = line.reshape(PLANES, KQ, 1) + LINES * np.arange(LANE) + 0.25
    omega = np.stack(turn_of(spot / SPAN), axis=2).reshape(PLANES, 2 * KQ, LANE)
    omega = np.concatenate([omega, np.zeros_like(omega)], axis=1).reshape(8 * PLANES, LANE)
    twist = np.concatenate([twist, np.concatenate([omega, np.zeros_like(omega)], axis=1)], axis=0).astype(np.float32)
    ahead = halves(np.concatenate([first, second], axis=0))
    behind = halves(np.concatenate([first_back, second.T], axis=1))
    return ahead, behind, halves(over), halves(under), twist


def mxu(left, right):
    return jnp.dot(left, right, preferred_element_type=jnp.float32)


def cut(value):
    upper = value.astype(jnp.bfloat16)
    return upper, (value - upper.astype(jnp.float32)).astype(jnp.bfloat16)


def short_filter(ext_ref, taps, seg, start=0):
    total = taps[0:1, :] * ext_ref[8 + start : 8 + start + seg, :]
    for tap in range(1, taps.shape[0]):
        total = total + taps[tap : tap + 1, :] * ext_ref[8 + start - tap : 8 + start - tap + seg, :]
    return total


def mix_of(filtered):
    mixture = (filtered[:, LANE : 2 * LANE] * filtered[:, 2 * LANE :]).astype(jnp.bfloat16)
    return mixture.astype(jnp.float32)


def pack_kernel(
    projected_ref, taps_ref, gain_ref, filter_ref, out_ref, queries_ref, direct_ref, head_ref, ext_ref, rows_ref, near_ref, sems
):
    seg = projected_ref.shape[0]
    copies = []
    for hi in range(HIGH):
        span = pl.ds(hi * LANE, LANE)
        copies.append(pltpu.make_async_copy(projected_ref.at[span, :], near_ref.at[span, :], sems.at[hi]))
        copies[hi].start()
    ext_ref[0:8, :] = jnp.zeros((8, 3 * LANE), jnp.float32)
    head_ref[8:11, :] = taps_ref[:, :LANE]
    head_ref[16:17, :] = gain_ref[...]
    for hi in range(HIGH):
        span = slice(hi * LANE, (hi + 1) * LANE)
        copies[hi].wait()
        ext_ref[8 + hi * LANE : 8 + (hi + 1) * LANE, :] = near_ref[span, :].astype(jnp.float32)
        filtered = short_filter(ext_ref, taps_ref[...], LANE, hi * LANE)
        mixture = mix_of(filtered)
        queries_ref[span, :] = filtered[:, :LANE]
        direct = gain_ref[...] * mixture
        direct_ref[span, :] = direct
        if hi == 0:
            direct_ref[0:8, :] = jnp.where(lax.broadcasted_iota(jnp.int32, (8, LANE), 0) < 2, 0.0, direct[0:8, :])
        flipped = mixture.T
        where = pl.ds(hi, PEERS, stride=HIGH)
        for ch in range(2):
            rows_ref[ch, where, :] = flipped[ch * PEERS : (ch + 1) * PEERS, :]
        taps_row = filter_ref[hi : hi + 1, :].astype(jnp.float32)
        rows_ref[2, where, :] = jnp.broadcast_to(taps_row, (PEERS, LANE))
    taps = taps_ref[:, LANE:]
    last = ext_ref[7 + seg : 8 + seg, LANE:]
    carry = taps[1:2, :] * last + taps[2:3, :] * ext_ref[6 + seg : 7 + seg, LANE:]
    opening = short_filter(ext_ref, taps_ref[...], 8)
    ends = [opening[0:1, LANE:], opening[1:2, LANE:], carry, taps[2:3, :] * last]
    ends = [ends[row][:, half * LANE : (half + 1) * LANE] for row, half in EDGE]
    upper, lower = cut(jnp.concatenate(ends, axis=0))
    pad = jnp.zeros((LANE - 16, LANE), jnp.float32)
    flipped = jnp.concatenate([upper.astype(jnp.float32), lower.astype(jnp.float32), pad], axis=0).T
    lane = lax.broadcasted_iota(jnp.int32, (PEERS, LANE), 1)
    edges = jnp.where(lane < 16, flipped[:PEERS, :], pltpu.roll(flipped[PEERS:, :], 16, 1))
    extra = [edges]
    for row in (6 + seg, 7 + seg):
        extra.append(jnp.broadcast_to(ext_ref[row : row + 1, :LANE], (PEERS, LANE)))
    extra.append(jnp.zeros((PEERS, LANE), jnp.float32))
    for hi in range(HIGH):
        rows_ref[3, pl.ds(hi, PEERS, stride=HIGH), :] = extra[hi]
    head_ref[0:8, :] = ext_ref[8:16, :LANE]
    for at in range(4):
        out_ref[:, :, at * LANE : (at + 1) * LANE] = rows_ref[at].reshape(PEERS, HIGH, LANE).astype(jnp.bfloat16)


def back(value, lanes):
    return pltpu.roll(value, LANE - lanes, 1)


def whole_edges(edges):
    return edges + back(edges, 8)


def rows_of(own, before):
    total = own + before
    return (total * back(total, 2)).astype(jnp.bfloat16).astype(jnp.float32)


def ahead_kernel(data_ref, table_ref, twist_ref, out_ref, mix_ref, tail_ref, rows_ref, edge_ref):
    def lines_of(at):
        return data_ref[:, :, at * LANE : (at + 1) * LANE].astype(jnp.float32).reshape(256, LANE)

    cos = twist_ref[:256, :LANE]
    sin = twist_ref[:256, LANE:]

    def transform(numbers, data):
        data = data.astype(jnp.bfloat16)
        waves = [
            mxu(table_ref[0, half, :], data) + mxu(table_ref[1, half, :], data)
            for half in (slice(0, 256), slice(256, 512))
        ]
        for spot, number in enumerate(numbers):
            real = waves[0][:, spot * LANE : (spot + 1) * LANE]
            imag = waves[1][:, spot * LANE : (spot + 1) * LANE]
            upper, lower = cut(jnp.concatenate([real * cos - imag * sin, real * sin + imag * cos], axis=1))
            second = table_ref[0, 512:, :]
            for kq in range(KQ):
                rows = slice(kq * 128, (kq + 1) * 128)
                freq = mxu(upper[rows], second) + (mxu(lower[rows], second) + mxu(upper[rows], table_ref[1, 512:, :]))
                at = (kq * 3 + number) * 256
                out_ref[:, :, at : at + 256] = freq.reshape(PLANES, BLOCKS, 256).astype(jnp.bfloat16)

    transform((2,), lines_of(2))
    for at in (0, 1, 3):
        rows_ref[at] = lines_of(at)
    where = pl.ds(0, PEERS, stride=HIGH)
    edges = rows_ref[3, where, :]
    edge_ref[...] = edges
    own = whole_edges(edges)
    mixture = rows_of(own, pltpu.roll(back(own, 4), 1, 0))
    inside = (lax.broadcasted_iota(jnp.int32, (PEERS, LANE), 0) & (RUN - 1)) != 0
    lane = lax.broadcasted_iota(jnp.int32, (PEERS, LANE), 1)
    mixture = jnp.where(inside, mixture, 0.0)
    mix_ref[...] = mixture
    own_place = lax.axis_index(FIRST)
    before = jnp.maximum(own_place - 1, 0)
    ending = jnp.where(lax.axis_index(SECOND) == PLANES - 1, before, jnp.minimum(own_place + RUN - 1, PEERS - 1))
    for row in range(2):
        tail_ref[row : row + 1, :] = rows_ref[3, pl.ds(before * HIGH + 1 + row, 1), :]
    relay = []
    for row in range(2):
        value = rows_ref[3, pl.ds(ending * HIGH + 1 + row, 1), :]
        relay += [pltpu.roll(value, LANE // 2, 1), value]
    relay = jnp.concatenate(relay + [jnp.zeros((BLOCKS - 4, LANE), jnp.float32)], axis=0)
    for ch in range(2):
        fresh = back(mixture, 16 * ch) if ch else mixture
        rows_ref[ch, where, :] = jnp.where(lane < 2, fresh, rows_ref[ch, where, :])
    opening = edge_ref[pl.ds(0, BLOCKS, stride=RUN), :]
    closing = edge_ref[pl.ds(RUN - 1, BLOCKS, stride=RUN), :]
    outside = jnp.where((lane[:BLOCKS, :] & 4) == 0, opening, closing)
    outside = jnp.where(lane[:BLOCKS, :] < LANE // 2, outside, relay).astype(jnp.bfloat16)
    for plane in range(PLANES):
        out_ref[plane, :, KQ * 3 * 256 :] = outside
    transform((0, 1), jnp.concatenate([rows_ref[0], rows_ref[1]], axis=1))


def blocks_kernel(data_ref, over_ref, under_ref, twist_ref, out_ref, start_ref, tail_ref, open_ref):
    def piece(kq, number, part):
        at = ((kq * 3 + number) * 2 + part) * LANE
        return data_ref[:, :, at : at + LANE].astype(jnp.float32).reshape(128, LANE)

    taps = [jnp.concatenate([piece(kq, 2, 0), piece(kq, 2, 1)], axis=0) for kq in range(KQ)]
    taps = jnp.concatenate(taps, axis=1).astype(jnp.bfloat16)
    tap_real, tap_imag = (
        mxu(over_ref[0, half], taps) + mxu(over_ref[1, half], taps) for half in (slice(0, WAVES), slice(WAVES, 2 * WAVES))
    )
    plane = lax.axis_index(SECOND)
    omega = twist_ref[pl.ds(256 + 8 * plane, 8), :LANE]
    before = jnp.where(plane == 0, PLANES - 1, plane - 1)
    relay = data_ref[pl.ds(before, 1), :, KQ * 3 * 256 :].astype(jnp.float32).reshape(BLOCKS, LANE)
    low = lax.broadcasted_iota(jnp.int32, (1, LANE), 1) < LANE // 2
    for row in range(2):
        value = pltpu.roll(relay[2 * row : 2 * row + 1, :], LANE // 2, 1)
        tail_ref[row : row + 1, :] = jnp.where(low, value, relay[2 * row + 1 : 2 * row + 2, :])
    owns = [whole_edges(data_ref[plane, :, KQ * 3 * 256 :].astype(jnp.float32)) for plane in range(PLANES)]
    row = lax.broadcasted_iota(jnp.int32, (BLOCKS, LANE), 0)
    wrapped = jnp.where(row == 0, 0.0, pltpu.roll(back(owns[PLANES - 1], 4), 1, 0))
    befores = [wrapped] + [back(own, 4) for own in owns[:-1]]
    opening = jnp.concatenate([rows_of(own, before) for own, before in zip(owns, befores)], axis=0)
    open_ref[...] = opening
    start_ref[...] = open_ref[pl.ds(pl.multiple_of(plane * BLOCKS, BLOCKS), BLOCKS), :]

    for ch in range(2):
        zeroth = jnp.broadcast_to(opening[:, 16 * ch : 16 * ch + 1], (128, LANE))
        second = jnp.broadcast_to(opening[:, 16 * ch + 1 : 16 * ch + 2], (128, LANE))
        columns = []
        for kq in range(KQ):
            real = piece(kq, ch, 0) + (zeroth + second * omega[2 * kq : 2 * kq + 1, :])
            imag = piece(kq, ch, 1) + second * omega[2 * kq + 1 : 2 * kq + 2, :]
            columns.append(jnp.concatenate([real, imag], axis=0))
        upper, lower = cut(jnp.concatenate(columns, axis=1))
        real, imag = (
            mxu(over_ref[0, half], upper) + (mxu(over_ref[0, half], lower) + mxu(over_ref[1, half], upper))
            for half in (slice(0, WAVES), slice(WAVES, 2 * WAVES))
        )
        both = [real * tap_real - imag * tap_imag, real * tap_imag + imag * tap_real]
        upper, lower = cut(jnp.concatenate(both, axis=0))
        for part in range(2):
            half = slice(part * 128, (part + 1) * 128)
            sums = mxu(under_ref[0, half], upper) + (mxu(under_ref[0, half], lower) + mxu(under_ref[1, half], upper))
            for kq in range(KQ):
                value = sums[:, kq * LANE : (kq + 1) * LANE]
                to = ((kq * 2 + ch) * 2 + part) * LANE
                out_ref[:, :, to : to + LANE] = value.reshape(PLANES, BLOCKS, LANE).astype(jnp.bfloat16)


def behind_kernel(data_ref, table_ref, twist_ref, head_ref, mix_ref, start_ref, out_ref, rows_ref, fix_ref):
    columns = []
    for ch in range(2):
        parts = [[], []]
        for kq in range(KQ):
            at = (kq * 2 + ch) * 256
            block = data_ref[:, :, at : at + 256].astype(jnp.float32).reshape(128, 256).astype(jnp.bfloat16)
            lines = mxu(block, table_ref[0, :, 512:]) + mxu(block, table_ref[1, :, 512:])
            cos = twist_ref[kq * 128 : (kq + 1) * 128, :LANE]
            sin = twist_ref[kq * 128 : (kq + 1) * 128, LANE:]
            real = lines[:, :LANE]
            imag = lines[:, LANE:]
            parts[0].append(real * cos + imag * sin)
            parts[1].append(imag * cos - real * sin)
        columns.append(jnp.concatenate(parts[0] + parts[1], axis=0))
    upper, lower = cut(jnp.concatenate(columns, axis=1))
    first = table_ref[0, :, :512]
    value = mxu(first, upper) + (mxu(first, lower) + mxu(table_ref[1, :, :512], upper))
    for hi in range(HIGH):
        for ch in range(2):
            where = pl.ds(ch * HIGH + hi, PEERS, stride=8)
            rows_ref[where, :] = value[hi * PEERS : (hi + 1) * PEERS, ch * LANE : (ch + 1) * LANE]
    fix_ref[...] = mix_ref[...]
    fix_ref[pl.ds(0, BLOCKS, stride=RUN), :] = start_ref[...]
    mixture = fix_ref[...]
    lane = lax.broadcasted_iota(jnp.int32, (PEERS, LANE), 1)
    for ch in range(2):
        mine = lane[0:1, :] == ch * PEERS + lax.axis_index(FIRST)
        gain = jnp.sum(jnp.where(mine, head_ref[16:17, :], 0.0), axis=1, keepdims=True)
        fresh = back(mixture, 16 * ch) if ch else mixture
        where = pl.ds(ch * HIGH, PEERS, stride=8)
        rows_ref[where, :] = rows_ref[where, :] + jnp.where(lane < 2, gain * fresh, 0.0)
    out_ref[...] = rows_ref[...].reshape(PEERS, 8, LANE).astype(jnp.bfloat16)


def gate_kernel(queries_ref, direct_ref, head_ref, inside_ref, outside_ref, data_ref, out_ref, rows_ref, ext_ref):
    place = lax.axis_index(FIRST)
    ext_ref[0:8, :] = jnp.zeros((8, LANE), jnp.float32)

    @pl.when((place & (RUN - 1)) != 0)
    def _():
        ext_ref[6:8, :] = inside_ref[0:2, :]

    @pl.when(((place & (RUN - 1)) == 0) & (place + lax.axis_index(SECOND) > 0))
    def _():
        ext_ref[6:8, :] = outside_ref[0:2, :]

    ext_ref[8:16, :] = head_ref[0:8, :]
    queries = short_filter(ext_ref, head_ref[8:11, :], 8)
    rows_ref[...] = data_ref[...].astype(jnp.float32).reshape(8 * PEERS, LANE)
    for hi in range(HIGH):
        rows = [rows_ref[pl.ds(ch * HIGH + hi, PEERS, stride=8), :] for ch in range(2)]
        convolved = jnp.concatenate(rows, axis=0).T
        span = slice(hi * LANE, (hi + 1) * LANE)
        out_ref[span, :] = queries_ref[span, :] * (convolved + direct_ref[span, :])
        if hi == 0:
            out_ref[0:8, :] = queries * (convolved[0:8, :] + direct_ref[0:8, :])


def exchange(value, axis):
    return lax.all_to_all(value, axis, split_axis=0, concat_axis=0, tiled=True)


def far(value):
    return pltpu.with_memory_space_constraint(value, pltpu.HBM)


def on_chip(kernel, outs, scratch, name, *args):
    near = pl.BlockSpec(memory_space=pltpu.VMEM)
    return pl.pallas_call(
        kernel,
        in_specs=[near] * len(args),
        out_specs=tuple(near for _ in outs) if len(outs) > 1 else near,
        out_shape=outs if len(outs) > 1 else outs[0],
        scratch_shapes=scratch,
        name=name,
        compiler_params=GRANT,
    )(*[pltpu.with_memory_space_constraint(arg, pltpu.VMEM) for arg in args])


def on_device(projected, short_taps, skip_gain, long_filter):
    seg, wide = projected.shape
    channels = skip_gain.shape[0]
    near = pl.BlockSpec(memory_space=pltpu.VMEM)
    ahead_table, behind_table, over, under, twist = tables()
    plane = pltpu.VMEM((seg, channels), jnp.float32)
    stack = pltpu.VMEM((4, 256, LANE), jnp.float32)
    corner = pltpu.VMEM((8, LANE), jnp.float32)
    wide_rows = pltpu.VMEM((PEERS, LANE), jnp.float32)
    packed, queries, direct, head = pl.pallas_call(
        pack_kernel,
        out_specs=(near,) * 4,
        out_shape=(
            pltpu.VMEM((PEERS, HIGH, 4 * LANE), jnp.bfloat16),
            plane,
            plane,
            pltpu.VMEM((24, LANE), jnp.float32),
        ),
        in_specs=[pl.BlockSpec(memory_space=pltpu.HBM), near, near, near],
        scratch_shapes=[
            pltpu.VMEM((seg + 8, wide), jnp.float32),
            stack,
            pltpu.VMEM((seg, wide), jnp.bfloat16),
            pltpu.SemaphoreType.DMA((HIGH,)),
        ],
        name="pack",
        cost_estimate=pl.CostEstimate(flops=200000000, bytes_accessed=800000, transcendentals=0),
        compiler_params=GRANT,
    )(
        far(projected),
        far(short_taps),
        far(skip_gain.reshape(1, channels)),
        far(long_filter.reshape(HIGH, LANE)),
    )
    arrived = exchange(packed, FIRST)
    ahead, mixture, inside = on_chip(
        ahead_kernel,
        (pltpu.VMEM((PLANES, BLOCKS, KQ * 3 * 256 + LANE), jnp.bfloat16), wide_rows, corner),
        [stack, wide_rows],
        "ahead",
        arrived,
        ahead_table,
        twist,
    )
    lined = exchange(ahead, SECOND)
    blocks, start, outside = on_chip(
        blocks_kernel,
        (
            pltpu.VMEM((PLANES, BLOCKS, KQ * 2 * 256), jnp.bfloat16),
            pltpu.VMEM((BLOCKS, LANE), jnp.float32),
            corner,
        ),
        [pltpu.VMEM((128, LANE), jnp.float32)],
        "blocks",
        lined,
        over,
        under,
        twist,
    )
    returned = exchange(blocks, SECOND)
    behind = on_chip(
        behind_kernel,
        (pltpu.VMEM((PEERS, 8, LANE), jnp.bfloat16),),
        [pltpu.VMEM((8 * PEERS, LANE), jnp.float32), wide_rows],
        "behind",
        returned,
        behind_table,
        twist,
        head,
        mixture,
        start,
    )
    home = exchange(behind, FIRST)
    return pl.pallas_call(
        gate_kernel,
        in_specs=[near] * 6,
        out_shape=jax.ShapeDtypeStruct((seg, channels), jnp.float32),
        scratch_shapes=[pltpu.VMEM((8 * PEERS, LANE), jnp.float32), pltpu.VMEM((16, LANE), jnp.float32)],
        name="gate",
        compiler_params=GRANT,
    )(*[pltpu.with_memory_space_constraint(arg, pltpu.VMEM) for arg in (queries, direct, head, inside, outside, home)])


def solution(mesh):
    fine = Mesh(mesh.devices.reshape(SPLIT), EVERY)
    placed = (P(EVERY, None), P(), P(), P(EVERY))
    return jax.shard_map(on_device, mesh=fine, in_specs=placed, out_specs=P(EVERY, None), check_vma=False)
```

```python
import numpy as np

import jax
import jax.numpy as jnp
from jax import lax
from jax.experimental import pallas as pl
from jax.experimental.pallas import tpu as pltpu
from jax.sharding import Mesh, PartitionSpec as P

LANE = 128
FIRST = ("zh", "y", "zl")
SECOND = ("core", "x")
EVERY = ("zh", "y", "core", "x", "zl")
SPLIT = (2, 8, 2, 4, 4)
PEERS = 64
BLOCKS = 16
PLANES = 8
HIGH = 4
RUN = 4
SPAN = 2048
LINES = 16
KQ = 2
WAVES = 256
GRANT = pltpu.CompilerParams(vmem_limit_bytes=12 * 2**20)
EDGE = ((0, 0), (1, 0), (0, 1), (1, 1), (2, 0), (3, 0), (2, 1), (3, 1))


def turn_of(phase):
    turn = 2.0 * np.pi * np.asarray(phase, np.float64)
    return np.cos(turn), np.sin(turn)


def halves(table):
    table = np.asarray(table, np.float32)
    upper = table.astype(jnp.bfloat16)
    lower = (table - upper.astype(np.float32)).astype(jnp.bfloat16)
    return np.stack([upper, lower])


def tables():
    line = np.arange(LINES)
    same = np.eye(BLOCKS)
    cos, sin = turn_of(np.outer(line + 0.25, line) / LINES)

    def forward(part):
        small = part.reshape(PLANES, KQ, RUN, HIGH)
        return np.einsum("jkzr,bc->kjbczr", small, same).reshape(256, 256)

    def backward(part):
        small = part.reshape(PLANES, KQ, RUN, HIGH) / SPAN
        return np.einsum("jkzr,bc->rczkjb", small, same).reshape(256, 256)

    first = np.concatenate([forward(cos), forward(sin)], axis=0)
    first_back = np.concatenate([backward(cos), backward(sin)], axis=1)
    cos, sin = turn_of(np.outer(line + 0.25, np.arange(LANE)) / SPAN)
    rows = np.broadcast_to(line.reshape(PLANES, KQ).T[:, :, None], (KQ, PLANES, BLOCKS)).reshape(-1)
    twist = np.concatenate([cos[rows], sin[rows]], axis=1)
    cos, sin = turn_of(np.outer(np.arange(LANE), np.arange(LANE)) / LANE)
    second = np.block([[cos, sin], [-sin, cos]])
    block = (np.arange(BLOCKS)[None, :] * PLANES + np.arange(PLANES)[:, None]).reshape(-1)
    wave = np.arange(WAVES)
    cos, sin = turn_of(np.outer(wave, block) / WAVES)
    over = np.block([[cos, sin], [-sin, cos]])
    cos_before, sin_before = turn_of(np.outer(wave, block - 1) / WAVES)
    real = (cos + sin_before).T / WAVES
    imag = (sin - cos_before).T / WAVES
    under = np.block([[real, -imag], [imag, real]])
    spot = line.reshape(PLANES, KQ, 1) + LINES * np.arange(LANE) + 0.25
    omega = np.stack(turn_of(spot / SPAN), axis=2).reshape(PLANES, 2 * KQ, LANE)
    omega = np.concatenate([omega, np.zeros_like(omega)], axis=1).reshape(8 * PLANES, LANE)
    twist = np.concatenate([twist, np.concatenate([omega, np.zeros_like(omega)], axis=1)], axis=0).astype(np.float32)
    ahead = halves(np.concatenate([first, second], axis=0))
    behind = halves(np.concatenate([first_back, second.T], axis=1))
    return ahead, behind, halves(over), halves(under), twist


def mxu(left, right):
    return jnp.dot(left, right, preferred_element_type=jnp.float32)


def cut(value):
    upper = value.astype(jnp.bfloat16)
    return upper, (value - upper.astype(jnp.float32)).astype(jnp.bfloat16)


def short_filter(ext_ref, taps, seg, start=0):
    total = taps[0:1, :] * ext_ref[8 + start : 8 + start + seg, :]
    for tap in range(1, taps.shape[0]):
        total = total + taps[tap : tap + 1, :] * ext_ref[8 + start - tap : 8 + start - tap + seg, :]
    return total


def mix_of(filtered):
    mixture = (filtered[:, LANE : 2 * LANE] * filtered[:, 2 * LANE :]).astype(jnp.bfloat16)
    return mixture.astype(jnp.float32)


def pack_kernel(
    projected_ref, taps_ref, gain_ref, filter_ref, out_ref, queries_ref, direct_ref, head_ref, ext_ref, rows_ref
):
    seg = projected_ref.shape[0]
    ext_ref[0:8, :] = jnp.zeros((8, 3 * LANE), jnp.float32)
    ext_ref[8 : 8 + seg, :] = projected_ref[...].astype(jnp.float32)
    head_ref[0:8, :] = ext_ref[8:16, :LANE]
    head_ref[8:11, :] = taps_ref[:, :LANE]
    head_ref[16:17, :] = gain_ref[...]
    taps = taps_ref[:, LANE:]
    last = ext_ref[7 + seg : 8 + seg, LANE:]
    carry = taps[1:2, :] * last + taps[2:3, :] * ext_ref[6 + seg : 7 + seg, LANE:]
    opening = short_filter(ext_ref, taps_ref[...], 8)
    ends = [opening[0:1, LANE:], opening[1:2, LANE:], carry, taps[2:3, :] * last]
    ends = [ends[row][:, half * LANE : (half + 1) * LANE] for row, half in EDGE]
    upper, lower = cut(jnp.concatenate(ends, axis=0))
    pad = jnp.zeros((LANE - 16, LANE), jnp.float32)
    flipped = jnp.concatenate([upper.astype(jnp.float32), lower.astype(jnp.float32), pad], axis=0).T
    lane = lax.broadcasted_iota(jnp.int32, (PEERS, LANE), 1)
    edges = jnp.where(lane < 16, flipped[:PEERS, :], pltpu.roll(flipped[PEERS:, :], 16, 1))
    extra = [edges]
    for row in (6 + seg, 7 + seg):
        extra.append(jnp.broadcast_to(ext_ref[row : row + 1, :LANE], (PEERS, LANE)))
    extra.append(jnp.zeros((PEERS, LANE), jnp.float32))
    for hi in range(HIGH):
        span = slice(hi * LANE, (hi + 1) * LANE)
        filtered = short_filter(ext_ref, taps_ref[...], LANE, hi * LANE)
        mixture = mix_of(filtered)
        queries_ref[span, :] = filtered[:, :LANE]
        direct = gain_ref[...] * mixture
        direct_ref[span, :] = direct
        if hi == 0:
            direct_ref[0:8, :] = jnp.where(lax.broadcasted_iota(jnp.int32, (8, LANE), 0) < 2, 0.0, direct[0:8, :])
        flipped = mixture.T
        where = pl.ds(hi, PEERS, stride=HIGH)
        for ch in range(2):
            rows_ref[ch, where, :] = flipped[ch * PEERS : (ch + 1) * PEERS, :]
        taps_row = filter_ref[hi : hi + 1, :].astype(jnp.float32)
        rows_ref[2, where, :] = jnp.broadcast_to(taps_row, (PEERS, LANE))
        rows_ref[3, where, :] = extra[hi]
    for at in range(4):
        out_ref[:, :, at * LANE : (at + 1) * LANE] = rows_ref[at].reshape(PEERS, HIGH, LANE).astype(jnp.bfloat16)


def back(value, lanes):
    return pltpu.roll(value, LANE - lanes, 1)


def whole_edges(edges):
    return edges + back(edges, 8)


def rows_of(own, before):
    total = own + before
    return (total * back(total, 2)).astype(jnp.bfloat16).astype(jnp.float32)


def ahead_kernel(data_ref, table_ref, twist_ref, out_ref, mix_ref, tail_ref, rows_ref, edge_ref):
    def lines_of(at):
        return data_ref[:, :, at * LANE : (at + 1) * LANE].astype(jnp.float32).reshape(256, LANE)

    cos = twist_ref[:256, :LANE]
    sin = twist_ref[:256, LANE:]

    def transform(numbers, data):
        data = data.astype(jnp.bfloat16)
        waves = [
            mxu(table_ref[0, half, :], data) + mxu(table_ref[1, half, :], data)
            for half in (slice(0, 256), slice(256, 512))
        ]
        for spot, number in enumerate(numbers):
            real = waves[0][:, spot * LANE : (spot + 1) * LANE]
            imag = waves[1][:, spot * LANE : (spot + 1) * LANE]
            upper, lower = cut(jnp.concatenate([real * cos - imag * sin, real * sin + imag * cos], axis=1))
            second = table_ref[0, 512:, :]
            for kq in range(KQ):
                rows = slice(kq * 128, (kq + 1) * 128)
                freq = mxu(upper[rows], second) + (mxu(lower[rows], second) + mxu(upper[rows], table_ref[1, 512:, :]))
                at = (kq * 3 + number) * 256
                out_ref[:, :, at : at + 256] = freq.reshape(PLANES, BLOCKS, 256).astype(jnp.bfloat16)

    transform((2,), lines_of(2))
    for at in (0, 1, 3):
        rows_ref[at] = lines_of(at)
    where = pl.ds(0, PEERS, stride=HIGH)
    edges = rows_ref[3, where, :]
    edge_ref[...] = edges
    own = whole_edges(edges)
    mixture = rows_of(own, pltpu.roll(back(own, 4), 1, 0))
    inside = (lax.broadcasted_iota(jnp.int32, (PEERS, LANE), 0) & (RUN - 1)) != 0
    lane = lax.broadcasted_iota(jnp.int32, (PEERS, LANE), 1)
    mixture = jnp.where(inside, mixture, 0.0)
    mix_ref[...] = mixture
    own_place = lax.axis_index(FIRST)
    before = jnp.maximum(own_place - 1, 0)
    ending = jnp.where(lax.axis_index(SECOND) == PLANES - 1, before, jnp.minimum(own_place + RUN - 1, PEERS - 1))
    for row in range(2):
        tail_ref[row : row + 1, :] = rows_ref[3, pl.ds(before * HIGH + 1 + row, 1), :]
    relay = []
    for row in range(2):
        value = rows_ref[3, pl.ds(ending * HIGH + 1 + row, 1), :]
        relay += [pltpu.roll(value, LANE // 2, 1), value]
    relay = jnp.concatenate(relay + [jnp.zeros((BLOCKS - 4, LANE), jnp.float32)], axis=0)
    for ch in range(2):
        fresh = back(mixture, 16 * ch) if ch else mixture
        rows_ref[ch, where, :] = jnp.where(lane < 2, fresh, rows_ref[ch, where, :])
    opening = edge_ref[pl.ds(0, BLOCKS, stride=RUN), :]
    closing = edge_ref[pl.ds(RUN - 1, BLOCKS, stride=RUN), :]
    outside = jnp.where((lane[:BLOCKS, :] & 4) == 0, opening, closing)
    outside = jnp.where(lane[:BLOCKS, :] < LANE // 2, outside, relay).astype(jnp.bfloat16)
    for plane in range(PLANES):
        out_ref[plane, :, KQ * 3 * 256 :] = outside
    transform((0, 1), jnp.concatenate([rows_ref[0], rows_ref[1]], axis=1))


def blocks_kernel(data_ref, over_ref, under_ref, twist_ref, out_ref, start_ref, tail_ref, open_ref):
    def piece(kq, number, part):
        at = ((kq * 3 + number) * 2 + part) * LANE
        return data_ref[:, :, at : at + LANE].astype(jnp.float32).reshape(128, LANE)

    taps = [jnp.concatenate([piece(kq, 2, 0), piece(kq, 2, 1)], axis=0) for kq in range(KQ)]
    taps = jnp.concatenate(taps, axis=1).astype(jnp.bfloat16)
    tap_real, tap_imag = (
        mxu(over_ref[0, half], taps) + mxu(over_ref[1, half], taps) for half in (slice(0, WAVES), slice(WAVES, 2 * WAVES))
    )
    plane = lax.axis_index(SECOND)
    omega = twist_ref[pl.ds(256 + 8 * plane, 8), :LANE]
    before = jnp.where(plane == 0, PLANES - 1, plane - 1)
    relay = data_ref[pl.ds(before, 1), :, KQ * 3 * 256 :].astype(jnp.float32).reshape(BLOCKS, LANE)
    low = lax.broadcasted_iota(jnp.int32, (1, LANE), 1) < LANE // 2
    for row in range(2):
        value = pltpu.roll(relay[2 * row : 2 * row + 1, :], LANE // 2, 1)
        tail_ref[row : row + 1, :] = jnp.where(low, value, relay[2 * row + 1 : 2 * row + 2, :])
    owns = [whole_edges(data_ref[plane, :, KQ * 3 * 256 :].astype(jnp.float32)) for plane in range(PLANES)]
    row = lax.broadcasted_iota(jnp.int32, (BLOCKS, LANE), 0)
    wrapped = jnp.where(row == 0, 0.0, pltpu.roll(back(owns[PLANES - 1], 4), 1, 0))
    befores = [wrapped] + [back(own, 4) for own in owns[:-1]]
    opening = jnp.concatenate([rows_of(own, before) for own, before in zip(owns, befores)], axis=0)
    open_ref[...] = opening
    start_ref[...] = open_ref[pl.ds(pl.multiple_of(plane * BLOCKS, BLOCKS), BLOCKS), :]

    for ch in range(2):
        zeroth = jnp.broadcast_to(opening[:, 16 * ch : 16 * ch + 1], (128, LANE))
        second = jnp.broadcast_to(opening[:, 16 * ch + 1 : 16 * ch + 2], (128, LANE))
        columns = []
        for kq in range(KQ):
            real = piece(kq, ch, 0) + (zeroth + second * omega[2 * kq : 2 * kq + 1, :])
            imag = piece(kq, ch, 1) + second * omega[2 * kq + 1 : 2 * kq + 2, :]
            columns.append(jnp.concatenate([real, imag], axis=0))
        upper, lower = cut(jnp.concatenate(columns, axis=1))
        real, imag = (
            mxu(over_ref[0, half], upper) + (mxu(over_ref[0, half], lower) + mxu(over_ref[1, half], upper))
            for half in (slice(0, WAVES), slice(WAVES, 2 * WAVES))
        )
        both = [real * tap_real - imag * tap_imag, real * tap_imag + imag * tap_real]
        upper, lower = cut(jnp.concatenate(both, axis=0))
        for part in range(2):
            half = slice(part * 128, (part + 1) * 128)
            sums = mxu(under_ref[0, half], upper) + (mxu(under_ref[0, half], lower) + mxu(under_ref[1, half], upper))
            for kq in range(KQ):
                value = sums[:, kq * LANE : (kq + 1) * LANE]
                to = ((kq * 2 + ch) * 2 + part) * LANE
                out_ref[:, :, to : to + LANE] = value.reshape(PLANES, BLOCKS, LANE).astype(jnp.bfloat16)


def behind_kernel(data_ref, table_ref, twist_ref, head_ref, mix_ref, start_ref, out_ref, rows_ref, fix_ref):
    columns = []
    for ch in range(2):
        parts = [[], []]
        for kq in range(KQ):
            at = (kq * 2 + ch) * 256
            block = data_ref[:, :, at : at + 256].astype(jnp.float32).reshape(128, 256).astype(jnp.bfloat16)
            lines = mxu(block, table_ref[0, :, 512:]) + mxu(block, table_ref[1, :, 512:])
            cos = twist_ref[kq * 128 : (kq + 1) * 128, :LANE]
            sin = twist_ref[kq * 128 : (kq + 1) * 128, LANE:]
            real = lines[:, :LANE]
            imag = lines[:, LANE:]
            parts[0].append(real * cos + imag * sin)
            parts[1].append(imag * cos - real * sin)
        columns.append(jnp.concatenate(parts[0] + parts[1], axis=0))
    upper, lower = cut(jnp.concatenate(columns, axis=1))
    first = table_ref[0, :, :512]
    value = mxu(first, upper) + (mxu(first, lower) + mxu(table_ref[1, :, :512], upper))
    for hi in range(HIGH):
        for ch in range(2):
            where = pl.ds(ch * HIGH + hi, PEERS, stride=8)
            rows_ref[where, :] = value[hi * PEERS : (hi + 1) * PEERS, ch * LANE : (ch + 1) * LANE]
    fix_ref[...] = mix_ref[...]
    fix_ref[pl.ds(0, BLOCKS, stride=RUN), :] = start_ref[...]
    mixture = fix_ref[...]
    lane = lax.broadcasted_iota(jnp.int32, (PEERS, LANE), 1)
    for ch in range(2):
        mine = lane[0:1, :] == ch * PEERS + lax.axis_index(FIRST)
        gain = jnp.sum(jnp.where(mine, head_ref[16:17, :], 0.0), axis=1, keepdims=True)
        fresh = back(mixture, 16 * ch) if ch else mixture
        where = pl.ds(ch * HIGH, PEERS, stride=8)
        rows_ref[where, :] = rows_ref[where, :] + jnp.where(lane < 2, gain * fresh, 0.0)
    out_ref[...] = rows_ref[...].reshape(PEERS, 8, LANE).astype(jnp.bfloat16)


def gate_kernel(queries_ref, direct_ref, head_ref, inside_ref, outside_ref, data_ref, out_ref, rows_ref, ext_ref):
    place = lax.axis_index(FIRST)
    ext_ref[0:8, :] = jnp.zeros((8, LANE), jnp.float32)

    @pl.when((place & (RUN - 1)) != 0)
    def _():
        ext_ref[6:8, :] = inside_ref[0:2, :]

    @pl.when(((place & (RUN - 1)) == 0) & (place + lax.axis_index(SECOND) > 0))
    def _():
        ext_ref[6:8, :] = outside_ref[0:2, :]

    ext_ref[8:16, :] = head_ref[0:8, :]
    queries = short_filter(ext_ref, head_ref[8:11, :], 8)
    rows_ref[...] = data_ref[...].astype(jnp.float32).reshape(8 * PEERS, LANE)
    for hi in range(HIGH):
        rows = [rows_ref[pl.ds(ch * HIGH + hi, PEERS, stride=8), :] for ch in range(2)]
        convolved = jnp.concatenate(rows, axis=0).T
        span = slice(hi * LANE, (hi + 1) * LANE)
        out_ref[span, :] = queries_ref[span, :] * (convolved + direct_ref[span, :])
        if hi == 0:
            out_ref[0:8, :] = queries * (convolved[0:8, :] + direct_ref[0:8, :])


def exchange(value, axis):
    return lax.all_to_all(value, axis, split_axis=0, concat_axis=0, tiled=True)


def far(value):
    return pltpu.with_memory_space_constraint(value, pltpu.HBM)


def on_chip(kernel, outs, scratch, name, *args):
    near = pl.BlockSpec(memory_space=pltpu.VMEM)
    return pl.pallas_call(
        kernel,
        in_specs=[near] * len(args),
        out_specs=tuple(near for _ in outs) if len(outs) > 1 else near,
        out_shape=outs if len(outs) > 1 else outs[0],
        scratch_shapes=scratch,
        name=name,
        compiler_params=GRANT,
    )(*[pltpu.with_memory_space_constraint(arg, pltpu.VMEM) for arg in args])


def on_device(projected, short_taps, skip_gain, long_filter):
    seg, wide = projected.shape
    channels = skip_gain.shape[0]
    near = pl.BlockSpec(memory_space=pltpu.VMEM)
    ahead_table, behind_table, over, under, twist = tables()
    plane = pltpu.VMEM((seg, channels), jnp.float32)
    stack = pltpu.VMEM((4, 256, LANE), jnp.float32)
    corner = pltpu.VMEM((8, LANE), jnp.float32)
    wide_rows = pltpu.VMEM((PEERS, LANE), jnp.float32)
    packed, queries, direct, head = pl.pallas_call(
        pack_kernel,
        out_specs=(near,) * 4,
        out_shape=(
            pltpu.VMEM((PEERS, HIGH, 4 * LANE), jnp.bfloat16),
            plane,
            plane,
            pltpu.VMEM((24, LANE), jnp.float32),
        ),
        scratch_shapes=[pltpu.VMEM((seg + 8, wide), jnp.float32), stack],
        name="pack",
        cost_estimate=pl.CostEstimate(flops=200000000, bytes_accessed=800000, transcendentals=0),
        compiler_params=GRANT,
    )(
        far(projected),
        far(short_taps),
        far(skip_gain.reshape(1, channels)),
        far(long_filter.reshape(HIGH, LANE)),
    )
    arrived = exchange(packed, FIRST)
    ahead, mixture, inside = on_chip(
        ahead_kernel,
        (pltpu.VMEM((PLANES, BLOCKS, KQ * 3 * 256 + LANE), jnp.bfloat16), wide_rows, corner),
        [stack, wide_rows],
        "ahead",
        arrived,
        ahead_table,
        twist,
    )
    lined = exchange(ahead, SECOND)
    blocks, start, outside = on_chip(
        blocks_kernel,
        (
            pltpu.VMEM((PLANES, BLOCKS, KQ * 2 * 256), jnp.bfloat16),
            pltpu.VMEM((BLOCKS, LANE), jnp.float32),
            corner,
        ),
        [pltpu.VMEM((128, LANE), jnp.float32)],
        "blocks",
        lined,
        over,
        under,
        twist,
    )
    returned = exchange(blocks, SECOND)
    behind = on_chip(
        behind_kernel,
        (pltpu.VMEM((PEERS, 8, LANE), jnp.bfloat16),),
        [pltpu.VMEM((8 * PEERS, LANE), jnp.float32), wide_rows],
        "behind",
        returned,
        behind_table,
        twist,
        head,
        mixture,
        start,
    )
    home = exchange(behind, FIRST)
    return pl.pallas_call(
        gate_kernel,
        in_specs=[near] * 6,
        out_shape=jax.ShapeDtypeStruct((seg, channels), jnp.float32),
        scratch_shapes=[pltpu.VMEM((8 * PEERS, LANE), jnp.float32), pltpu.VMEM((16, LANE), jnp.float32)],
        name="gate",
        compiler_params=GRANT,
    )(*[pltpu.with_memory_space_constraint(arg, pltpu.VMEM) for arg in (queries, direct, head, inside, outside, home)])


def solution(mesh):
    fine = Mesh(mesh.devices.reshape(SPLIT), EVERY)
    placed = (P(EVERY, None), P(), P(), P(EVERY))
    return jax.shard_map(on_device, mesh=fine, in_specs=placed, out_specs=P(EVERY, None), check_vma=False)
```
